32 devices in a mesh: expert: 8 (over z, core), dp: 4 (over y, x).
Axes of the slice: x: 2, y: 2, z: 4, core: 2. Of those that a mesh axis runs over, the one named last changes fastest.
Arguments:
- tokens: bfloat16 [4096, 1024], P(('expert', 'dp')), may hold values from -6 to 6
- out_grad: bfloat16 [4096, 1024], P(('expert', 'dp')), may hold values from -0.59765625 to 0.59765625
- expert_ids: int32 [4096, 3], P(('expert', 'dp')), may hold values from 0 to 7, all different within a row; in each aligned block of 128 rows (0 to 127, 128 to 255, ...) at most 64 rows name the same one
- gate_probs: float32 [4096, 3], P(('expert', 'dp')), may hold values from 0.05 to 0.5
- w_gate: bfloat16 [8, 1024, 384], P('expert'), may hold values from -0.1875 to 0.1875
- w_up: bfloat16 [8, 1024, 384], P('expert'), may hold values from -0.1875 to 0.1875
- w_down: bfloat16 [8, 384, 1024], P('expert'), may hold values from -0.3125 to 0.3125
Outputs:
- grad_gate: bfloat16 [8, 1024, 384], P('expert', 'dp')
- grad_up: bfloat16 [8, 1024, 384], P('expert', 'dp')
- grad_down: bfloat16 [8, 384, 1024], P('expert', 'dp')
The draws below stay inside these ranges and needn't reach their ends.
Inputs may be any that keep to these rules, and one draw needn't show every extreme that they name: `expert_ids`: each row names 3 different experts. In the 128 rows of one device no expert is named by more than 64 rows, a bound that some block reaches.
All inputs are finite; a program needn't handle non-finite values.
Results may differ from the reference program's by a relative error of at most 0.018.
Values may be sent and summed in bfloat16 or wider, within the bound.
A program may use at most 64 MiB of HBM per device.

```python
import math
import jax
import jax.numpy as jnp
import numpy as np
from jax import lax

D = 1024
H = 384
TOP = 3
TOK_DEV = 128
EXPERTS = 8
CAP = 64
TOKENS = 4096
N_EXPERT = 8
N_DP = 4


def shard_levels(own_key, dims, split, least, largest):
    def one(position, parts):
        draws = jax.random.uniform(jax.random.fold_in(jax.random.fold_in(own_key, 6), position), (parts,), jnp.float32, least / len(split), largest / len(split))
        return jnp.repeat(jnp.exp(draws), dims[position] // parts).reshape((-1,) + (1,) * (len(dims) - position - 1))

    loudness = one(*split[0])
    for cut in split[1:]:
        loudness = loudness * one(*cut)
    return loudness


def deal_out(key, own, number, rows, amount, top, most, slope):
    sequence = jax.random.permutation(key, amount)
    packed, common = portions_of(amount, rows * top, most, slope, True), portions_of(amount, rows * top, most, slope, False)
    places = jnp.arange(amount)

    def named(lengths, offset_by):
        used = int((lengths > 0).sum())
        fixed = max(1, used // 4)
        shifted = fixed + (places - fixed + offset_by * (used - fixed)) % max(1, amount - fixed)
        return jnp.zeros((amount,), jnp.int32).at[sequence[jnp.where(places < fixed, places, shifted)]].set(jnp.asarray(lengths, jnp.int32))

    lengths = jnp.where(number % 4 == 0, named(packed, number // 4), named(common, number - number // 4 - 1))
    mixed = jax.random.permutation(jax.random.fold_in(own, 3), amount)
    donor, taker = mixed[0:amount // 2 * 2:2], mixed[1:amount // 2 * 2:2]
    margin = jnp.minimum(lengths[donor] - 1, most - lengths[taker]) // 2
    margin = jnp.where((donor == sequence[0]) | (taker == sequence[0]) | (lengths[taker] == 0), 0, jnp.maximum(margin, 0))
    shifted = jax.random.randint(jax.random.fold_in(own, 4), (amount // 2,), 0, 1 << 20) % (margin + 1)
    lengths = lengths.at[donor].add(-shifted).at[taker].add(shifted)
    items = jnp.searchsorted(jnp.cumsum(lengths), jnp.arange(rows * top), side="right").astype(jnp.int32)
    listing = items.reshape(top, rows).T
    listing = listing[jax.random.permutation(jax.random.fold_in(own, 1), rows)]
    offset_by = jax.random.randint(jax.random.fold_in(own, 2), (rows, 1), 0, top)
    return jnp.take_along_axis(listing, (jnp.arange(top)[None, :] + offset_by) % top, axis=1)


def portions_of(count, total, most, lean, full):
    loads = [(1 << 20) // math.isqrt(rank ** lean) + 1 for rank in range(1, count + 1)]
    largest = most if full else min(most, max(-(-total // count), total * loads[0] // sum(loads)))
    least = 1 if total - largest >= count - 1 else 0
    given, rest = [largest] + [least] * (count - 1), total - largest - least * (count - 1)
    while rest > 0:
        movable = [i for i in range(1, count) if given[i] < largest] or [i for i in range(1, count) if given[i] < most]
        mass, left = sum([loads[i] for i in movable]), rest
        for i in movable:
            more = min(most - given[i], max(1, left * loads[i] // mass), rest)
            given[i] = given[i] + more
            rest = rest - more
    return np.array(given)


def scatter_about(rng, extent, width, most, cuts=(), dtype=jnp.bfloat16):
    result = jax.random.normal(rng, extent, jnp.float32) * width
    if len(cuts) > 0:
        result = shard_levels(rng, extent, cuts, -0.22, 0.18) * result
    return jnp.clip(result, min=-most, max=most).astype(dtype)


def setup_inputs(seed: int = 0) -> dict:
    splits = jax.random.split(jax.random.key(seed), 8)
    tokens = scatter_about(splits[0], (TOKENS, D), 1.0, 6.0, ((0, 32),))
    out_grad = scatter_about(splits[1], (TOKENS, D), 0.1, 0.59765625, ((0, 32),))
    expert_ids_keys = jax.random.split(jax.random.fold_in(splits[2], 1), TOKENS // TOK_DEV)
    expert_ids_turns = jax.random.permutation(jax.random.fold_in(splits[2], 3), TOKENS // TOK_DEV)
    expert_ids = jax.vmap(lambda own, number: deal_out(jax.random.fold_in(splits[2], 2), own, number, TOK_DEV, EXPERTS, TOP, CAP, 2))(expert_ids_keys, expert_ids_turns).reshape((TOKENS, TOP))
    gate_probs = jnp.clip(0.05 + 0.45 * jax.random.uniform(splits[3], (TOKENS, TOP), jnp.float32) ** shard_levels(splits[3], (TOKENS, TOP), ((0, 32),), -0.2, 0.2), 0.05, 0.5)
    w_gate = scatter_about(splits[4], (EXPERTS, D, H), D ** -0.5, 0.1875, ((0, 8),))
    w_up = scatter_about(splits[5], (EXPERTS, D, H), D ** -0.5, 0.1875, ((0, 8),))
    w_down = scatter_about(splits[6], (EXPERTS, H, D), H ** -0.5, 0.3125, ((0, 8),))
    return dict(tokens=tokens, out_grad=out_grad, expert_ids=expert_ids, gate_probs=gate_probs, w_gate=w_gate, w_up=w_up, w_down=w_down)


def expert_grads(rows_in, rows_grad, gate_w, up_w, down_w):
    gate_pre = jnp.dot(rows_in, gate_w, preferred_element_type=jnp.float32)
    up_pre = jnp.dot(rows_in, up_w, preferred_element_type=jnp.float32)
    sigma = jax.nn.sigmoid(gate_pre)
    active = gate_pre * sigma
    hidden = (active * up_pre).astype(jnp.bfloat16)
    grad_down = lax.dot_general(hidden, rows_grad, (((0,), (0,)), ((), ())), preferred_element_type=jnp.float32)
    grad_hidden = lax.dot_general(rows_grad, down_w, (((1,), (1,)), ((), ())), preferred_element_type=jnp.float32)
    grad_upper = (grad_hidden * active).astype(jnp.bfloat16)
    grad_gate_pre = (grad_hidden * up_pre * sigma * (1.0 + gate_pre * (1.0 - sigma))).astype(jnp.bfloat16)
    grad_gate = lax.dot_general(rows_in, grad_gate_pre, (((0,), (0,)), ((), ())), preferred_element_type=jnp.float32)
    grad_up = lax.dot_general(rows_in, grad_upper, (((0,), (0,)), ((), ())), preferred_element_type=jnp.float32)
    return grad_gate, grad_up, grad_down


def regroup(array):
    tail = array.shape[1:]
    shaped = array.reshape((N_EXPERT, N_DP, TOK_DEV) + tail)
    shaped = jnp.swapaxes(shaped, 0, 1)
    return shaped.reshape((N_DP, N_EXPERT * TOK_DEV) + tail)


def reference(tokens, out_grad, expert_ids, gate_probs, w_gate, w_up, w_down):
    group_tokens = regroup(tokens)
    group_cot = regroup(out_grad)
    group_ids = regroup(expert_ids)
    group_probs = regroup(gate_probs)
    limit = N_EXPERT * CAP

    def one_group(carry, inputs):
        tok_block, cot_block, id_block, prob_block = inputs
        flat_ids = id_block.reshape(-1)
        flat_probs = prob_block.reshape(-1)

        def one_expert(expert):
            chosen = flat_ids == expert
            picked = jnp.nonzero(chosen, size=limit, fill_value=0)[0]
            valid = jnp.arange(limit) < jnp.sum(chosen.astype(jnp.int32))
            token_row = picked // TOP
            rows_in = jnp.where(valid[:, None], tok_block[token_row], jnp.zeros((), jnp.bfloat16)).astype(jnp.bfloat16)
            scaled = flat_probs[picked][:, None] * cot_block[token_row].astype(jnp.float32)
            scaled = jnp.where(valid[:, None], scaled, jnp.zeros((), jnp.float32)).astype(jnp.bfloat16)
            grads = expert_grads(rows_in, scaled, w_gate[expert], w_up[expert], w_down[expert])
            return (grads[0].astype(jnp.bfloat16), grads[1].astype(jnp.bfloat16), grads[2].astype(jnp.bfloat16))

        stacked = lax.map(one_expert, jnp.arange(EXPERTS))
        carry = (carry[0] + stacked[0].astype(jnp.float32), carry[1] + stacked[1].astype(jnp.float32), carry[2] + stacked[2].astype(jnp.float32))
        return carry, None

    start = (jnp.zeros((EXPERTS, D, H), jnp.float32), jnp.zeros((EXPERTS, D, H), jnp.float32), jnp.zeros((EXPERTS, H, D), jnp.float32))
    totals, _ = lax.scan(one_group, start, (group_tokens, group_cot, group_ids, group_probs))
    return totals[0].astype(jnp.bfloat16), totals[1].astype(jnp.bfloat16), totals[2].astype(jnp.bfloat16)
```

```python
import functools
import math

import jax
import jax.numpy as jnp
from jax import lax
from jax.experimental import pallas as pl
from jax.experimental.pallas import tpu as pltpu
from jax.sharding import PartitionSpec as P

MESH = pl.DeviceIdType.MESH
CORES = 2


def kernel(
    n_e, n_a, n_b,
    tok, cot, ids_in, probs_in, wg_in, wu_in, wd_in,
    out_g, out_u, out_d,
    ids, probs, X, G, PT, WG, WU, WD, GU, XT, HT, GG, S, MB, DB, MR, DR, MP, DP, MQ, DQ,
    lsem, chain_s, sib_s, blk_r, one_s, one_r, two_s, two_r,
):
    n_d = n_a * n_b
    rows, width = tok.shape
    hid = wg_in.shape[2]
    top = ids_in.shape[0]
    n_z = n_e // CORES
    me = lax.axis_index("expert")
    dd = lax.axis_index("dp")
    z, c = me // CORES, me % CORES
    sib = z * CORES + (1 - c)

    barrier = pltpu.get_barrier_semaphore()
    for step in (-1, 1):
        @pl.when(jnp.logical_and(z + step >= 0, z + step < n_z))
        def _():
            pl.semaphore_signal(barrier, inc=1, device_id={"expert": me + step * CORES}, device_id_type=MESH)
    pl.semaphore_signal(barrier, inc=1, device_id={"expert": sib}, device_id_type=MESH)
    for i in range(1, n_a):
        pl.semaphore_signal(barrier, inc=1, device_id={"dp": ((dd // n_b + i) % n_a) * n_b + dd % n_b}, device_id_type=MESH)
    for i in range(1, n_b):
        pl.semaphore_signal(barrier, inc=1, device_id={"dp": dd // n_b * n_b + (dd % n_b + i) % n_b}, device_id_type=MESH)
    small = [
        pltpu.make_async_copy(ids_in, ids, lsem.at[5]),
        pltpu.make_async_copy(probs_in, probs, lsem.at[6]),
    ]
    for copy in small:
        copy.start()
    for copy in small:
        copy.wait()
    erow = lax.broadcasted_iota(jnp.int32, PT.shape[1:], 0)
    table = jnp.zeros(PT.shape[1:], jnp.float32)
    for k in range(top):
        table = table + jnp.where(ids[k : k + 1, :] == erow, probs[k : k + 1, :], 0.0)
    PT[me] = table

    arrivals = n_a + n_b - 1 + jnp.where(z > 0, 1, 0) + jnp.where(z < n_z - 1, 1, 0)
    pl.semaphore_wait(barrier, arrivals)

    full = (PT, X, G)
    own = (PT.at[me], tok, cot)

    def hop(k, d, src, mine):
        there = me + (CORES if d == 0 else -CORES)
        return pltpu.make_async_remote_copy(
            src_ref=own[k] if mine else full[k].at[src],
            dst_ref=full[k].at[src],
            send_sem=chain_s.at[k, d, src],
            recv_sem=blk_r.at[k, src],
            device_id={"expert": there},
            device_id_type=MESH,
        )

    def across(k, src, mine):
        return pltpu.make_async_remote_copy(
            src_ref=own[k] if mine else full[k].at[src],
            dst_ref=full[k].at[src],
            send_sem=sib_s.at[k, src],
            recv_sem=blk_r.at[k, src],
            device_id={"expert": sib},
            device_id_type=MESH,
        )

    def can(d):
        return z < n_z - 1 if d == 0 else z > 0

    for k in range(3):
        for d in range(2):
            @pl.when(can(d))
            def _():
                hop(k, d, me, True).start()
        across(k, me, True).start()
    local = [
        pltpu.make_async_copy(tok, X.at[me], lsem.at[0]),
        pltpu.make_async_copy(cot, G.at[me], lsem.at[1]),
        pltpu.make_async_copy(wg_in.at[0], WG, lsem.at[2]),
        pltpu.make_async_copy(wu_in.at[0], WU, lsem.at[3]),
        pltpu.make_async_copy(wd_in.at[0], WD, lsem.at[4]),
    ]
    for copy in local:
        copy.start()
    for copy in local:
        copy.wait()

    pair = CORES * rows

    def base(zz):
        return pl.multiple_of(zz * pair, pair)

    def forward_tokens(zz, d):
        for k in range(2):
            across(k, zz * CORES + (1 - c), False).wait_recv()
        x = X[pl.ds(zz * CORES, CORES)].reshape(pair, width)
        GU[d, :, :hid] = jnp.dot(x, WG[...], preferred_element_type=jnp.float32)
        GU[d, :, hid:] = jnp.dot(x, WU[...], preferred_element_type=jnp.float32)
        XT[:, pl.ds(base(zz), pair)] = x.T

    def forward_cots(zz, d):
        across(2, zz * CORES + (1 - c), False).wait_recv()
        at = base(zz)
        parts = []
        for h in range(CORES):
            p = PT[zz * CORES + h, pl.ds(me, 1), :]
            p = jnp.broadcast_to(p, (rows, rows)).T[:, :1]
            parts.append((p * G[zz * CORES + h].astype(jnp.float32)).astype(jnp.bfloat16))
        scaled = jnp.concatenate(parts, axis=0)
        S[pl.ds(at, pair), :] = scaled
        gh = lax.dot_general(scaled, WD[...], (((1,), (1,)), ((), ())), preferred_element_type=jnp.float32)
        gate, up = GU[d, :, :hid], GU[d, :, hid:]
        sigma = jax.nn.sigmoid(gate)
        active = gate * sigma
        GG[pl.ds(at, pair), :hid] = (gh * up * sigma * (1.0 + gate * (1.0 - sigma))).astype(jnp.bfloat16)
        GG[pl.ds(at, pair), hid:] = (gh * active).astype(jnp.bfloat16)
        HT[:, pl.ds(at, pair)] = (active * up).astype(jnp.bfloat16).T

    def both(s, work):
        @pl.loop(0, 2)
        def _(d):
            zz = jnp.where(d == 0, z - s, z + s)

            @pl.when((zz >= 0) & (zz < n_z) & ((s > 0) | (d == 0)))
            def _():
                work(zz, d)

    def pass_on(s, kinds):
        for k in kinds:
            for d in range(2):
                zz = z - s if d == 0 else z + s
                src = zz * CORES + c

                @pl.when((zz >= 0) & (zz < n_z))
                def _():
                    hop(k, d, src, False).wait_recv()

                    @pl.when(can(d))
                    def _():
                        hop(k, d, src, False).start()

                    across(k, src, False).start()

    @pl.loop(0, n_z)
    def _(s):
        @pl.when(s > 0)
        def _():
            pass_on(s, (0, 1))

        both(s, forward_tokens)

        @pl.when(s > 0)
        def _():
            pass_on(s, (2,))

        both(s, forward_cots)

    piece, hpiece = width // n_d, hid // n_d
    chunk = max(piece, min(256, width))
    n_c = width // chunk
    hchunk, per = hid // n_c, chunk // piece
    half = width // 2

    def index(p, second, first):
        return second * n_b + first if p == 0 else first * n_b + second

    def first_of(p, j):
        return j % n_b if p == 0 else j // n_b

    def second_of(p, j):
        return j // n_b if p == 0 else j % n_b

    def mpiece(p, j):
        return MB.at[p, pl.ds(pl.multiple_of(j * piece, piece), piece)]

    def one(p, t, j):
        mine, there = first_of(p, dd), second_of(p, j)
        return pltpu.make_async_remote_copy(
            src_ref=mpiece(p, j) if t == 0 else DB.at[p, j],
            dst_ref=(MR if t == 0 else DR).at[p, mine, there],
            send_sem=one_s.at[p, t, j],
            recv_sem=one_r.at[p, t, mine, there],
            device_id={"dp": index(p, second_of(p, dd), first_of(p, j))},
            device_id_type=MESH,
        )

    def one_from(p, t, first, second):
        dst = (MR if t == 0 else DR).at[p, first, second]
        return pltpu.make_async_remote_copy(
            src_ref=dst, dst_ref=dst,
            send_sem=one_s.at[p, t, 0],
            recv_sem=one_r.at[p, t, first, second],
            device_id={"dp": index(p, second_of(p, dd), first)},
            device_id_type=MESH,
        )

    def two(p, t, second, slot):
        return pltpu.make_async_remote_copy(
            src_ref=(MP if t == 0 else DP).at[p, second],
            dst_ref=(MQ if t == 0 else DQ).at[p, slot],
            send_sem=two_s.at[p, t, second],
            recv_sem=two_r.at[p, t, slot],
            device_id={"dp": index(p, second, first_of(p, dd))},
            device_id_type=MESH,
        )

    @pl.loop(0, n_c)
    def _(i):
        if per == 1:
            step_a, step_b = n_a - 1 - i // n_b, n_b - 1 - i % n_b
            cc = ((dd // n_b + step_a) % n_a) * n_b + (dd % n_b + step_b) % n_b
        else:
            cc = (dd // per + 1 + i) % n_c
        at = pl.multiple_of(cc * chunk, chunk)
        hat = pl.multiple_of(cc * hchunk, hchunk)
        up_gate = jnp.dot(
            XT[pl.ds(at, chunk), :], GG[...], preferred_element_type=jnp.float32
        ).astype(jnp.bfloat16)
        for p in range(2):
            MB[p, pl.ds(at, chunk), :] = up_gate[:, p * hid : (p + 1) * hid]
        for t in range(2):
            if t == 1:
                down = jnp.dot(
                    HT[pl.ds(hat, hchunk), :], S[...], preferred_element_type=jnp.float32
                ).astype(jnp.bfloat16)
                for p in range(2):
                    for q in range(per):
                        DB[p, cc * per + q] = down[q * hpiece : (q + 1) * hpiece, p * half : (p + 1) * half]
            for p in range(2):
                for q in range(per):
                    j = cc * per + q

                    @pl.when(first_of(p, j) != first_of(p, dd))
                    def _():
                        one(p, t, j).start()

    def partial(p, t, second):
        first = first_of(p, dd)
        count = n_b if p == 0 else n_a
        j = index(p, second, first)
        total = (mpiece(p, j)[...] if t == 0 else DB[p, j]).astype(jnp.float32)
        for i in range(1, count):
            other = (first + i) % count
            one_from(p, t, other, second).wait_recv()
            total = total + (MR if t == 0 else DR)[p, other, second].astype(jnp.float32)
        return total

    for t in range(2):
        for p in range(2):
            count = n_a if p == 0 else n_b

            @pl.loop(1, count)
            def _(i):
                second = (second_of(p, dd) + i) % count
                (MP if t == 0 else DP)[p, second] = partial(p, t, second).astype(jnp.bfloat16)
                two(p, t, second, second_of(p, dd)).start()

    for t in range(2):
        for p in range(2):
            count = n_a if p == 0 else n_b
            mine = second_of(p, dd)
            total = partial(p, t, mine)
            for i in range(1, count):
                other = (mine + i) % count
                two(p, t, other, other).wait_recv()
                total = total + (MQ if t == 0 else DQ)[p, other].astype(jnp.float32)
            if t == 0:
                (out_g, out_u)[p][0] = total.astype(jnp.bfloat16)
            else:
                out_d[0, :, p * half : (p + 1) * half] = total.astype(jnp.bfloat16)

    for p in range(2):
        for t in range(2):
            @pl.loop(0, n_d)
            def _(j):
                @pl.when(first_of(p, j) != first_of(p, dd))
                def _():
                    one(p, t, j).wait_send()

            count = n_a if p == 0 else n_b

            @pl.loop(1, count)
            def _(i):
                two(p, t, (second_of(p, dd) + i) % count, second_of(p, dd)).wait_send()

    @pl.loop(0, n_z)
    def _(s):
        for k in range(3):
            for d in range(2):
                zz = z - s if d == 0 else z + s
                src = zz * CORES + c

                @pl.when((zz >= 0) & (zz < n_z) & can(d))
                def _():
                    hop(k, d, src, False).wait_send()

            across(k, s * CORES + c, False).wait_send()


def copy_out(*refs):
    n = len(refs) // 2
    copies = [pltpu.make_async_copy(refs[i], refs[n + i], refs[-1].at[i]) for i in range(n)]
    for copy in copies:
        copy.start()
    for copy in copies:
        copy.wait()


def write_out(arrays):
    anywhere = pl.BlockSpec(memory_space=pl.ANY)
    return pl.pallas_call(
        copy_out,
        out_shape=tuple(jax.ShapeDtypeStruct(x.shape, x.dtype) for x in arrays),
        in_specs=[anywhere] * len(arrays),
        out_specs=(anywhere,) * len(arrays),
        scratch_shapes=[pltpu.SemaphoreType.DMA((len(arrays),))],
        compiler_params=pltpu.CompilerParams(vmem_limit_bytes=1 << 20),
    )(*arrays)


def grid_kernel(
    n_e, cap, n_q,
    tok, cot, ids_in, probs_in, wg_in, wu_in, wd_in,
    out_g, out_u, out_d,
    ids, probs, TB, SEL, PSC, B, C, RC, WG, WU, WD, E, WGG, WUU, WDD, GA, UP, XT, GG, HT,
    SM, SD, RM, RD, OM, OD, TM, TD, FM, FD,
    small_l, own_l, wt_l, wt_s, wt_r, tab_s, tab_r, blk_s, blk_r, row_s, row_r,
    red_s, red_r, fin_s, fin_r,
):
    bf, f32 = jnp.bfloat16, jnp.float32
    rows, width = tok.shape
    hid = wg_in.shape[2]
    top = ids_in.shape[0]
    n_z = n_e // CORES
    cw = width // n_q
    me = lax.axis_index("expert")
    dd = lax.axis_index("dp")
    z, c = me // CORES, me % CORES
    y, x = dd // 2, dd % 2
    sib = z * CORES + (1 - c)
    g, f = jnp.where(c == 0, x, y), jnp.where(c == 0, y, x)
    across_x, across_y = y * 2 + (1 - x), (1 - y) * 2 + x

    def greet(where):
        pl.semaphore_signal(barrier, inc=1, device_id=where, device_id_type=MESH)

    barrier = pltpu.get_barrier_semaphore()
    for step in (-1, 1):
        @pl.when(jnp.logical_and(z + step >= 0, z + step < n_z))
        def _():
            greet({"expert": me + step * CORES, "dp": dd})
    greet({"expert": sib, "dp": dd})
    for other in (across_x, across_y):
        for core in range(CORES):
            greet({"expert": z * CORES + core, "dp": other})

    small = [
        pltpu.make_async_copy(ids_in, ids, small_l.at[0]),
        pltpu.make_async_copy(probs_in, probs, small_l.at[1]),
    ]
    for copy in small:
        copy.start()

    def own_copy(k, q):
        return pltpu.make_async_copy(
            (tok, cot)[k].at[:, pl.ds(q * cw, cw)], B.at[k, z, q], own_l.at[k, q]
        )

    for k in range(2):
        for q in range(n_q):
            own_copy(k, q).start()
    for copy in small:
        copy.wait()
    lanes = TB.shape[1] // 2
    erow = lax.broadcasted_iota(jnp.int32, (lanes, rows), 0)
    table = jnp.zeros((lanes, rows), f32)
    named = jnp.zeros((lanes, rows), f32)
    for k in range(top):
        hit = ids[k : k + 1, :] == erow
        table = table + jnp.where(hit, probs[k : k + 1, :], 0.0)
        named = named + jnp.where(hit, 1.0, 0.0)
    before = jnp.where(
        lax.broadcasted_iota(jnp.int32, (rows, rows), 0) < lax.broadcasted_iota(jnp.int32, (rows, rows), 1), 1.0, 0.0
    ).astype(bf)
    place = jnp.dot(named.astype(bf), before, preferred_element_type=f32)
    TB[z, :lanes] = table
    TB[z, lanes:] = jnp.where(named > 0.0, place, -1.0)

    pl.semaphore_wait(barrier, 5 + jnp.where(z > 0, 1, 0) + jnp.where(z < n_z - 1, 1, 0))

    def onward(d):
        return {"expert": me + jnp.where(d == 0, CORES, -CORES), "dp": dd}

    def can(d):
        return jnp.where(d == 0, n_z - 1 - z, z) > 0

    def plane(s, d):
        return jnp.where(d == 0, z - s, z + s)

    def tab_hop(d, src):
        return pltpu.make_async_remote_copy(
            src_ref=TB.at[src], dst_ref=TB.at[src], send_sem=tab_s.at[d, src], recv_sem=tab_r.at[src],
            device_id=onward(d), device_id_type=MESH,
        )

    def hop(k, q, d, src, mine):
        return pltpu.make_async_remote_copy(
            src_ref=(tok, cot)[k].at[:, pl.ds(q * cw, cw)] if mine else B.at[k, src, q],
            dst_ref=B.at[k, src, q],
            send_sem=blk_s.at[k, q, d, src],
            recv_sem=blk_r.at[k, q, src],
            device_id=onward(d), device_id_type=MESH,
        )

    for d in range(2):
        @pl.when(can(d))
        def _():
            tab_hop(d, z).start()
    for k in range(2):
        for q in range(n_q):
            for d in range(2):
                @pl.when(can(d))
                def _():
                    hop(k, q, d, z, True).start()

    weights = ((wg_in, WG), (wu_in, WU), (wd_in, WD))

    def share(i):
        return pltpu.make_async_remote_copy(
            src_ref=weights[i][0].at[0], dst_ref=weights[i][1], send_sem=wt_s.at[i], recv_sem=wt_r.at[i],
            device_id={"expert": sib, "dp": dd}, device_id_type=MESH,
        )

    def keep(i):
        return pltpu.make_async_copy(weights[i][0].at[0], weights[i][1], wt_l.at[i])

    g_sib = jnp.where(c == 0, y, x)
    mine_here, mine_there = g == c, g_sib == c
    for i in range(3):
        @pl.when(mine_there)
        def _():
            share(i).start()

        @pl.when(mine_here)
        def _():
            keep(i).start()

    half, hh = hid // 2, hid // 8
    for slot in range(2):
        for t in range(2):
            j = lax.broadcasted_iota(jnp.int32, (hid, hid), 0) - t * half
            u = j + slot * hh
            for cut in range(1, 4):
                u = u + jnp.where(j >= cut * hh, hh, 0)
            inside = (j >= 0) & (j < half)
            there = lax.broadcasted_iota(jnp.int32, (hid, hid), 1)
            E[slot, t] = jnp.where(inside & (u == there), 1.0, 0.0).astype(bf)

    def row(k, q, src, to, part):
        where = (
            {"expert": sib, "dp": dd},
            {"expert": z * CORES, "dp": across_x},
            {"expert": z * CORES + 1, "dp": across_y},
        )[to]
        return pltpu.make_async_remote_copy(
            src_ref=C.at[k, src, q, (g_sib, 1 - x, 1 - y)[to]],
            dst_ref=RC.at[k, q, src, part],
            send_sem=row_s.at[k, q, src, to],
            recv_sem=row_r.at[k, q, src, part],
            device_id=where, device_id_type=MESH,
        )

    def each(s, work):
        @pl.loop(0, 2)
        def _(d):
            src = plane(s, d)

            @pl.when((src >= 0) & (src < n_z) & ((s > 0) | (d == 0)))
            def _():
                work(src, d)

    def tables(s):
        def work(src, d):
            @pl.when(s > 0)
            def _():
                tab_hop(d, src).wait_recv()

                @pl.when(can(d))
                def _():
                    tab_hop(d, src).start()

            slot = lax.broadcasted_iota(jnp.int32, (cap, rows), 0).astype(f32)
            for ee in range(2):
                hit = TB[src, pl.ds(lanes + z * CORES + ee, 1), :] == slot
                SEL[src, ee * cap : (ee + 1) * cap] = jnp.where(hit, 1.0, 0.0).astype(bf)
                weight = jnp.where(hit, TB[src, pl.ds(z * CORES + ee, 1), :], 0.0).sum(axis=1, keepdims=True)
                PSC[src, ee * cap : (ee + 1) * cap] = jnp.broadcast_to(weight, (cap, 128))

        each(s, work)

    def arrive(s, k, q):
        def work(src, d):
            @pl.when(s == 0)
            def _():
                own_copy(k, q).wait()

            @pl.when(s > 0)
            def _():
                hop(k, q, d, src, False).wait_recv()

                @pl.when(can(d))
                def _():
                    hop(k, q, d, src, False).start()

            picked = jnp.dot(SEL[src], B[k, src, q], preferred_element_type=f32)
            if k == 1:
                picked = picked * PSC[src][:, :1]
            C[k, src, q] = picked.astype(bf).reshape(2, cap, cw)
            row(k, q, src, 1, 2 + c).start()
            row(k, q, src, 2, 2 + c).start()
            row(k, q, src, 0, c).start()
            RC[k, q, src, c] = C[k, src, q, g]

        each(s, work)

    def collect(k, src):
        for q in range(n_q):
            for part in (1 - c, 2, 3):
                row(k, q, src, 0, part).wait_recv()

    block = 4 * cap

    def base(src):
        return pl.multiple_of(src * block, block)

    def forward_tokens(s):
        def work(src, d):
            collect(0, src)
            gate = jnp.zeros((block, hid), f32)
            up = jnp.zeros((block, hid), f32)
            for q in range(n_q):
                xs = RC[0, q, src].reshape(block, cw)
                gate = gate + jnp.dot(xs, WGG[q * cw : (q + 1) * cw], preferred_element_type=f32)
                up = up + jnp.dot(xs, WUU[q * cw : (q + 1) * cw], preferred_element_type=f32)
                XT[q * cw : (q + 1) * cw, pl.ds(base(src), block)] = xs.T
            GA[d] = gate
            UP[d] = up

        each(s, work)

    def forward_cots(s):
        def work(src, d):
            collect(1, src)
            gh = jnp.zeros((block, hid), f32)
            for q in range(n_q):
                gh = gh + lax.dot_general(
                    RC[1, q, src].reshape(block, cw), WDD[:, q * cw : (q + 1) * cw],
                    (((1,), (1,)), ((), ())), preferred_element_type=f32,
                )
            gate, up = GA[d], UP[d]
            sigma = jax.nn.sigmoid(gate)
            active = gate * sigma
            first = lax.broadcasted_iota(jnp.int32, (block, hid), 1) < half
            slope = jnp.where(first, up * sigma * (1.0 + gate * (1.0 - sigma)), active)
            GG[pl.ds(base(src), block), :] = (gh * slope).astype(bf)
            HT[:, pl.ds(base(src), block)] = (active * up).astype(bf).T[:half]

        each(s, work)

    def prepare():
        for i in range(3):
            @pl.when(mine_here)
            def _():
                keep(i).wait()

            @pl.when(jnp.logical_not(mine_here))
            def _():
                share(i).wait_recv()
        spread = (E[c, 0].astype(f32) + E[c, 1].astype(f32)).astype(bf)
        for source, made in ((WG, WGG), (WU, WUU)):
            made[...] = lax.dot_general(
                source[...], spread, (((1,), (1,)), ((), ())), preferred_element_type=f32
            ).astype(bf)
        WDD[...] = jnp.dot(spread, WD[...], preferred_element_type=f32).astype(bf)

    @pl.loop(0, n_z)
    def _(s):
        tables(s)
        for q in range(n_q):
            arrive(s, 0, q)

        @pl.when(s > 0)
        def _():
            forward_cots(s - 1)

        for q in range(n_q - 1):
            arrive(s, 1, q)

        @pl.when(s == 0)
        def _():
            prepare()

        forward_tokens(s)
        arrive(s, 1, n_q - 1)

    forward_cots(n_z - 1)

    piece, hpiece = width // 4, half // 4
    part = piece // 2

    def quarter(ff, gg):
        return jnp.where(c == 0, ff * 2 + gg, gg * 2 + ff)

    def wide(j, t):
        at = pl.multiple_of(j * piece + t * part, part)
        return jnp.dot(XT[pl.ds(at, part), :], GG[...], preferred_element_type=f32)

    def deep(j, q):
        at = pl.multiple_of(j * hpiece, hpiece)
        return jnp.dot(
            HT[pl.ds(at, hpiece), :], RC[1, q].reshape(n_z * block, cw), preferred_element_type=f32
        )

    def spot(M, D, i, t):
        return M.at[i, pl.ds(t * part, part)] if t < 2 else D.at[i]

    def reduce_copy(i, t):
        return pltpu.make_async_remote_copy(
            src_ref=spot(SM, SD, i, t), dst_ref=spot(RM, RD, i, t),
            send_sem=red_s.at[i, t], recv_sem=red_r.at[i, t],
            device_id={"expert": me, "dp": quarter(1 - f, g)}, device_id_type=MESH,
        )

    def final_copy(i, t):
        return pltpu.make_async_remote_copy(
            src_ref=spot(TM, TD, i, t), dst_ref=spot(FM, FD, c, t),
            send_sem=fin_s.at[i, t], recv_sem=fin_r.at[c, t],
            device_id={"expert": z * CORES + g, "dp": quarter(f, 1 - g) if i == 0 else dd}, device_id_type=MESH,
        )

    for i in range(2):
        j = quarter(1 - f, (1 - g) if i == 0 else g)
        for t in range(2):
            SM[i, t * part : (t + 1) * part] = wide(j, t).astype(bf)
            reduce_copy(i, t).start()
        for q in range(n_q):
            SD[i, :, q * cw : (q + 1) * cw] = deep(j, q).astype(bf)
        reduce_copy(i, 2).start()
    for i in range(2):
        j = quarter(f, (1 - g) if i == 0 else g)
        for t in range(2):
            OM[i, t * part : (t + 1) * part] = wide(j, t)
        for q in range(n_q):
            OD[i, :, q * cw : (q + 1) * cw] = deep(j, q)
    for i in range(2):
        for t in range(3):
            reduce_copy(i, t).wait_recv()
            if t < 2:
                at = slice(t * part, (t + 1) * part)
                TM[i, at] = (OM[i, at] + RM[i, at].astype(f32)).astype(bf)
            else:
                TD[i] = (OD[i] + RD[i].astype(f32)).astype(bf)
            if i == 0:
                final_copy(0, t).start()
            else:
                @pl.when(g != c)
                def _():
                    final_copy(1, t).start()

                @pl.when(g == c)
                def _():
                    if t < 2:
                        FM[c, at] = TM[1, at]
                    else:
                        FD[c] = TD[1]

    def landed(slot, t):
        return pltpu.make_async_remote_copy(
            src_ref=spot(FM, FD, slot, t), dst_ref=spot(FM, FD, slot, t),
            send_sem=fin_s.at[0, t], recv_sem=fin_r.at[slot, t],
            device_id={"expert": sib, "dp": dd}, device_id_type=MESH,
        )

    for t in range(3):
        @pl.when(g != c)
        def _():
            landed(c, t).wait_recv()

        landed(1 - c, t).wait_recv()
        if t < 2:
            at = slice(t * part, (t + 1) * part)
            for o, out in enumerate((out_g, out_u)):
                out[0, at] = (
                    jnp.dot(FM[0, at], E[0, o], preferred_element_type=f32)
                    + jnp.dot(FM[1, at], E[1, o], preferred_element_type=f32)
                ).astype(bf)
        else:
            for slot in range(2):
                out_d[0, slot * hpiece : (slot + 1) * hpiece] = FD[slot]

    for i in range(2):
        for t in range(3):
            reduce_copy(i, t).wait_send()
            if i == 0:
                final_copy(0, t).wait_send()
            else:
                @pl.when(g != c)
                def _():
                    final_copy(1, t).wait_send()

    @pl.when(mine_there)
    def _():
        for i in range(3):
            share(i).wait_send()

    @pl.loop(0, n_z)
    def _(src):
        for d in range(2):
            @pl.when(can(d) & (jnp.where(d == 0, z - src, src - z) >= 0))
            def _():
                tab_hop(d, src).wait_send()
                for k in range(2):
                    for q in range(n_q):
                        hop(k, q, d, src, False).wait_send()
        for k in range(2):
            for q in range(n_q):
                for to in range(3):
                    row(k, q, src, to, 0).wait_send()


def grid_step(n_e, tokens, out_grad, expert_ids, gate_probs, w_gate, w_up, w_down):
    rows, width = tokens.shape
    hid = w_gate.shape[2]
    n_z, top, n_q = n_e // CORES, expert_ids.shape[1], 2
    cap = rows * (top + 1) // n_e
    lanes = -(-n_e // 8) * 8
    block, cw, half = 4 * cap, width // n_q, hid // 2
    piece, hpiece = width // 4, hid // 8
    total = n_z * block
    bf, f32 = jnp.bfloat16, jnp.float32
    vmem = pl.BlockSpec(memory_space=pltpu.VMEM)
    hbm = pl.BlockSpec(memory_space=pltpu.HBM)
    dma = pltpu.SemaphoreType.DMA
    scratch = [
        (expert_ids.shape[::-1], expert_ids.dtype),
        (gate_probs.shape[::-1], gate_probs.dtype),
        ((n_z, 2 * lanes, rows), f32),
        ((n_z, 2 * cap, rows), bf),
        ((n_z, 2 * cap, 128), f32),
        ((2, n_z, n_q, rows, cw), bf),
        ((2, n_z, n_q, 2, cap, cw), bf),
        ((2, n_q, n_z, 4, cap, cw), bf),
        ((width, hid), bf),
        ((width, hid), bf),
        ((hid, width), bf),
        ((2, 2, hid, hid), bf),
        ((width, hid), bf),
        ((width, hid), bf),
        ((hid, width), bf),
        ((2, block, hid), f32),
        ((2, block, hid), f32),
        ((width, total), bf),
        ((total, hid), bf),
        ((half, total), bf),
    ]
    scratch += [((2, piece, hid), bf), ((2, hpiece, width), bf)] * 2
    scratch += [((2, piece, hid), f32), ((2, hpiece, width), f32)]
    scratch += [((2, piece, hid), bf), ((2, hpiece, width), bf)] * 2
    held = sum(math.prod(shape) * jnp.dtype(kind).itemsize for shape, kind in scratch)
    args = (tokens, out_grad, expert_ids.T, gate_probs.T, w_gate, w_up, w_down)
    made = pl.pallas_call(
        functools.partial(grid_kernel, n_e, cap, n_q),
        out_shape=(
            jax.ShapeDtypeStruct((1, piece, hid), bf),
            jax.ShapeDtypeStruct((1, piece, hid), bf),
            jax.ShapeDtypeStruct((1, 2 * hpiece, width), bf),
        ),
        in_specs=[hbm] * 7,
        out_specs=(vmem, vmem, vmem),
        scratch_shapes=[pltpu.VMEM(shape, kind) for shape, kind in scratch]
        + [
            dma((2,)),
            dma((2, n_q)),
            dma((3,)),
            dma((3,)),
            dma((3,)),
            dma((2, n_z)),
            dma((n_z,)),
            dma((2, n_q, 2, n_z)),
            dma((2, n_q, n_z)),
            dma((2, n_q, n_z, 3)),
            dma((2, n_q, n_z, 4)),
            dma((2, 3)),
            dma((2, 3)),
            dma((2, 3)),
            dma((2, 3)),
        ],
        compiler_params=pltpu.CompilerParams(
            collective_id=1, has_side_effects=True, vmem_limit_bytes=held + (12 << 20)
        ),
    )(*(pltpu.with_memory_space_constraint(x, pltpu.HBM) for x in args))
    return write_out(made)


def solution(mesh):
    n_e, n_d = mesh.shape["expert"], mesh.shape["dp"]
    n_b = max(b for b in range(1, n_d + 1) if n_d % b == 0 and b * b <= n_d)
    n_a = n_d // n_b

    def step(tokens, out_grad, expert_ids, gate_probs, w_gate, w_up, w_down):
        rows, width = tokens.shape
        hid = w_gate.shape[2]
        total = n_e * rows
        lanes = -(-n_e // 8) * 8
        bf, f32 = jnp.bfloat16, jnp.float32
        vmem = pl.BlockSpec(memory_space=pltpu.VMEM)
        hbm = pl.BlockSpec(memory_space=pltpu.HBM)
        piece, hpiece = width // n_d, hid // n_d
        dma = pltpu.SemaphoreType.DMA
        scratch = [
            (expert_ids.shape[::-1], expert_ids.dtype),
            (gate_probs.shape[::-1], gate_probs.dtype),
            ((n_e, rows, width), bf),
            ((n_e, rows, width), bf),
            ((n_e, lanes, rows), f32),
            ((width, hid), bf),
            ((width, hid), bf),
            ((hid, width), bf),
            ((2, CORES * rows, 2 * hid), f32),
            ((width, total), bf),
            ((hid, total), bf),
            ((total, 2 * hid), bf),
            ((total, width), bf),
            ((2, width, hid), bf),
            ((2, n_d, hpiece, width // 2), bf),
            ((2, n_a, n_a, piece, hid), bf),
            ((2, n_a, n_a, hpiece, width // 2), bf),
            ((2, n_a, piece, hid), bf),
            ((2, n_a, hpiece, width // 2), bf),
            ((2, n_a, piece, hid), bf),
            ((2, n_a, hpiece, width // 2), bf),
        ]
        held = sum(math.prod(shape) * jnp.dtype(kind).itemsize for shape, kind in scratch)
        args = (tokens, out_grad, expert_ids.T, gate_probs.T, w_gate, w_up, w_down)
        made = pl.pallas_call(
            functools.partial(kernel, n_e, n_a, n_b),
            out_shape=(
                jax.ShapeDtypeStruct((1, piece, hid), bf),
                jax.ShapeDtypeStruct((1, piece, hid), bf),
                jax.ShapeDtypeStruct((1, hpiece, width), bf),
            ),
            in_specs=[hbm] * 7,
            out_specs=(vmem, vmem, vmem),
            scratch_shapes=[pltpu.VMEM(shape, kind) for shape, kind in scratch]
            + [
                dma((7,)),
                dma((3, 2, n_e)),
                dma((3, n_e)),
                dma((3, n_e)),
                dma((2, 2, n_d)),
                dma((2, 2, n_a, n_a)),
                dma((2, 2, n_a)),
                dma((2, 2, n_a)),
            ],
            compiler_params=pltpu.CompilerParams(
                collective_id=0, has_side_effects=True, vmem_limit_bytes=held + (10 << 20)
            ),
        )(*(pltpu.with_memory_space_constraint(x, pltpu.HBM) for x in args))
        return write_out(made)

    if n_a == 2 and n_b == 2:
        step = functools.partial(grid_step, n_e)
    spread = P(("expert", "dp"), None)
    return jax.shard_map(
        step,
        mesh=mesh,
        in_specs=(spread, spread, spread, spread) + (P("expert", None, None),) * 3,
        out_specs=(P("expert", "dp", None),) * 3,
        check_vma=False,
    )
```

```python
import functools
import math

import jax
import jax.numpy as jnp
from jax import lax
from jax.experimental import pallas as pl
from jax.experimental.pallas import tpu as pltpu
from jax.sharding import PartitionSpec as P

MESH = pl.DeviceIdType.MESH
CORES = 2
XCUTS, GCUTS = (8,), (4, 4)


def kernel(
    n_e, n_a, n_b,
    tok, cot, ids_in, probs_in, wg_in, wu_in, wd_in,
    out_g, out_u, out_d,
    ids, probs, X, G, PT, WG, WU, WD, GU, XT, HT, GG, S, MB, DB, MR, DR, MP, DP, MQ, DQ,
    lsem, chain_s, sib_s, blk_r, one_s, one_r, two_s, two_r,
):
    n_d = n_a * n_b
    rows, width = tok.shape
    hid = wg_in.shape[2]
    top = ids_in.shape[0]
    n_z = n_e // CORES
    me = lax.axis_index("expert")
    dd = lax.axis_index("dp")
    z, c = me // CORES, me % CORES
    sib = z * CORES + (1 - c)

    barrier = pltpu.get_barrier_semaphore()
    for step in (-1, 1):
        @pl.when(jnp.logical_and(z + step >= 0, z + step < n_z))
        def _():
            pl.semaphore_signal(barrier, inc=1, device_id={"expert": me + step * CORES}, device_id_type=MESH)
    pl.semaphore_signal(barrier, inc=1, device_id={"expert": sib}, device_id_type=MESH)
    for i in range(1, n_a):
        pl.semaphore_signal(barrier, inc=1, device_id={"dp": ((dd // n_b + i) % n_a) * n_b + dd % n_b}, device_id_type=MESH)
    for i in range(1, n_b):
        pl.semaphore_signal(barrier, inc=1, device_id={"dp": dd // n_b * n_b + (dd % n_b + i) % n_b}, device_id_type=MESH)
    small = [
        pltpu.make_async_copy(ids_in, ids, lsem.at[5]),
        pltpu.make_async_copy(probs_in, probs, lsem.at[6]),
    ]
    for copy in small:
        copy.start()
    for copy in small:
        copy.wait()
    erow = lax.broadcasted_iota(jnp.int32, PT.shape[1:], 0)
    table = jnp.zeros(PT.shape[1:], jnp.float32)
    for k in range(top):
        table = table + jnp.where(ids[k : k + 1, :] == erow, probs[k : k + 1, :], 0.0)
    PT[me] = table

    arrivals = n_a + n_b - 1 + jnp.where(z > 0, 1, 0) + jnp.where(z < n_z - 1, 1, 0)
    pl.semaphore_wait(barrier, arrivals)

    full = (PT, X, G)
    own = (PT.at[me], tok, cot)

    def hop(k, d, src, mine):
        there = me + (CORES if d == 0 else -CORES)
        return pltpu.make_async_remote_copy(
            src_ref=own[k] if mine else full[k].at[src],
            dst_ref=full[k].at[src],
            send_sem=chain_s.at[k, d, src],
            recv_sem=blk_r.at[k, src],
            device_id={"expert": there},
            device_id_type=MESH,
        )

    def across(k, src, mine):
        return pltpu.make_async_remote_copy(
            src_ref=own[k] if mine else full[k].at[src],
            dst_ref=full[k].at[src],
            send_sem=sib_s.at[k, src],
            recv_sem=blk_r.at[k, src],
            device_id={"expert": sib},
            device_id_type=MESH,
        )

    def can(d):
        return z < n_z - 1 if d == 0 else z > 0

    for k in range(3):
        for d in range(2):
            @pl.when(can(d))
            def _():
                hop(k, d, me, True).start()
        across(k, me, True).start()
    local = [
        pltpu.make_async_copy(tok, X.at[me], lsem.at[0]),
        pltpu.make_async_copy(cot, G.at[me], lsem.at[1]),
        pltpu.make_async_copy(wg_in.at[0], WG, lsem.at[2]),
        pltpu.make_async_copy(wu_in.at[0], WU, lsem.at[3]),
        pltpu.make_async_copy(wd_in.at[0], WD, lsem.at[4]),
    ]
    for copy in local:
        copy.start()
    for copy in local:
        copy.wait()

    pair = CORES * rows

    def base(zz):
        return pl.multiple_of(zz * pair, pair)

    def forward_tokens(zz, d):
        for k in range(2):
            across(k, zz * CORES + (1 - c), False).wait_recv()
        x = X[pl.ds(zz * CORES, CORES)].reshape(pair, width)
        GU[d, :, :hid] = jnp.dot(x, WG[...], preferred_element_type=jnp.float32)
        GU[d, :, hid:] = jnp.dot(x, WU[...], preferred_element_type=jnp.float32)
        XT[:, pl.ds(base(zz), pair)] = x.T

    def forward_cots(zz, d):
        across(2, zz * CORES + (1 - c), False).wait_recv()
        at = base(zz)
        parts = []
        for h in range(CORES):
            p = PT[zz * CORES + h, pl.ds(me, 1), :]
            p = jnp.broadcast_to(p, (rows, rows)).T[:, :1]
            parts.append((p * G[zz * CORES + h].astype(jnp.float32)).astype(jnp.bfloat16))
        scaled = jnp.concatenate(parts, axis=0)
        S[pl.ds(at, pair), :] = scaled
        gh = lax.dot_general(scaled, WD[...], (((1,), (1,)), ((), ())), preferred_element_type=jnp.float32)
        gate, up = GU[d, :, :hid], GU[d, :, hid:]
        sigma = jax.nn.sigmoid(gate)
        active = gate * sigma
        GG[pl.ds(at, pair), :hid] = (gh * up * sigma * (1.0 + gate * (1.0 - sigma))).astype(jnp.bfloat16)
        GG[pl.ds(at, pair), hid:] = (gh * active).astype(jnp.bfloat16)
        HT[:, pl.ds(at, pair)] = (active * up).astype(jnp.bfloat16).T

    def both(s, work):
        @pl.loop(0, 2)
        def _(d):
            zz = jnp.where(d == 0, z - s, z + s)

            @pl.when((zz >= 0) & (zz < n_z) & ((s > 0) | (d == 0)))
            def _():
                work(zz, d)

    def pass_on(s, kinds):
        for k in kinds:
            for d in range(2):
                zz = z - s if d == 0 else z + s
                src = zz * CORES + c

                @pl.when((zz >= 0) & (zz < n_z))
                def _():
                    hop(k, d, src, False).wait_recv()

                    @pl.when(can(d))
                    def _():
                        hop(k, d, src, False).start()

                    across(k, src, False).start()

    @pl.loop(0, n_z)
    def _(s):
        @pl.when(s > 0)
        def _():
            pass_on(s, (0, 1))

        both(s, forward_tokens)

        @pl.when(s > 0)
        def _():
            pass_on(s, (2,))

        both(s, forward_cots)

    piece, hpiece = width // n_d, hid // n_d
    chunk = max(piece, min(256, width))
    n_c = width // chunk
    hchunk, per = hid // n_c, chunk // piece
    half = width // 2

    def index(p, second, first):
        return second * n_b + first if p == 0 else first * n_b + second

    def first_of(p, j):
        return j % n_b if p == 0 else j // n_b

    def second_of(p, j):
        return j // n_b if p == 0 else j % n_b

    def mpiece(p, j):
        return MB.at[p, pl.ds(pl.multiple_of(j * piece, piece), piece)]

    def one(p, t, j):
        mine, there = first_of(p, dd), second_of(p, j)
        return pltpu.make_async_remote_copy(
            src_ref=mpiece(p, j) if t == 0 else DB.at[p, j],
            dst_ref=(MR if t == 0 else DR).at[p, mine, there],
            send_sem=one_s.at[p, t, j],
            recv_sem=one_r.at[p, t, mine, there],
            device_id={"dp": index(p, second_of(p, dd), first_of(p, j))},
            device_id_type=MESH,
        )

    def one_from(p, t, first, second):
        dst = (MR if t == 0 else DR).at[p, first, second]
        return pltpu.make_async_remote_copy(
            src_ref=dst, dst_ref=dst,
            send_sem=one_s.at[p, t, 0],
            recv_sem=one_r.at[p, t, first, second],
            device_id={"dp": index(p, second_of(p, dd), first)},
            device_id_type=MESH,
        )

    def two(p, t, second, slot):
        return pltpu.make_async_remote_copy(
            src_ref=(MP if t == 0 else DP).at[p, second],
            dst_ref=(MQ if t == 0 else DQ).at[p, slot],
            send_sem=two_s.at[p, t, second],
            recv_sem=two_r.at[p, t, slot],
            device_id={"dp": index(p, second, first_of(p, dd))},
            device_id_type=MESH,
        )

    @pl.loop(0, n_c)
    def _(i):
        if per == 1:
            step_a, step_b = n_a - 1 - i // n_b, n_b - 1 - i % n_b
            cc = ((dd // n_b + step_a) % n_a) * n_b + (dd % n_b + step_b) % n_b
        else:
            cc = (dd // per + 1 + i) % n_c
        at = pl.multiple_of(cc * chunk, chunk)
        hat = pl.multiple_of(cc * hchunk, hchunk)
        up_gate = jnp.dot(
            XT[pl.ds(at, chunk), :], GG[...], preferred_element_type=jnp.float32
        ).astype(jnp.bfloat16)
        for p in range(2):
            MB[p, pl.ds(at, chunk), :] = up_gate[:, p * hid : (p + 1) * hid]
        for t in range(2):
            if t == 1:
                down = jnp.dot(
                    HT[pl.ds(hat, hchunk), :], S[...], preferred_element_type=jnp.float32
                ).astype(jnp.bfloat16)
                for p in range(2):
                    for q in range(per):
                        DB[p, cc * per + q] = down[q * hpiece : (q + 1) * hpiece, p * half : (p + 1) * half]
            for p in range(2):
                for q in range(per):
                    j = cc * per + q

                    @pl.when(first_of(p, j) != first_of(p, dd))
                    def _():
                        one(p, t, j).start()

    def partial(p, t, second):
        first = first_of(p, dd)
        count = n_b if p == 0 else n_a
        j = index(p, second, first)
        total = (mpiece(p, j)[...] if t == 0 else DB[p, j]).astype(jnp.float32)
        for i in range(1, count):
            other = (first + i) % count
            one_from(p, t, other, second).wait_recv()
            total = total + (MR if t == 0 else DR)[p, other, second].astype(jnp.float32)
        return total

    for t in range(2):
        for p in range(2):
            count = n_a if p == 0 else n_b

            @pl.loop(1, count)
            def _(i):
                second = (second_of(p, dd) + i) % count
                (MP if t == 0 else DP)[p, second] = partial(p, t, second).astype(jnp.bfloat16)
                two(p, t, second, second_of(p, dd)).start()

    for t in range(2):
        for p in range(2):
            count = n_a if p == 0 else n_b
            mine = second_of(p, dd)
            total = partial(p, t, mine)
            for i in range(1, count):
                other = (mine + i) % count
                two(p, t, other, other).wait_recv()
                total = total + (MQ if t == 0 else DQ)[p, other].astype(jnp.float32)
            if t == 0:
                (out_g, out_u)[p][0] = total.astype(jnp.bfloat16)
            else:
                out_d[0, :, p * half : (p + 1) * half] = total.astype(jnp.bfloat16)

    for p in range(2):
        for t in range(2):
            @pl.loop(0, n_d)
            def _(j):
                @pl.when(first_of(p, j) != first_of(p, dd))
                def _():
                    one(p, t, j).wait_send()

            count = n_a if p == 0 else n_b

            @pl.loop(1, count)
            def _(i):
                two(p, t, (second_of(p, dd) + i) % count, second_of(p, dd)).wait_send()

    @pl.loop(0, n_z)
    def _(s):
        for k in range(3):
            for d in range(2):
                zz = z - s if d == 0 else z + s
                src = zz * CORES + c

                @pl.when((zz >= 0) & (zz < n_z) & can(d))
                def _():
                    hop(k, d, src, False).wait_send()

            across(k, s * CORES + c, False).wait_send()


def copy_out(*refs):
    n = len(refs) // 2
    copies = [pltpu.make_async_copy(refs[i], refs[n + i], refs[-1].at[i]) for i in range(n)]
    for copy in copies:
        copy.start()
    for copy in copies:
        copy.wait()


def write_out(arrays):
    anywhere = pl.BlockSpec(memory_space=pl.ANY)
    return pl.pallas_call(
        copy_out,
        out_shape=tuple(jax.ShapeDtypeStruct(x.shape, x.dtype) for x in arrays),
        in_specs=[anywhere] * len(arrays),
        out_specs=(anywhere,) * len(arrays),
        scratch_shapes=[pltpu.SemaphoreType.DMA((len(arrays),))],
        compiler_params=pltpu.CompilerParams(vmem_limit_bytes=1 << 20),
    )(*arrays)


def grid_kernel(
    n_e, cap, chunks,
    tok, cot, ids_in, probs_in, wg_in, wu_in, wd_in,
    out_g, out_u, out_d,
    ids, probs, TB, SEL, PSC, WG, WU, WD, E, WGG, WUU, WDD, SL, GH, XT, GG, HT,
    SM, SD, RM, RD, OM, OD, TM, TD, FM, FD, *more,
):
    n_c = len(chunks)
    firsts = [i for i, (k, _, _) in enumerate(chunks) if k == 0]
    seconds = [i for i, (k, _, _) in enumerate(chunks) if k == 1]
    groups = [more[i * n_c : (i + 1) * n_c] for i in range(3)]
    B, C, RC = groups
    more = more[3 * n_c :]
    n_s = len(seconds)
    (
        small_l, own_l, wt_l, wt_s, wt_r, tab_s, tab_r, blk_s, blk_r, row_s, row_r,
        red_s, red_r, fin_s, fin_r,
    ) = more
    bf, f32 = jnp.bfloat16, jnp.float32
    rows, width = tok.shape
    hid = wg_in.shape[2]
    top = ids_in.shape[0]
    n_z = n_e // CORES
    me = lax.axis_index("expert")
    dd = lax.axis_index("dp")
    z, c = me // CORES, me % CORES
    y, x = dd // 2, dd % 2
    sib = z * CORES + (1 - c)
    g, f = jnp.where(c == 0, x, y), jnp.where(c == 0, y, x)
    across_x, across_y = y * 2 + (1 - x), (1 - y) * 2 + x

    def greet(where):
        pl.semaphore_signal(barrier, inc=1, device_id=where, device_id_type=MESH)

    barrier = pltpu.get_barrier_semaphore()
    for step in (-1, 1):
        @pl.when(jnp.logical_and(z + step >= 0, z + step < n_z))
        def _():
            greet({"expert": me + step * CORES, "dp": dd})
    greet({"expert": sib, "dp": dd})
    for other in (across_x, across_y):
        for core in range(CORES):
            greet({"expert": z * CORES + core, "dp": other})

    small = [
        pltpu.make_async_copy(ids_in, ids, small_l.at[0]),
        pltpu.make_async_copy(probs_in, probs, small_l.at[1]),
    ]
    for copy in small:
        copy.start()

    def own(i):
        k, at, w = chunks[i]
        return (tok, cot)[k].at[:, pl.ds(at, w)]

    def own_copy(i):
        return pltpu.make_async_copy(own(i), B[i].at[z], own_l.at[i])

    for i in range(n_c):
        own_copy(i).start()
    for copy in small:
        copy.wait()
    lanes = TB.shape[1] // 2
    erow = lax.broadcasted_iota(jnp.int32, (lanes, rows), 0)
    table = jnp.zeros((lanes, rows), f32)
    named = jnp.zeros((lanes, rows), f32)
    for k in range(top):
        hit = ids[k : k + 1, :] == erow
        table = table + jnp.where(hit, probs[k : k + 1, :], 0.0)
        named = named + jnp.where(hit, 1.0, 0.0)
    before = jnp.where(
        lax.broadcasted_iota(jnp.int32, (rows, rows), 0) < lax.broadcasted_iota(jnp.int32, (rows, rows), 1), 1.0, 0.0
    ).astype(bf)
    place = jnp.dot(named.astype(bf), before, preferred_element_type=f32)
    TB[z, :lanes] = table
    TB[z, lanes:] = jnp.where(named > 0.0, place, -1.0)

    pl.semaphore_wait(barrier, 5 + jnp.where(z > 0, 1, 0) + jnp.where(z < n_z - 1, 1, 0))

    def onward(d):
        return {"expert": me + jnp.where(d == 0, CORES, -CORES), "dp": dd}

    def can(d):
        return jnp.where(d == 0, n_z - 1 - z, z) > 0

    def plane(s, d):
        return jnp.where(d == 0, z - s, z + s)

    def tab_hop(d, src):
        return pltpu.make_async_remote_copy(
            src_ref=TB.at[src], dst_ref=TB.at[src], send_sem=tab_s.at[d, src], recv_sem=tab_r.at[src],
            device_id=onward(d), device_id_type=MESH,
        )

    def hop(i, d, src, mine):
        return pltpu.make_async_remote_copy(
            src_ref=own(i) if mine else B[i].at[src],
            dst_ref=B[i].at[src],
            send_sem=blk_s.at[i, d, src],
            recv_sem=blk_r.at[i, src],
            device_id=onward(d), device_id_type=MESH,
        )

    for d in range(2):
        @pl.when(can(d))
        def _():
            tab_hop(d, z).start()
    for i in range(n_c):
        for d in range(2):
            @pl.when(can(d))
            def _():
                hop(i, d, z, True).start()

    weights = ((wg_in, WG), (wu_in, WU), (wd_in, WD))

    def share(i):
        return pltpu.make_async_remote_copy(
            src_ref=weights[i][0].at[0], dst_ref=weights[i][1], send_sem=wt_s.at[i], recv_sem=wt_r.at[i],
            device_id={"expert": sib, "dp": dd}, device_id_type=MESH,
        )

    def keep(i):
        return pltpu.make_async_copy(weights[i][0].at[0], weights[i][1], wt_l.at[i])

    g_sib = jnp.where(c == 0, y, x)
    mine_here, mine_there = g == c, g_sib == c
    for i in range(3):
        @pl.when(mine_there)
        def _():
            share(i).start()

        @pl.when(mine_here)
        def _():
            keep(i).start()

    half, hh = hid // 2, hid // 8
    for slot in range(2):
        for t in range(2):
            j = lax.broadcasted_iota(jnp.int32, (hid, hid), 0) - t * half
            u = j + slot * hh
            for cut in range(1, 4):
                u = u + jnp.where(j >= cut * hh, hh, 0)
            inside = (j >= 0) & (j < half)
            there = lax.broadcasted_iota(jnp.int32, (hid, hid), 1)
            E[slot, t] = jnp.where(inside & (u == there), 1.0, 0.0).astype(bf)

    def row(i, src, to, part):
        where = (
            {"expert": sib, "dp": dd},
            {"expert": z * CORES, "dp": across_x},
            {"expert": z * CORES + 1, "dp": across_y},
        )[to]
        return pltpu.make_async_remote_copy(
            src_ref=C[i].at[src, (g_sib, 1 - x, 1 - y)[to]],
            dst_ref=RC[i].at[src, part],
            send_sem=row_s.at[i, src, to],
            recv_sem=row_r.at[i, src, part],
            device_id=where, device_id_type=MESH,
        )

    def each(s, work):
        @pl.loop(0, 2)
        def _(d):
            src = plane(s, d)

            @pl.when((src >= 0) & (src < n_z) & ((s > 0) | (d == 0)))
            def _():
                work(src, d)

    def tables(s):
        def work(src, d):
            @pl.when(s > 0)
            def _():
                tab_hop(d, src).wait_recv()

                @pl.when(can(d))
                def _():
                    tab_hop(d, src).start()

            slot = lax.broadcasted_iota(jnp.int32, (cap, rows), 0).astype(f32)
            for ee in range(2):
                hit = TB[src, pl.ds(lanes + z * CORES + ee, 1), :] == slot
                SEL[src, ee * cap : (ee + 1) * cap] = jnp.where(hit, 1.0, 0.0).astype(bf)
                weight = jnp.where(hit, TB[src, pl.ds(z * CORES + ee, 1), :], 0.0).sum(axis=1, keepdims=True)
                PSC[src, ee * cap : (ee + 1) * cap] = jnp.broadcast_to(weight, (cap, 128))

        each(s, work)

    def arrive(s, i):
        def work(src, d):
            @pl.when(s == 0)
            def _():
                own_copy(i).wait()

            @pl.when(s > 0)
            def _():
                hop(i, d, src, False).wait_recv()

                @pl.when(can(d))
                def _():
                    hop(i, d, src, False).start()

            picked = jnp.dot(SEL[src], B[i][src], preferred_element_type=f32)
            if chunks[i][0] == 1:
                picked = picked * PSC[src][:, :1]
            C[i][src] = picked.astype(bf).reshape(2, cap, chunks[i][2])
            row(i, src, 1, 2 + c).start()
            row(i, src, 2, 2 + c).start()
            row(i, src, 0, c).start()
            RC[i][src, c] = C[i][src, g]

        each(s, work)

    def collect(i, src):
        for part in (1 - c, 2, 3):
            row(i, src, 0, part).wait_recv()
        return RC[i][src].reshape(block, chunks[i][2])

    block = 4 * cap

    def base(src):
        return pl.multiple_of(src * block, block)

    def forward_tokens(s):
        def work(src, d):
            gate = jnp.zeros((block, hid), f32)
            up = jnp.zeros((block, hid), f32)
            for i in firsts:
                _, at, w = chunks[i]
                xs = collect(i, src)
                gate = gate + jnp.dot(xs, WGG[at : at + w], preferred_element_type=f32)
                up = up + jnp.dot(xs, WUU[at : at + w], preferred_element_type=f32)
                XT[at : at + w, pl.ds(base(src), block)] = xs.T
            sigma = jax.nn.sigmoid(gate)
            active = gate * sigma
            lane = lax.broadcasted_iota(jnp.int32, (block, hid), 1)
            SL[d] = jnp.where(lane < half, up * sigma * (1.0 + gate * (1.0 - sigma)), active)
            HT[:, pl.ds(base(src), block)] = (active * up).astype(bf).T[:half]

        each(s, work)

    def forward_cots(s, which):
        def work(src, d):
            total = jnp.zeros((block, hid), f32) if which[0] == seconds[0] else GH[d]
            for i in which:
                _, at, w = chunks[i]
                total = total + lax.dot_general(
                    collect(i, src), WDD[:, at : at + w], (((1,), (1,)), ((), ())), preferred_element_type=f32
                )
            if which[-1] == seconds[-1]:
                GG[pl.ds(base(src), block), :] = (total * SL[d]).astype(bf)
            else:
                GH[d] = total

        each(s, work)

    def prepare():
        for i in range(3):
            @pl.when(mine_here)
            def _():
                keep(i).wait()

            @pl.when(jnp.logical_not(mine_here))
            def _():
                share(i).wait_recv()
        spread = (E[c, 0].astype(f32) + E[c, 1].astype(f32)).astype(bf)
        for source, made in ((WG, WGG), (WU, WUU)):
            made[...] = lax.dot_general(
                source[...], spread, (((1,), (1,)), ((), ())), preferred_element_type=f32
            ).astype(bf)
        WDD[...] = jnp.dot(spread, WD[...], preferred_element_type=f32).astype(bf)

    @pl.loop(0, n_z - 1)
    def _(s):
        tables(s)
        for i in firsts:
            arrive(s, i)

        @pl.when(s > 0)
        def _():
            forward_cots(s - 1, seconds)

        for i in seconds[:-1]:
            arrive(s, i)

        @pl.when(s == 0)
        def _():
            prepare()

        forward_tokens(s)
        arrive(s, seconds[-1])

    last = n_z - 1
    tables(last)
    for i in firsts:
        arrive(last, i)
    forward_cots(last - 1, seconds)
    arrive(last, seconds[0])
    forward_tokens(last)
    for i in seconds[1:]:
        arrive(last, i)
    for n in range(n_s):
        forward_cots(last, seconds[n : n + 1])

    piece, hpiece = width // 4, half // 4
    part = piece // 2

    def quarter(ff, gg):
        return jnp.where(c == 0, ff * 2 + gg, gg * 2 + ff)

    def wide(j, t):
        at = pl.multiple_of(j * piece + t * part, part)
        return jnp.dot(XT[pl.ds(at, part), :], GG[...], preferred_element_type=f32)

    def deep(j, n):
        at = pl.multiple_of(j * hpiece, hpiece)
        i = seconds[n]
        return jnp.dot(
            HT[pl.ds(at, hpiece), :], RC[i][...].reshape(n_z * block, chunks[i][2]), preferred_element_type=f32
        )

    def columns(n):
        _, at, w = chunks[seconds[n]]
        return slice(at, at + w)

    def spot(M, D, i, t):
        return M.at[i, pl.ds(t * part, part)] if t < 2 else D.at[i]

    def reduce_copy(i, t):
        return pltpu.make_async_remote_copy(
            src_ref=spot(SM, SD, i, t), dst_ref=spot(RM, RD, i, t),
            send_sem=red_s.at[i, t], recv_sem=red_r.at[i, t],
            device_id={"expert": me, "dp": quarter(1 - f, g)}, device_id_type=MESH,
        )

    def final_copy(i, t):
        return pltpu.make_async_remote_copy(
            src_ref=spot(TM, TD, i, t), dst_ref=spot(FM, FD, c, t),
            send_sem=fin_s.at[i, t], recv_sem=fin_r.at[c, t],
            device_id={"expert": z * CORES + g, "dp": quarter(f, 1 - g) if i == 0 else dd}, device_id_type=MESH,
        )

    for i in range(2):
        j = quarter(1 - f, (1 - g) if i == 0 else g)
        for t in range(2):
            SM[i, t * part : (t + 1) * part] = wide(j, t).astype(bf)
            reduce_copy(i, t).start()
        for n in range(n_s):
            SD[i, :, columns(n)] = deep(j, n).astype(bf)
        reduce_copy(i, 2).start()
    for i in range(2):
        j = quarter(f, (1 - g) if i == 0 else g)
        for t in range(2):
            OM[i, t * part : (t + 1) * part] = wide(j, t)
        for n in range(n_s):
            OD[i, :, columns(n)] = deep(j, n)
    for i in range(2):
        for t in range(3):
            reduce_copy(i, t).wait_recv()
            if t < 2:
                at = slice(t * part, (t + 1) * part)
                TM[i, at] = (OM[i, at] + RM[i, at].astype(f32)).astype(bf)
            else:
                TD[i] = (OD[i] + RD[i].astype(f32)).astype(bf)
            if i == 0:
                final_copy(0, t).start()
            else:
                @pl.when(g != c)
                def _():
                    final_copy(1, t).start()

                @pl.when(g == c)
                def _():
                    if t < 2:
                        FM[c, at] = TM[1, at]
                    else:
                        FD[c] = TD[1]

    def landed(slot, t):
        return pltpu.make_async_remote_copy(
            src_ref=spot(FM, FD, slot, t), dst_ref=spot(FM, FD, slot, t),
            send_sem=fin_s.at[0, t], recv_sem=fin_r.at[slot, t],
            device_id={"expert": sib, "dp": dd}, device_id_type=MESH,
        )

    for t in range(3):
        @pl.when(g != c)
        def _():
            landed(c, t).wait_recv()

        landed(1 - c, t).wait_recv()
        if t < 2:
            at = slice(t * part, (t + 1) * part)
            for o, out in enumerate((out_g, out_u)):
                out[0, at] = (
                    jnp.dot(FM[0, at], E[0, o], preferred_element_type=f32)
                    + jnp.dot(FM[1, at], E[1, o], preferred_element_type=f32)
                ).astype(bf)
        else:
            for slot in range(2):
                out_d[0, slot * hpiece : (slot + 1) * hpiece] = FD[slot]

    for i in range(2):
        for t in range(3):
            reduce_copy(i, t).wait_send()
            if i == 0:
                final_copy(0, t).wait_send()
            else:
                @pl.when(g != c)
                def _():
                    final_copy(1, t).wait_send()

    @pl.when(mine_there)
    def _():
        for i in range(3):
            share(i).wait_send()

    @pl.loop(0, n_z)
    def _(src):
        for d in range(2):
            @pl.when(can(d) & (jnp.where(d == 0, z - src, src - z) >= 0))
            def _():
                tab_hop(d, src).wait_send()
                for i in range(n_c):
                    hop(i, d, src, False).wait_send()
        for i in range(n_c):
            for to in range(3):
                row(i, src, to, 0).wait_send()


def grid_step(n_e, tokens, out_grad, expert_ids, gate_probs, w_gate, w_up, w_down):
    rows, width = tokens.shape
    hid = w_gate.shape[2]
    n_z, top = n_e // CORES, expert_ids.shape[1]
    cap = rows * (top + 1) // n_e
    lanes = -(-n_e // 8) * 8
    block, half = 4 * cap, hid // 2
    piece, hpiece = width // 4, hid // 8
    total = n_z * block
    chunks = []
    for k, cuts in ((0, XCUTS), (1, GCUTS)):
        at = 0
        for eighths in cuts:
            chunks.append((k, at * width // 8, eighths * width // 8))
            at += eighths
    n_c = len(chunks)
    bf, f32 = jnp.bfloat16, jnp.float32
    vmem = pl.BlockSpec(memory_space=pltpu.VMEM)
    hbm = pl.BlockSpec(memory_space=pltpu.HBM)
    dma = pltpu.SemaphoreType.DMA
    scratch = [
        (expert_ids.shape[::-1], expert_ids.dtype),
        (gate_probs.shape[::-1], gate_probs.dtype),
        ((n_z, 2 * lanes, rows), f32),
        ((n_z, 2 * cap, rows), bf),
        ((n_z, 2 * cap, 128), f32),
        ((width, hid), bf),
        ((width, hid), bf),
        ((hid, width), bf),
        ((2, 2, hid, hid), bf),
        ((width, hid), bf),
        ((width, hid), bf),
        ((hid, width), bf),
        ((2, block, hid), f32),
        ((2, block, hid), f32),
        ((width, total), bf),
        ((total, hid), bf),
        ((half, total), bf),
    ]
    scratch += [((2, piece, hid), bf), ((2, hpiece, width), bf)] * 2
    scratch += [((2, piece, hid), f32), ((2, hpiece, width), f32)]
    scratch += [((2, piece, hid), bf), ((2, hpiece, width), bf)] * 2
    sizes = [w for _, _, w in chunks]
    scratch += [((n_z, rows, w), bf) for w in sizes]
    scratch += [((n_z, 2, cap, w), bf) for w in sizes]
    scratch += [((n_z, 4, cap, w), bf) for w in sizes]
    held = sum(math.prod(shape) * jnp.dtype(kind).itemsize for shape, kind in scratch)
    args = (tokens, out_grad, expert_ids.T, gate_probs.T, w_gate, w_up, w_down)
    made = pl.pallas_call(
        functools.partial(grid_kernel, n_e, cap, chunks),
        out_shape=(
            jax.ShapeDtypeStruct((1, piece, hid), bf),
            jax.ShapeDtypeStruct((1, piece, hid), bf),
            jax.ShapeDtypeStruct((1, 2 * hpiece, width), bf),
        ),
        in_specs=[hbm] * 7,
        out_specs=(vmem, vmem, vmem),
        scratch_shapes=[pltpu.VMEM(shape, kind) for shape, kind in scratch]
        + [
            dma((2,)),
            dma((n_c,)),
            dma((3,)),
            dma((3,)),
            dma((3,)),
            dma((2, n_z)),
            dma((n_z,)),
            dma((n_c, 2, n_z)),
            dma((n_c, n_z)),
            dma((n_c, n_z, 3)),
            dma((n_c, n_z, 4)),
        ]
        + [dma((2, 3))] * 4,
        compiler_params=pltpu.CompilerParams(
            collective_id=1, has_side_effects=True, vmem_limit_bytes=held + (12 << 20)
        ),
    )(*(pltpu.with_memory_space_constraint(x, pltpu.HBM) for x in args))
    return write_out(made)


def solution(mesh):
    n_e, n_d = mesh.shape["expert"], mesh.shape["dp"]
    n_b = max(b for b in range(1, n_d + 1) if n_d % b == 0 and b * b <= n_d)
    n_a = n_d // n_b

    def step(tokens, out_grad, expert_ids, gate_probs, w_gate, w_up, w_down):
        rows, width = tokens.shape
        hid = w_gate.shape[2]
        total = n_e * rows
        lanes = -(-n_e // 8) * 8
        bf, f32 = jnp.bfloat16, jnp.float32
        vmem = pl.BlockSpec(memory_space=pltpu.VMEM)
        hbm = pl.BlockSpec(memory_space=pltpu.HBM)
        piece, hpiece = width // n_d, hid // n_d
        dma = pltpu.SemaphoreType.DMA
        scratch = [
            (expert_ids.shape[::-1], expert_ids.dtype),
            (gate_probs.shape[::-1], gate_probs.dtype),
            ((n_e, rows, width), bf),
            ((n_e, rows, width), bf),
            ((n_e, lanes, rows), f32),
            ((width, hid), bf),
            ((width, hid), bf),
            ((hid, width), bf),
            ((2, CORES * rows, 2 * hid), f32),
            ((width, total), bf),
            ((hid, total), bf),
            ((total, 2 * hid), bf),
            ((total, width), bf),
            ((2, width, hid), bf),
            ((2, n_d, hpiece, width // 2), bf),
            ((2, n_a, n_a, piece, hid), bf),
            ((2, n_a, n_a, hpiece, width // 2), bf),
            ((2, n_a, piece, hid), bf),
            ((2, n_a, hpiece, width // 2), bf),
            ((2, n_a, piece, hid), bf),
            ((2, n_a, hpiece, width // 2), bf),
        ]
        held = sum(math.prod(shape) * jnp.dtype(kind).itemsize for shape, kind in scratch)
        args = (tokens, out_grad, expert_ids.T, gate_probs.T, w_gate, w_up, w_down)
        made = pl.pallas_call(
            functools.partial(kernel, n_e, n_a, n_b),
            out_shape=(
                jax.ShapeDtypeStruct((1, piece, hid), bf),
                jax.ShapeDtypeStruct((1, piece, hid), bf),
                jax.ShapeDtypeStruct((1, hpiece, width), bf),
            ),
            in_specs=[hbm] * 7,
            out_specs=(vmem, vmem, vmem),
            scratch_shapes=[pltpu.VMEM(shape, kind) for shape, kind in scratch]
            + [
                dma((7,)),
                dma((3, 2, n_e)),
                dma((3, n_e)),
                dma((3, n_e)),
                dma((2, 2, n_d)),
                dma((2, 2, n_a, n_a)),
                dma((2, 2, n_a)),
                dma((2, 2, n_a)),
            ],
            compiler_params=pltpu.CompilerParams(
                collective_id=0, has_side_effects=True, vmem_limit_bytes=held + (10 << 20)
            ),
        )(*(pltpu.with_memory_space_constraint(x, pltpu.HBM) for x in args))
        return write_out(made)

    if n_a == 2 and n_b == 2:
        step = functools.partial(grid_step, n_e)
    spread = P(("expert", "dp"), None)
    return jax.shard_map(
        step,
        mesh=mesh,
        in_specs=(spread, spread, spread, spread) + (P("expert", None, None),) * 3,
        out_specs=(P("expert", "dp", None),) * 3,
        check_vma=False,
    )
```

```python
import functools
import math

import jax
import jax.numpy as jnp
from jax import lax
from jax.experimental import pallas as pl
from jax.experimental.pallas import tpu as pltpu
from jax.sharding import PartitionSpec as P

MESH = pl.DeviceIdType.MESH
CORES = 2
XCUTS, GCUTS = (8,), (4, 4)


def kernel(
    n_e, n_a, n_b,
    tok, cot, ids_in, probs_in, wg_in, wu_in, wd_in,
    out_g, out_u, out_d,
    ids, probs, X, G, PT, WG, WU, WD, GU, XT, HT, GG, S, MB, DB, MR, DR, MP, DP, MQ, DQ,
    lsem, chain_s, sib_s, blk_r, one_s, one_r, two_s, two_r,
):
    n_d = n_a * n_b
    rows, width = tok.shape
    hid = wg_in.shape[2]
    top = ids_in.shape[0]
    n_z = n_e // CORES
    me = lax.axis_index("expert")
    dd = lax.axis_index("dp")
    z, c = me // CORES, me % CORES
    sib = z * CORES + (1 - c)

    barrier = pltpu.get_barrier_semaphore()
    for step in (-1, 1):
        @pl.when(jnp.logical_and(z + step >= 0, z + step < n_z))
        def _():
            pl.semaphore_signal(barrier, inc=1, device_id={"expert": me + step * CORES}, device_id_type=MESH)
    pl.semaphore_signal(barrier, inc=1, device_id={"expert": sib}, device_id_type=MESH)
    for i in range(1, n_a):
        pl.semaphore_signal(barrier, inc=1, device_id={"dp": ((dd // n_b + i) % n_a) * n_b + dd % n_b}, device_id_type=MESH)
    for i in range(1, n_b):
        pl.semaphore_signal(barrier, inc=1, device_id={"dp": dd // n_b * n_b + (dd % n_b + i) % n_b}, device_id_type=MESH)
    small = [
        pltpu.make_async_copy(ids_in, ids, lsem.at[5]),
        pltpu.make_async_copy(probs_in, probs, lsem.at[6]),
    ]
    for copy in small:
        copy.start()
    for copy in small:
        copy.wait()
    erow = lax.broadcasted_iota(jnp.int32, PT.shape[1:], 0)
    table = jnp.zeros(PT.shape[1:], jnp.float32)
    for k in range(top):
        table = table + jnp.where(ids[k : k + 1, :] == erow, probs[k : k + 1, :], 0.0)
    PT[me] = table

    arrivals = n_a + n_b - 1 + jnp.where(z > 0, 1, 0) + jnp.where(z < n_z - 1, 1, 0)
    pl.semaphore_wait(barrier, arrivals)

    full = (PT, X, G)
    own = (PT.at[me], tok, cot)

    def hop(k, d, src, mine):
        there = me + (CORES if d == 0 else -CORES)
        return pltpu.make_async_remote_copy(
            src_ref=own[k] if mine else full[k].at[src],
            dst_ref=full[k].at[src],
            send_sem=chain_s.at[k, d, src],
            recv_sem=blk_r.at[k, src],
            device_id={"expert": there},
            device_id_type=MESH,
        )

    def across(k, src, mine):
        return pltpu.make_async_remote_copy(
            src_ref=own[k] if mine else full[k].at[src],
            dst_ref=full[k].at[src],
            send_sem=sib_s.at[k, src],
            recv_sem=blk_r.at[k, src],
            device_id={"expert": sib},
            device_id_type=MESH,
        )

    def can(d):
        return z < n_z - 1 if d == 0 else z > 0

    for k in range(3):
        for d in range(2):
            @pl.when(can(d))
            def _():
                hop(k, d, me, True).start()
        across(k, me, True).start()
    local = [
        pltpu.make_async_copy(tok, X.at[me], lsem.at[0]),
        pltpu.make_async_copy(cot, G.at[me], lsem.at[1]),
        pltpu.make_async_copy(wg_in.at[0], WG, lsem.at[2]),
        pltpu.make_async_copy(wu_in.at[0], WU, lsem.at[3]),
        pltpu.make_async_copy(wd_in.at[0], WD, lsem.at[4]),
    ]
    for copy in local:
        copy.start()
    for copy in local:
        copy.wait()

    pair = CORES * rows

    def base(zz):
        return pl.multiple_of(zz * pair, pair)

    def forward_tokens(zz, d):
        for k in range(2):
            across(k, zz * CORES + (1 - c), False).wait_recv()
        x = X[pl.ds(zz * CORES, CORES)].reshape(pair, width)
        GU[d, :, :hid] = jnp.dot(x, WG[...], preferred_element_type=jnp.float32)
        GU[d, :, hid:] = jnp.dot(x, WU[...], preferred_element_type=jnp.float32)
        XT[:, pl.ds(base(zz), pair)] = x.T

    def forward_cots(zz, d):
        across(2, zz * CORES + (1 - c), False).wait_recv()
        at = base(zz)
        parts = []
        for h in range(CORES):
            p = PT[zz * CORES + h, pl.ds(me, 1), :]
            p = jnp.broadcast_to(p, (rows, rows)).T[:, :1]
            parts.append((p * G[zz * CORES + h].astype(jnp.float32)).astype(jnp.bfloat16))
        scaled = jnp.concatenate(parts, axis=0)
        S[pl.ds(at, pair), :] = scaled
        gh = lax.dot_general(scaled, WD[...], (((1,), (1,)), ((), ())), preferred_element_type=jnp.float32)
        gate, up = GU[d, :, :hid], GU[d, :, hid:]
        sigma = jax.nn.sigmoid(gate)
        active = gate * sigma
        GG[pl.ds(at, pair), :hid] = (gh * up * sigma * (1.0 + gate * (1.0 - sigma))).astype(jnp.bfloat16)
        GG[pl.ds(at, pair), hid:] = (gh * active).astype(jnp.bfloat16)
        HT[:, pl.ds(at, pair)] = (active * up).astype(jnp.bfloat16).T

    def both(s, work):
        @pl.loop(0, 2)
        def _(d):
            zz = jnp.where(d == 0, z - s, z + s)

            @pl.when((zz >= 0) & (zz < n_z) & ((s > 0) | (d == 0)))
            def _():
                work(zz, d)

    def pass_on(s, kinds):
        for k in kinds:
            for d in range(2):
                zz = z - s if d == 0 else z + s
                src = zz * CORES + c

                @pl.when((zz >= 0) & (zz < n_z))
                def _():
                    hop(k, d, src, False).wait_recv()

                    @pl.when(can(d))
                    def _():
                        hop(k, d, src, False).start()

                    across(k, src, False).start()

    @pl.loop(0, n_z)
    def _(s):
        @pl.when(s > 0)
        def _():
            pass_on(s, (0, 1))

        both(s, forward_tokens)

        @pl.when(s > 0)
        def _():
            pass_on(s, (2,))

        both(s, forward_cots)

    piece, hpiece = width // n_d, hid // n_d
    chunk = max(piece, min(256, width))
    n_c = width // chunk
    hchunk, per = hid // n_c, chunk // piece
    half = width // 2

    def index(p, second, first):
        return second * n_b + first if p == 0 else first * n_b + second

    def first_of(p, j):
        return j % n_b if p == 0 else j // n_b

    def second_of(p, j):
        return j // n_b if p == 0 else j % n_b

    def mpiece(p, j):
        return MB.at[p, pl.ds(pl.multiple_of(j * piece, piece), piece)]

    def one(p, t, j):
        mine, there = first_of(p, dd), second_of(p, j)
        return pltpu.make_async_remote_copy(
            src_ref=mpiece(p, j) if t == 0 else DB.at[p, j],
            dst_ref=(MR if t == 0 else DR).at[p, mine, there],
            send_sem=one_s.at[p, t, j],
            recv_sem=one_r.at[p, t, mine, there],
            device_id={"dp": index(p, second_of(p, dd), first_of(p, j))},
            device_id_type=MESH,
        )

    def one_from(p, t, first, second):
        dst = (MR if t == 0 else DR).at[p, first, second]
        return pltpu.make_async_remote_copy(
            src_ref=dst, dst_ref=dst,
            send_sem=one_s.at[p, t, 0],
            recv_sem=one_r.at[p, t, first, second],
            device_id={"dp": index(p, second_of(p, dd), first)},
            device_id_type=MESH,
        )

    def two(p, t, second, slot):
        return pltpu.make_async_remote_copy(
            src_ref=(MP if t == 0 else DP).at[p, second],
            dst_ref=(MQ if t == 0 else DQ).at[p, slot],
            send_sem=two_s.at[p, t, second],
            recv_sem=two_r.at[p, t, slot],
            device_id={"dp": index(p, second, first_of(p, dd))},
            device_id_type=MESH,
        )

    @pl.loop(0, n_c)
    def _(i):
        if per == 1:
            step_a, step_b = n_a - 1 - i // n_b, n_b - 1 - i % n_b
            cc = ((dd // n_b + step_a) % n_a) * n_b + (dd % n_b + step_b) % n_b
        else:
            cc = (dd // per + 1 + i) % n_c
        at = pl.multiple_of(cc * chunk, chunk)
        hat = pl.multiple_of(cc * hchunk, hchunk)
        up_gate = jnp.dot(
            XT[pl.ds(at, chunk), :], GG[...], preferred_element_type=jnp.float32
        ).astype(jnp.bfloat16)
        for p in range(2):
            MB[p, pl.ds(at, chunk), :] = up_gate[:, p * hid : (p + 1) * hid]
        for t in range(2):
            if t == 1:
                down = jnp.dot(
                    HT[pl.ds(hat, hchunk), :], S[...], preferred_element_type=jnp.float32
                ).astype(jnp.bfloat16)
                for p in range(2):
                    for q in range(per):
                        DB[p, cc * per + q] = down[q * hpiece : (q + 1) * hpiece, p * half : (p + 1) * half]
            for p in range(2):
                for q in range(per):
                    j = cc * per + q

                    @pl.when(first_of(p, j) != first_of(p, dd))
                    def _():
                        one(p, t, j).start()

    def partial(p, t, second):
        first = first_of(p, dd)
        count = n_b if p == 0 else n_a
        j = index(p, second, first)
        total = (mpiece(p, j)[...] if t == 0 else DB[p, j]).astype(jnp.float32)
        for i in range(1, count):
            other = (first + i) % count
            one_from(p, t, other, second).wait_recv()
            total = total + (MR if t == 0 else DR)[p, other, second].astype(jnp.float32)
        return total

    for t in range(2):
        for p in range(2):
            count = n_a if p == 0 else n_b

            @pl.loop(1, count)
            def _(i):
                second = (second_of(p, dd) + i) % count
                (MP if t == 0 else DP)[p, second] = partial(p, t, second).astype(jnp.bfloat16)
                two(p, t, second, second_of(p, dd)).start()

    for t in range(2):
        for p in range(2):
            count = n_a if p == 0 else n_b
            mine = second_of(p, dd)
            total = partial(p, t, mine)
            for i in range(1, count):
                other = (mine + i) % count
                two(p, t, other, other).wait_recv()
                total = total + (MQ if t == 0 else DQ)[p, other].astype(jnp.float32)
            if t == 0:
                (out_g, out_u)[p][0] = total.astype(jnp.bfloat16)
            else:
                out_d[0, :, p * half : (p + 1) * half] = total.astype(jnp.bfloat16)

    for p in range(2):
        for t in range(2):
            @pl.loop(0, n_d)
            def _(j):
                @pl.when(first_of(p, j) != first_of(p, dd))
                def _():
                    one(p, t, j).wait_send()

            count = n_a if p == 0 else n_b

            @pl.loop(1, count)
            def _(i):
                two(p, t, (second_of(p, dd) + i) % count, second_of(p, dd)).wait_send()

    @pl.loop(0, n_z)
    def _(s):
        for k in range(3):
            for d in range(2):
                zz = z - s if d == 0 else z + s
                src = zz * CORES + c

                @pl.when((zz >= 0) & (zz < n_z) & can(d))
                def _():
                    hop(k, d, src, False).wait_send()

            across(k, s * CORES + c, False).wait_send()


def copy_out(*refs):
    n = len(refs) // 2
    copies = [pltpu.make_async_copy(refs[i], refs[n + i], refs[-1].at[i]) for i in range(n)]
    for copy in copies:
        copy.start()
    for copy in copies:
        copy.wait()


def write_out(arrays):
    anywhere = pl.BlockSpec(memory_space=pl.ANY)
    return pl.pallas_call(
        copy_out,
        out_shape=tuple(jax.ShapeDtypeStruct(x.shape, x.dtype) for x in arrays),
        in_specs=[anywhere] * len(arrays),
        out_specs=(anywhere,) * len(arrays),
        scratch_shapes=[pltpu.SemaphoreType.DMA((len(arrays),))],
        compiler_params=pltpu.CompilerParams(vmem_limit_bytes=1 << 20),
    )(*arrays)


def grid_kernel(
    n_e, cap, chunks,
    tok, cot, ids_in, probs_in, wg_in, wu_in, wd_in,
    out_g, out_u, out_d,
    ids, probs, TB, SEL, PSC, WG, WU, WD, E, WGG, WUU, WDD, SL, GH, XT, GG, HT,
    SM, SD, RM, RD, OM, OD, TM, TD, FM, FD, RL, *more,
):
    n_c = len(chunks)
    firsts = [i for i, (k, _, _) in enumerate(chunks) if k == 0]
    seconds = [i for i, (k, _, _) in enumerate(chunks) if k == 1]
    groups = [more[i * n_c : (i + 1) * n_c] for i in range(3)]
    B, C, RC = groups
    more = more[3 * n_c :]
    n_s = len(seconds)
    (
        small_l, own_l, wt_l, wt_s, wt_r, tab_s, tab_r, blk_s, blk_r, row_s, row_r,
        red_s, red_r, fin_s, fin_r, lent_r, lent_s,
    ) = more
    bf, f32 = jnp.bfloat16, jnp.float32
    rows, width = tok.shape
    hid = wg_in.shape[2]
    top = ids_in.shape[0]
    n_z = n_e // CORES
    me = lax.axis_index("expert")
    dd = lax.axis_index("dp")
    z, c = me // CORES, me % CORES
    y, x = dd // 2, dd % 2
    sib = z * CORES + (1 - c)
    g, f = jnp.where(c == 0, x, y), jnp.where(c == 0, y, x)
    across_x, across_y = y * 2 + (1 - x), (1 - y) * 2 + x

    def greet(where):
        pl.semaphore_signal(barrier, inc=1, device_id=where, device_id_type=MESH)

    barrier = pltpu.get_barrier_semaphore()
    for step in (-1, 1):
        @pl.when(jnp.logical_and(z + step >= 0, z + step < n_z))
        def _():
            greet({"expert": me + step * CORES, "dp": dd})
    greet({"expert": sib, "dp": dd})
    for other in (across_x, across_y):
        for core in range(CORES):
            greet({"expert": z * CORES + core, "dp": other})

    lends, lent = n_z >= 4, (0,)
    across = jnp.where(c == 0, across_y, across_x)
    at_end = (z == 0) | (z == n_z - 1)
    beside_end = (z == 1) | (z == n_z - 2)
    inner, outer = jnp.where(z == 0, 1, n_z - 2), jnp.where(z == 1, 0, n_z - 1)
    lenders = 0
    if lends:
        lenders = jnp.where(at_end, 1, 0)

        @pl.when(beside_end)
        def _():
            greet({"expert": outer * CORES + c, "dp": across})

    small = [
        pltpu.make_async_copy(ids_in, ids, small_l.at[0]),
        pltpu.make_async_copy(probs_in, probs, small_l.at[1]),
    ]
    for copy in small:
        copy.start()

    def own(i):
        k, at, w = chunks[i]
        return (tok, cot)[k].at[:, pl.ds(at, w)]

    def own_copy(i):
        return pltpu.make_async_copy(own(i), B[i].at[z], own_l.at[i])

    for i in range(n_c):
        own_copy(i).start()
    for copy in small:
        copy.wait()
    lanes = TB.shape[1] // 2
    erow = lax.broadcasted_iota(jnp.int32, (lanes, rows), 0)
    table = jnp.zeros((lanes, rows), f32)
    named = jnp.zeros((lanes, rows), f32)
    for k in range(top):
        hit = ids[k : k + 1, :] == erow
        table = table + jnp.where(hit, probs[k : k + 1, :], 0.0)
        named = named + jnp.where(hit, 1.0, 0.0)
    before = jnp.where(
        lax.broadcasted_iota(jnp.int32, (rows, rows), 0) < lax.broadcasted_iota(jnp.int32, (rows, rows), 1), 1.0, 0.0
    ).astype(bf)
    place = jnp.dot(named.astype(bf), before, preferred_element_type=f32)
    TB[z, :lanes] = table
    TB[z, lanes:] = jnp.where(named > 0.0, place, -1.0)

    pl.semaphore_wait(barrier, 5 + lenders + jnp.where(z > 0, 1, 0) + jnp.where(z < n_z - 1, 1, 0))

    def onward(d):
        return {"expert": me + jnp.where(d == 0, CORES, -CORES), "dp": dd}

    def can(d):
        return jnp.where(d == 0, n_z - 1 - z, z) > 0

    def plane(s, d):
        return jnp.where(d == 0, z - s, z + s)

    def tab_hop(d, src):
        return pltpu.make_async_remote_copy(
            src_ref=TB.at[src], dst_ref=TB.at[src], send_sem=tab_s.at[d, src], recv_sem=tab_r.at[src],
            device_id=onward(d), device_id_type=MESH,
        )

    def hop(i, d, src, mine):
        return pltpu.make_async_remote_copy(
            src_ref=own(i) if mine else B[i].at[src],
            dst_ref=B[i].at[src],
            send_sem=blk_s.at[i, d, src],
            recv_sem=blk_r.at[i, src],
            device_id=onward(d), device_id_type=MESH,
        )

    for d in range(2):
        @pl.when(can(d))
        def _():
            tab_hop(d, z).start()
    for i in range(n_c):
        for d in range(2):
            @pl.when(can(d))
            def _():
                hop(i, d, z, True).start()

    weights = ((wg_in, WG), (wu_in, WU), (wd_in, WD))

    def share(i):
        return pltpu.make_async_remote_copy(
            src_ref=weights[i][0].at[0], dst_ref=weights[i][1], send_sem=wt_s.at[i], recv_sem=wt_r.at[i],
            device_id={"expert": sib, "dp": dd}, device_id_type=MESH,
        )

    def keep(i):
        return pltpu.make_async_copy(weights[i][0].at[0], weights[i][1], wt_l.at[i])

    g_sib = jnp.where(c == 0, y, x)
    mine_here, mine_there = g == c, g_sib == c
    for i in range(3):
        @pl.when(mine_there)
        def _():
            share(i).start()

        @pl.when(mine_here)
        def _():
            keep(i).start()

    half, hh = hid // 2, hid // 8
    for slot in range(2):
        for t in range(2):
            j = lax.broadcasted_iota(jnp.int32, (hid, hid), 0) - t * half
            u = j + slot * hh
            for cut in range(1, 4):
                u = u + jnp.where(j >= cut * hh, hh, 0)
            inside = (j >= 0) & (j < half)
            there = lax.broadcasted_iota(jnp.int32, (hid, hid), 1)
            E[slot, t] = jnp.where(inside & (u == there), 1.0, 0.0).astype(bf)

    def row(i, src, to, part):
        where = (
            {"expert": sib, "dp": dd},
            {"expert": z * CORES, "dp": across_x},
            {"expert": z * CORES + 1, "dp": across_y},
        )[to]
        return pltpu.make_async_remote_copy(
            src_ref=C[i].at[src, (g_sib, 1 - x, 1 - y)[to]],
            dst_ref=RC[i].at[src, part],
            send_sem=row_s.at[i, src, to],
            recv_sem=row_r.at[i, src, part],
            device_id=where, device_id_type=MESH,
        )

    def each(s, work):
        @pl.loop(0, 2)
        def _(d):
            src = plane(s, d)

            @pl.when((src >= 0) & (src < n_z) & ((s > 0) | (d == 0)))
            def _():
                work(src, d)

    def tables(s):
        def work(src, d):
            @pl.when(s > 0)
            def _():
                tab_hop(d, src).wait_recv()

                @pl.when(can(d))
                def _():
                    tab_hop(d, src).start()

            slot = lax.broadcasted_iota(jnp.int32, (cap, rows), 0).astype(f32)
            for ee in range(2):
                hit = TB[src, pl.ds(lanes + z * CORES + ee, 1), :] == slot
                SEL[src, ee * cap : (ee + 1) * cap] = jnp.where(hit, 1.0, 0.0).astype(bf)
                weight = jnp.where(hit, TB[src, pl.ds(z * CORES + ee, 1), :], 0.0).sum(axis=1, keepdims=True)
                PSC[src, ee * cap : (ee + 1) * cap] = jnp.broadcast_to(weight, (cap, 128))

        each(s, work)

    def arrive(s, i):
        def work(src, d):
            @pl.when(s == 0)
            def _():
                own_copy(i).wait()

            @pl.when(s > 0)
            def _():
                hop(i, d, src, False).wait_recv()

                @pl.when(can(d))
                def _():
                    hop(i, d, src, False).start()

            picked = jnp.dot(SEL[src], B[i][src], preferred_element_type=f32)
            if chunks[i][0] == 1:
                picked = picked * PSC[src][:, :1]
            C[i][src] = picked.astype(bf).reshape(2, cap, chunks[i][2])
            row(i, src, 1, 2 + c).start()
            row(i, src, 2, 2 + c).start()
            row(i, src, 0, c).start()
            RC[i][src, c] = C[i][src, g]

        each(s, work)

    def collect(i, src):
        for part in (1 - c, 2, 3):
            row(i, src, 0, part).wait_recv()
        return RC[i][src].reshape(block, chunks[i][2])

    block = 4 * cap

    def base(src):
        return pl.multiple_of(src * block, block)

    def forward_tokens(s):
        def work(src, d):
            gate = jnp.zeros((block, hid), f32)
            up = jnp.zeros((block, hid), f32)
            for i in firsts:
                _, at, w = chunks[i]
                xs = collect(i, src)
                gate = gate + jnp.dot(xs, WGG[at : at + w], preferred_element_type=f32)
                up = up + jnp.dot(xs, WUU[at : at + w], preferred_element_type=f32)
                XT[at : at + w, pl.ds(base(src), block)] = xs.T
            sigma = jax.nn.sigmoid(gate)
            active = gate * sigma
            lane = lax.broadcasted_iota(jnp.int32, (block, hid), 1)
            SL[d] = jnp.where(lane < half, up * sigma * (1.0 + gate * (1.0 - sigma)), active)
            HT[:, pl.ds(base(src), block)] = (active * up).astype(bf).T[:half]

        each(s, work)

    def forward_cots(s, which):
        def work(src, d):
            total = jnp.zeros((block, hid), f32) if which[0] == seconds[0] else GH[d]
            for i in which:
                _, at, w = chunks[i]
                total = total + lax.dot_general(
                    collect(i, src), WDD[:, at : at + w], (((1,), (1,)), ((), ())), preferred_element_type=f32
                )
            if which[-1] == seconds[-1]:
                GG[pl.ds(base(src), block), :] = (total * SL[d]).astype(bf)
            else:
                GH[d] = total

        each(s, work)

    def prepare():
        for i in range(3):
            @pl.when(mine_here)
            def _():
                keep(i).wait()

            @pl.when(jnp.logical_not(mine_here))
            def _():
                share(i).wait_recv()
        spread = (E[c, 0].astype(f32) + E[c, 1].astype(f32)).astype(bf)
        for source, made in ((WG, WGG), (WU, WUU)):
            made[...] = lax.dot_general(
                source[...], spread, (((1,), (1,)), ((), ())), preferred_element_type=f32
            ).astype(bf)
        WDD[...] = jnp.dot(spread, WD[...], preferred_element_type=f32).astype(bf)

    @pl.loop(0, n_z - 1)
    def _(s):
        tables(s)
        for i in firsts:
            arrive(s, i)

        @pl.when(s > 0)
        def _():
            forward_cots(s - 1, seconds)

        for i in seconds[:-1]:
            arrive(s, i)

        @pl.when(s == 0)
        def _():
            prepare()

        forward_tokens(s)
        arrive(s, seconds[-1])

    last = n_z - 1
    tables(last)
    for i in firsts:
        arrive(last, i)
    forward_cots(last - 1, seconds)
    arrive(last, seconds[0])
    forward_tokens(last)
    for i in seconds[1:]:
        arrive(last, i)
    for n in range(n_s):
        forward_cots(last, seconds[n : n + 1])

    piece, hpiece = width // 4, half // 4
    part = piece // 2

    def quarter(ff, gg):
        return jnp.where(c == 0, ff * 2 + gg, gg * 2 + ff)

    def wide(j, t):
        at = pl.multiple_of(j * piece + t * part, part)
        return jnp.dot(XT[pl.ds(at, part), :], GG[...], preferred_element_type=f32)

    def deep(j, n):
        at = pl.multiple_of(j * hpiece, hpiece)
        i = seconds[n]
        return jnp.dot(
            HT[pl.ds(at, hpiece), :], RC[i][...].reshape(n_z * block, chunks[i][2]), preferred_element_type=f32
        )

    def columns(n):
        _, at, w = chunks[seconds[n]]
        return slice(at, at + w)

    def spot(M, D, i, t):
        return M.at[i, pl.ds(t * part, part)] if t < 2 else D.at[i]

    def reduce_copy(i, t):
        return pltpu.make_async_remote_copy(
            src_ref=spot(SM, SD, i, t), dst_ref=spot(RM, RD, i, t),
            send_sem=red_s.at[i, t], recv_sem=red_r.at[i, t],
            device_id={"expert": me, "dp": quarter(1 - f, g)}, device_id_type=MESH,
        )

    def final_copy(i, t):
        return pltpu.make_async_remote_copy(
            src_ref=spot(TM, TD, i, t), dst_ref=spot(FM, FD, c, t),
            send_sem=fin_s.at[i, t], recv_sem=fin_r.at[c, t],
            device_id={"expert": z * CORES + g, "dp": quarter(f, 1 - g) if i == 0 else dd}, device_id_type=MESH,
        )

    def lend(t):
        return pltpu.make_async_remote_copy(
            src_ref=spot(SM, SD, 1, t), dst_ref=RL.at[pl.ds(t * part, part)],
            send_sem=red_s.at[1, t], recv_sem=lent_r.at[t],
            device_id={"expert": inner * CORES + c, "dp": across}, device_id_type=MESH,
        )

    def give_back(t):
        return pltpu.make_async_remote_copy(
            src_ref=RL.at[pl.ds(t * part, part)], dst_ref=spot(RM, RD, 1, t),
            send_sem=lent_s.at[t], recv_sem=red_r.at[1, t],
            device_id={"expert": outer * CORES + c, "dp": dd}, device_id_type=MESH,
        )

    def send_wide(i, t):
        j = quarter(1 - f, (1 - g) if i == 0 else g)
        SM[i, t * part : (t + 1) * part] = wide(j, t).astype(bf)
        if i == 0 or t not in lent or not lends:
            reduce_copy(i, t).start()
        else:
            @pl.when(at_end)
            def _():
                lend(t).start()

            @pl.when(jnp.logical_not(at_end))
            def _():
                reduce_copy(1, t).start()

    def send_deep(i):
        j = quarter(1 - f, (1 - g) if i == 0 else g)
        for n in range(n_s):
            SD[i, :, columns(n)] = deep(j, n).astype(bf)
        reduce_copy(i, 2).start()

    def keep_own(i, t):
        j = quarter(f, (1 - g) if i == 0 else g)
        if t < 2:
            OM[i, t * part : (t + 1) * part] = wide(j, t)
        else:
            for n in range(n_s):
                OD[i, :, columns(n)] = deep(j, n)

    def pass_total(i, t):
        reduce_copy(i, t).wait_recv()
        if t < 2:
            at = slice(t * part, (t + 1) * part)
            TM[i, at] = (OM[i, at] + RM[i, at].astype(f32)).astype(bf)
        else:
            TD[i] = (OD[i] + RD[i].astype(f32)).astype(bf)
        if i == 0:
            final_copy(0, t).start()
        else:
            @pl.when(g != c)
            def _():
                final_copy(1, t).start()

            @pl.when(g == c)
            def _():
                if t < 2:
                    FM[c, at] = TM[1, at]
                else:
                    FD[c] = TD[1]

    send_wide(0, 0)
    send_wide(1, 0)
    send_wide(0, 1)
    send_deep(0)
    send_deep(1)
    keep_own(0, 0)
    keep_own(0, 1)
    pass_total(0, 0)
    send_wide(1, 1)
    keep_own(0, 2)
    pass_total(0, 1)
    pass_total(0, 2)
    keep_own(1, 0)
    keep_own(1, 1)
    keep_own(1, 2)
    pass_total(1, 2)
    pass_total(1, 0)
    pass_total(1, 1)
    def landed(slot, t):
        return pltpu.make_async_remote_copy(
            src_ref=spot(FM, FD, slot, t), dst_ref=spot(FM, FD, slot, t),
            send_sem=fin_s.at[0, t], recv_sem=fin_r.at[slot, t],
            device_id={"expert": sib, "dp": dd}, device_id_type=MESH,
        )

    for t in range(3):
        @pl.when(g != c)
        def _():
            landed(c, t).wait_recv()

        landed(1 - c, t).wait_recv()
        if t < 2:
            at = slice(t * part, (t + 1) * part)
            for o, out in enumerate((out_g, out_u)):
                out[0, at] = (
                    jnp.dot(FM[0, at], E[0, o], preferred_element_type=f32)
                    + jnp.dot(FM[1, at], E[1, o], preferred_element_type=f32)
                ).astype(bf)
        else:
            for slot in range(2):
                out_d[0, slot * hpiece : (slot + 1) * hpiece] = FD[slot]

    if lends:
        @pl.when(beside_end)
        def _():
            for t in lent:
                lend(t).wait_recv()
                give_back(t).start()
            for t in lent:
                give_back(t).wait_send()

    for i in range(2):
        for t in range(3):
            reduce_copy(i, t).wait_send()
            if i == 0:
                final_copy(0, t).wait_send()
            else:
                @pl.when(g != c)
                def _():
                    final_copy(1, t).wait_send()

    @pl.when(mine_there)
    def _():
        for i in range(3):
            share(i).wait_send()

    @pl.loop(0, n_z)
    def _(src):
        for d in range(2):
            @pl.when(can(d) & (jnp.where(d == 0, z - src, src - z) >= 0))
            def _():
                tab_hop(d, src).wait_send()
                for i in range(n_c):
                    hop(i, d, src, False).wait_send()
        for i in range(n_c):
            for to in range(3):
                row(i, src, to, 0).wait_send()


def grid_step(n_e, tokens, out_grad, expert_ids, gate_probs, w_gate, w_up, w_down):
    rows, width = tokens.shape
    hid = w_gate.shape[2]
    n_z, top = n_e // CORES, expert_ids.shape[1]
    cap = rows * (top + 1) // n_e
    lanes = -(-n_e // 8) * 8
    block, half = 4 * cap, hid // 2
    piece, hpiece = width // 4, hid // 8
    total = n_z * block
    chunks = []
    for k, cuts in ((0, XCUTS), (1, GCUTS)):
        at = 0
        for eighths in cuts:
            chunks.append((k, at * width // 8, eighths * width // 8))
            at += eighths
    n_c = len(chunks)
    bf, f32 = jnp.bfloat16, jnp.float32
    vmem = pl.BlockSpec(memory_space=pltpu.VMEM)
    hbm = pl.BlockSpec(memory_space=pltpu.HBM)
    dma = pltpu.SemaphoreType.DMA
    scratch = [
        (expert_ids.shape[::-1], expert_ids.dtype),
        (gate_probs.shape[::-1], gate_probs.dtype),
        ((n_z, 2 * lanes, rows), f32),
        ((n_z, 2 * cap, rows), bf),
        ((n_z, 2 * cap, 128), f32),
        ((width, hid), bf),
        ((width, hid), bf),
        ((hid, width), bf),
        ((2, 2, hid, hid), bf),
        ((width, hid), bf),
        ((width, hid), bf),
        ((hid, width), bf),
        ((2, block, hid), f32),
        ((2, block, hid), f32),
        ((width, total), bf),
        ((total, hid), bf),
        ((half, total), bf),
    ]
    scratch += [((2, piece, hid), bf), ((2, hpiece, width), bf)] * 2
    scratch += [((2, piece, hid), f32), ((2, hpiece, width), f32)]
    scratch += [((2, piece, hid), bf), ((2, hpiece, width), bf)] * 2
    scratch += [((piece, hid), bf)]
    sizes = [w for _, _, w in chunks]
    scratch += [((n_z, rows, w), bf) for w in sizes]
    scratch += [((n_z, 2, cap, w), bf) for w in sizes]
    scratch += [((n_z, 4, cap, w), bf) for w in sizes]
    held = sum(math.prod(shape) * jnp.dtype(kind).itemsize for shape, kind in scratch)
    args = (tokens, out_grad, expert_ids.T, gate_probs.T, w_gate, w_up, w_down)
    made = pl.pallas_call(
        functools.partial(grid_kernel, n_e, cap, chunks),
        out_shape=(
            jax.ShapeDtypeStruct((1, piece, hid), bf),
            jax.ShapeDtypeStruct((1, piece, hid), bf),
            jax.ShapeDtypeStruct((1, 2 * hpiece, width), bf),
        ),
        in_specs=[hbm] * 7,
        out_specs=(vmem, vmem, vmem),
        scratch_shapes=[pltpu.VMEM(shape, kind) for shape, kind in scratch]
        + [
            dma((2,)),
            dma((n_c,)),
            dma((3,)),
            dma((3,)),
            dma((3,)),
            dma((2, n_z)),
            dma((n_z,)),
            dma((n_c, 2, n_z)),
            dma((n_c, n_z)),
            dma((n_c, n_z, 3)),
            dma((n_c, n_z, 4)),
        ]
        + [dma((2, 3))] * 4
        + [dma((2,))] * 2,
        compiler_params=pltpu.CompilerParams(
            collective_id=1, has_side_effects=True, vmem_limit_bytes=held + (12 << 20)
        ),
    )(*(pltpu.with_memory_space_constraint(x, pltpu.HBM) for x in args))
    return write_out(made)


def solution(mesh):
    n_e, n_d = mesh.shape["expert"], mesh.shape["dp"]
    n_b = max(b for b in range(1, n_d + 1) if n_d % b == 0 and b * b <= n_d)
    n_a = n_d // n_b

    def step(tokens, out_grad, expert_ids, gate_probs, w_gate, w_up, w_down):
        rows, width = tokens.shape
        hid = w_gate.shape[2]
        total = n_e * rows
        lanes = -(-n_e // 8) * 8
        bf, f32 = jnp.bfloat16, jnp.float32
        vmem = pl.BlockSpec(memory_space=pltpu.VMEM)
        hbm = pl.BlockSpec(memory_space=pltpu.HBM)
        piece, hpiece = width // n_d, hid // n_d
        dma = pltpu.SemaphoreType.DMA
        scratch = [
            (expert_ids.shape[::-1], expert_ids.dtype),
            (gate_probs.shape[::-1], gate_probs.dtype),
            ((n_e, rows, width), bf),
            ((n_e, rows, width), bf),
            ((n_e, lanes, rows), f32),
            ((width, hid), bf),
            ((width, hid), bf),
            ((hid, width), bf),
            ((2, CORES * rows, 2 * hid), f32),
            ((width, total), bf),
            ((hid, total), bf),
            ((total, 2 * hid), bf),
            ((total, width), bf),
            ((2, width, hid), bf),
            ((2, n_d, hpiece, width // 2), bf),
            ((2, n_a, n_a, piece, hid), bf),
            ((2, n_a, n_a, hpiece, width // 2), bf),
            ((2, n_a, piece, hid), bf),
            ((2, n_a, hpiece, width // 2), bf),
            ((2, n_a, piece, hid), bf),
            ((2, n_a, hpiece, width // 2), bf),
        ]
        held = sum(math.prod(shape) * jnp.dtype(kind).itemsize for shape, kind in scratch)
        args = (tokens, out_grad, expert_ids.T, gate_probs.T, w_gate, w_up, w_down)
        made = pl.pallas_call(
            functools.partial(kernel, n_e, n_a, n_b),
            out_shape=(
                jax.ShapeDtypeStruct((1, piece, hid), bf),
                jax.ShapeDtypeStruct((1, piece, hid), bf),
                jax.ShapeDtypeStruct((1, hpiece, width), bf),
            ),
            in_specs=[hbm] * 7,
            out_specs=(vmem, vmem, vmem),
            scratch_shapes=[pltpu.VMEM(shape, kind) for shape, kind in scratch]
            + [
                dma((7,)),
                dma((3, 2, n_e)),
                dma((3, n_e)),
                dma((3, n_e)),
                dma((2, 2, n_d)),
                dma((2, 2, n_a, n_a)),
                dma((2, 2, n_a)),
                dma((2, 2, n_a)),
            ],
            compiler_params=pltpu.CompilerParams(
                collective_id=0, has_side_effects=True, vmem_limit_bytes=held + (10 << 20)
            ),
        )(*(pltpu.with_memory_space_constraint(x, pltpu.HBM) for x in args))
        return write_out(made)

    if n_a == 2 and n_b == 2:
        step = functools.partial(grid_step, n_e)
    spread = P(("expert", "dp"), None)
    return jax.shard_map(
        step,
        mesh=mesh,
        in_specs=(spread, spread, spread, spread) + (P("expert", None, None),) * 3,
        out_specs=(P("expert", "dp", None),) * 3,
        check_vma=False,
    )
```

```python
import functools
import math

import jax
import jax.numpy as jnp
from jax import lax
from jax.experimental import pallas as pl
from jax.experimental.pallas import tpu as pltpu
from jax.sharding import PartitionSpec as P

MESH = pl.DeviceIdType.MESH
CORES = 2
XCUTS, GCUTS = (8,), (4, 4)


def kernel(
    n_e, n_a, n_b,
    tok, cot, ids_in, probs_in, wg_in, wu_in, wd_in,
    out_g, out_u, out_d,
    ids, probs, X, G, PT, WG, WU, WD, GU, XT, HT, GG, S, MB, DB, MR, DR, MP, DP, MQ, DQ,
    lsem, chain_s, sib_s, blk_r, one_s, one_r, two_s, two_r,
):
    n_d = n_a * n_b
    rows, width = tok.shape
    hid = wg_in.shape[2]
    top = ids_in.shape[0]
    n_z = n_e // CORES
    me = lax.axis_index("expert")
    dd = lax.axis_index("dp")
    z, c = me // CORES, me % CORES
    sib = z * CORES + (1 - c)

    barrier = pltpu.get_barrier_semaphore()
    for step in (-1, 1):
        @pl.when(jnp.logical_and(z + step >= 0, z + step < n_z))
        def _():
            pl.semaphore_signal(barrier, inc=1, device_id={"expert": me + step * CORES}, device_id_type=MESH)
    pl.semaphore_signal(barrier, inc=1, device_id={"expert": sib}, device_id_type=MESH)
    for i in range(1, n_a):
        pl.semaphore_signal(barrier, inc=1, device_id={"dp": ((dd // n_b + i) % n_a) * n_b + dd % n_b}, device_id_type=MESH)
    for i in range(1, n_b):
        pl.semaphore_signal(barrier, inc=1, device_id={"dp": dd // n_b * n_b + (dd % n_b + i) % n_b}, device_id_type=MESH)
    small = [
        pltpu.make_async_copy(ids_in, ids, lsem.at[5]),
        pltpu.make_async_copy(probs_in, probs, lsem.at[6]),
    ]
    for copy in small:
        copy.start()
    for copy in small:
        copy.wait()
    erow = lax.broadcasted_iota(jnp.int32, PT.shape[1:], 0)
    table = jnp.zeros(PT.shape[1:], jnp.float32)
    for k in range(top):
        table = table + jnp.where(ids[k : k + 1, :] == erow, probs[k : k + 1, :], 0.0)
    PT[me] = table

    arrivals = n_a + n_b - 1 + jnp.where(z > 0, 1, 0) + jnp.where(z < n_z - 1, 1, 0)
    pl.semaphore_wait(barrier, arrivals)

    full = (PT, X, G)
    own = (PT.at[me], tok, cot)

    def hop(k, d, src, mine):
        there = me + (CORES if d == 0 else -CORES)
        return pltpu.make_async_remote_copy(
            src_ref=own[k] if mine else full[k].at[src],
            dst_ref=full[k].at[src],
            send_sem=chain_s.at[k, d, src],
            recv_sem=blk_r.at[k, src],
            device_id={"expert": there},
            device_id_type=MESH,
        )

    def across(k, src, mine):
        return pltpu.make_async_remote_copy(
            src_ref=own[k] if mine else full[k].at[src],
            dst_ref=full[k].at[src],
            send_sem=sib_s.at[k, src],
            recv_sem=blk_r.at[k, src],
            device_id={"expert": sib},
            device_id_type=MESH,
        )

    def can(d):
        return z < n_z - 1 if d == 0 else z > 0

    for k in range(3):
        for d in range(2):
            @pl.when(can(d))
            def _():
                hop(k, d, me, True).start()
        across(k, me, True).start()
    local = [
        pltpu.make_async_copy(tok, X.at[me], lsem.at[0]),
        pltpu.make_async_copy(cot, G.at[me], lsem.at[1]),
        pltpu.make_async_copy(wg_in.at[0], WG, lsem.at[2]),
        pltpu.make_async_copy(wu_in.at[0], WU, lsem.at[3]),
        pltpu.make_async_copy(wd_in.at[0], WD, lsem.at[4]),
    ]
    for copy in local:
        copy.start()
    for copy in local:
        copy.wait()

    pair = CORES * rows

    def base(zz):
        return pl.multiple_of(zz * pair, pair)

    def forward_tokens(zz, d):
        for k in range(2):
            across(k, zz * CORES + (1 - c), False).wait_recv()
        x = X[pl.ds(zz * CORES, CORES)].reshape(pair, width)
        GU[d, :, :hid] = jnp.dot(x, WG[...], preferred_element_type=jnp.float32)
        GU[d, :, hid:] = jnp.dot(x, WU[...], preferred_element_type=jnp.float32)
        XT[:, pl.ds(base(zz), pair)] = x.T

    def forward_cots(zz, d):
        across(2, zz * CORES + (1 - c), False).wait_recv()
        at = base(zz)
        parts = []
        for h in range(CORES):
            p = PT[zz * CORES + h, pl.ds(me, 1), :]
            p = jnp.broadcast_to(p, (rows, rows)).T[:, :1]
            parts.append((p * G[zz * CORES + h].astype(jnp.float32)).astype(jnp.bfloat16))
        scaled = jnp.concatenate(parts, axis=0)
        S[pl.ds(at, pair), :] = scaled
        gh = lax.dot_general(scaled, WD[...], (((1,), (1,)), ((), ())), preferred_element_type=jnp.float32)
        gate, up = GU[d, :, :hid], GU[d, :, hid:]
        sigma = jax.nn.sigmoid(gate)
        active = gate * sigma
        GG[pl.ds(at, pair), :hid] = (gh * up * sigma * (1.0 + gate * (1.0 - sigma))).astype(jnp.bfloat16)
        GG[pl.ds(at, pair), hid:] = (gh * active).astype(jnp.bfloat16)
        HT[:, pl.ds(at, pair)] = (active * up).astype(jnp.bfloat16).T

    def both(s, work):
        @pl.loop(0, 2)
        def _(d):
            zz = jnp.where(d == 0, z - s, z + s)

            @pl.when((zz >= 0) & (zz < n_z) & ((s > 0) | (d == 0)))
            def _():
                work(zz, d)

    def pass_on(s, kinds):
        for k in kinds:
            for d in range(2):
                zz = z - s if d == 0 else z + s
                src = zz * CORES + c

                @pl.when((zz >= 0) & (zz < n_z))
                def _():
                    hop(k, d, src, False).wait_recv()

                    @pl.when(can(d))
                    def _():
                        hop(k, d, src, False).start()

                    across(k, src, False).start()

    @pl.loop(0, n_z)
    def _(s):
        @pl.when(s > 0)
        def _():
            pass_on(s, (0, 1))

        both(s, forward_tokens)

        @pl.when(s > 0)
        def _():
            pass_on(s, (2,))

        both(s, forward_cots)

    piece, hpiece = width // n_d, hid // n_d
    chunk = max(piece, min(256, width))
    n_c = width // chunk
    hchunk, per = hid // n_c, chunk // piece
    half = width // 2

    def index(p, second, first):
        return second * n_b + first if p == 0 else first * n_b + second

    def first_of(p, j):
        return j % n_b if p == 0 else j // n_b

    def second_of(p, j):
        return j // n_b if p == 0 else j % n_b

    def mpiece(p, j):
        return MB.at[p, pl.ds(pl.multiple_of(j * piece, piece), piece)]

    def one(p, t, j):
        mine, there = first_of(p, dd), second_of(p, j)
        return pltpu.make_async_remote_copy(
            src_ref=mpiece(p, j) if t == 0 else DB.at[p, j],
            dst_ref=(MR if t == 0 else DR).at[p, mine, there],
            send_sem=one_s.at[p, t, j],
            recv_sem=one_r.at[p, t, mine, there],
            device_id={"dp": index(p, second_of(p, dd), first_of(p, j))},
            device_id_type=MESH,
        )

    def one_from(p, t, first, second):
        dst = (MR if t == 0 else DR).at[p, first, second]
        return pltpu.make_async_remote_copy(
            src_ref=dst, dst_ref=dst,
            send_sem=one_s.at[p, t, 0],
            recv_sem=one_r.at[p, t, first, second],
            device_id={"dp": index(p, second_of(p, dd), first)},
            device_id_type=MESH,
        )

    def two(p, t, second, slot):
        return pltpu.make_async_remote_copy(
            src_ref=(MP if t == 0 else DP).at[p, second],
            dst_ref=(MQ if t == 0 else DQ).at[p, slot],
            send_sem=two_s.at[p, t, second],
            recv_sem=two_r.at[p, t, slot],
            device_id={"dp": index(p, second, first_of(p, dd))},
            device_id_type=MESH,
        )

    @pl.loop(0, n_c)
    def _(i):
        if per == 1:
            step_a, step_b = n_a - 1 - i // n_b, n_b - 1 - i % n_b
            cc = ((dd // n_b + step_a) % n_a) * n_b + (dd % n_b + step_b) % n_b
        else:
            cc = (dd // per + 1 + i) % n_c
        at = pl.multiple_of(cc * chunk, chunk)
        hat = pl.multiple_of(cc * hchunk, hchunk)
        up_gate = jnp.dot(
            XT[pl.ds(at, chunk), :], GG[...], preferred_element_type=jnp.float32
        ).astype(jnp.bfloat16)
        for p in range(2):
            MB[p, pl.ds(at, chunk), :] = up_gate[:, p * hid : (p + 1) * hid]
        for t in range(2):
            if t == 1:
                down = jnp.dot(
                    HT[pl.ds(hat, hchunk), :], S[...], preferred_element_type=jnp.float32
                ).astype(jnp.bfloat16)
                for p in range(2):
                    for q in range(per):
                        DB[p, cc * per + q] = down[q * hpiece : (q + 1) * hpiece, p * half : (p + 1) * half]
            for p in range(2):
                for q in range(per):
                    j = cc * per + q

                    @pl.when(first_of(p, j) != first_of(p, dd))
                    def _():
                        one(p, t, j).start()

    def partial(p, t, second):
        first = first_of(p, dd)
        count = n_b if p == 0 else n_a
        j = index(p, second, first)
        total = (mpiece(p, j)[...] if t == 0 else DB[p, j]).astype(jnp.float32)
        for i in range(1, count):
            other = (first + i) % count
            one_from(p, t, other, second).wait_recv()
            total = total + (MR if t == 0 else DR)[p, other, second].astype(jnp.float32)
        return total

    for t in range(2):
        for p in range(2):
            count = n_a if p == 0 else n_b

            @pl.loop(1, count)
            def _(i):
                second = (second_of(p, dd) + i) % count
                (MP if t == 0 else DP)[p, second] = partial(p, t, second).astype(jnp.bfloat16)
                two(p, t, second, second_of(p, dd)).start()

    for t in range(2):
        for p in range(2):
            count = n_a if p == 0 else n_b
            mine = second_of(p, dd)
            total = partial(p, t, mine)
            for i in range(1, count):
                other = (mine + i) % count
                two(p, t, other, other).wait_recv()
                total = total + (MQ if t == 0 else DQ)[p, other].astype(jnp.float32)
            if t == 0:
                (out_g, out_u)[p][0] = total.astype(jnp.bfloat16)
            else:
                out_d[0, :, p * half : (p + 1) * half] = total.astype(jnp.bfloat16)

    for p in range(2):
        for t in range(2):
            @pl.loop(0, n_d)
            def _(j):
                @pl.when(first_of(p, j) != first_of(p, dd))
                def _():
                    one(p, t, j).wait_send()

            count = n_a if p == 0 else n_b

            @pl.loop(1, count)
            def _(i):
                two(p, t, (second_of(p, dd) + i) % count, second_of(p, dd)).wait_send()

    @pl.loop(0, n_z)
    def _(s):
        for k in range(3):
            for d in range(2):
                zz = z - s if d == 0 else z + s
                src = zz * CORES + c

                @pl.when((zz >= 0) & (zz < n_z) & can(d))
                def _():
                    hop(k, d, src, False).wait_send()

            across(k, s * CORES + c, False).wait_send()


def copy_out(*refs):
    n = len(refs) // 2
    copies = [pltpu.make_async_copy(refs[i], refs[n + i], refs[-1].at[i]) for i in range(n)]
    for copy in copies:
        copy.start()
    for copy in copies:
        copy.wait()


def write_out(arrays):
    anywhere = pl.BlockSpec(memory_space=pl.ANY)
    return pl.pallas_call(
        copy_out,
        out_shape=tuple(jax.ShapeDtypeStruct(x.shape, x.dtype) for x in arrays),
        in_specs=[anywhere] * len(arrays),
        out_specs=(anywhere,) * len(arrays),
        scratch_shapes=[pltpu.SemaphoreType.DMA((len(arrays),))],
        compiler_params=pltpu.CompilerParams(vmem_limit_bytes=1 << 20),
    )(*arrays)


def grid_kernel(
    n_e, cap, chunks,
    tok, cot, ids_in, probs_in, wg_in, wu_in, wd_in,
    out_g, out_u, out_d,
    ids, probs, TB, SEL, PSC, WG, WU, WD, E, WGG, WUU, WDD, SL, GH, XT, GG, HT,
    SM, SD, RM, RD, OM, OD, TM, TD, FM, FD, RL, *more,
):
    n_c = len(chunks)
    firsts = [i for i, (k, _, _) in enumerate(chunks) if k == 0]
    seconds = [i for i, (k, _, _) in enumerate(chunks) if k == 1]
    groups = [more[i * n_c : (i + 1) * n_c] for i in range(3)]
    B, C, RC = groups
    more = more[3 * n_c :]
    n_s = len(seconds)
    (
        small_l, own_l, wt_l, wt_s, wt_r, tab_s, tab_r, blk_s, blk_r, row_s, row_r,
        red_s, red_r, fin_s, fin_r, lent_r, lent_s,
    ) = more
    bf, f32 = jnp.bfloat16, jnp.float32
    rows, width = tok.shape
    hid = wg_in.shape[2]
    top = ids_in.shape[0]
    n_z = n_e // CORES
    me = lax.axis_index("expert")
    dd = lax.axis_index("dp")
    z, c = me // CORES, me % CORES
    y, x = dd // 2, dd % 2
    sib = z * CORES + (1 - c)
    g, f = jnp.where(c == 0, x, y), jnp.where(c == 0, y, x)
    across_x, across_y = y * 2 + (1 - x), (1 - y) * 2 + x

    def greet(where):
        pl.semaphore_signal(barrier, inc=1, device_id=where, device_id_type=MESH)

    barrier = pltpu.get_barrier_semaphore()
    for step in (-1, 1):
        @pl.when(jnp.logical_and(z + step >= 0, z + step < n_z))
        def _():
            greet({"expert": me + step * CORES, "dp": dd})
    greet({"expert": sib, "dp": dd})
    for other in (across_x, across_y):
        for core in range(CORES):
            greet({"expert": z * CORES + core, "dp": other})

    lends, lent = n_z >= 4, [0, 1, 2]
    across = jnp.where(c == 0, across_y, across_x)
    at_end = (z == 0) | (z == n_z - 1)
    beside_end = (z == 1) | (z == n_z - 2)
    inner, outer = jnp.where(z == 0, 1, n_z - 2), jnp.where(z == 1, 0, n_z - 1)
    lenders = 0
    if lends:
        lenders = jnp.where(at_end, 1, 0)

        @pl.when(beside_end)
        def _():
            greet({"expert": outer * CORES + c, "dp": across})

    small = [
        pltpu.make_async_copy(ids_in, ids, small_l.at[0]),
        pltpu.make_async_copy(probs_in, probs, small_l.at[1]),
    ]
    for copy in small:
        copy.start()

    def own(i):
        k, at, w = chunks[i]
        return (tok, cot)[k].at[:, pl.ds(at, w)]

    def own_copy(i):
        return pltpu.make_async_copy(own(i), B[i].at[z], own_l.at[i])

    for i in range(n_c):
        own_copy(i).start()
    for copy in small:
        copy.wait()
    lanes = TB.shape[1] // 2
    erow = lax.broadcasted_iota(jnp.int32, (lanes, rows), 0)
    table = jnp.zeros((lanes, rows), f32)
    named = jnp.zeros((lanes, rows), f32)
    for k in range(top):
        hit = ids[k : k + 1, :] == erow
        table = table + jnp.where(hit, probs[k : k + 1, :], 0.0)
        named = named + jnp.where(hit, 1.0, 0.0)
    before = jnp.where(
        lax.broadcasted_iota(jnp.int32, (rows, rows), 0) < lax.broadcasted_iota(jnp.int32, (rows, rows), 1), 1.0, 0.0
    ).astype(bf)
    place = jnp.dot(named.astype(bf), before, preferred_element_type=f32)
    TB[z, :lanes] = table
    TB[z, lanes:] = jnp.where(named > 0.0, place, -1.0)

    pl.semaphore_wait(barrier, 5 + lenders + jnp.where(z > 0, 1, 0) + jnp.where(z < n_z - 1, 1, 0))

    def onward(d):
        return {"expert": me + jnp.where(d == 0, CORES, -CORES), "dp": dd}

    def can(d):
        return jnp.where(d == 0, n_z - 1 - z, z) > 0

    def plane(s, d):
        return jnp.where(d == 0, z - s, z + s)

    def tab_hop(d, src):
        return pltpu.make_async_remote_copy(
            src_ref=TB.at[src], dst_ref=TB.at[src], send_sem=tab_s.at[d, src], recv_sem=tab_r.at[src],
            device_id=onward(d), device_id_type=MESH,
        )

    def hop(i, d, src, mine):
        return pltpu.make_async_remote_copy(
            src_ref=own(i) if mine else B[i].at[src],
            dst_ref=B[i].at[src],
            send_sem=blk_s.at[i, d, src],
            recv_sem=blk_r.at[i, src],
            device_id=onward(d), device_id_type=MESH,
        )

    for d in range(2):
        @pl.when(can(d))
        def _():
            tab_hop(d, z).start()
    for i in range(n_c):
        for d in range(2):
            @pl.when(can(d))
            def _():
                hop(i, d, z, True).start()

    weights = ((wg_in, WG), (wu_in, WU), (wd_in, WD))

    def share(i):
        return pltpu.make_async_remote_copy(
            src_ref=weights[i][0].at[0], dst_ref=weights[i][1], send_sem=wt_s.at[i], recv_sem=wt_r.at[i],
            device_id={"expert": sib, "dp": dd}, device_id_type=MESH,
        )

    def keep(i):
        return pltpu.make_async_copy(weights[i][0].at[0], weights[i][1], wt_l.at[i])

    g_sib = jnp.where(c == 0, y, x)
    mine_here, mine_there = g == c, g_sib == c
    for i in range(3):
        @pl.when(mine_there)
        def _():
            share(i).start()

        @pl.when(mine_here)
        def _():
            keep(i).start()

    half, hh = hid // 2, hid // 8
    for slot in range(2):
        for t in range(2):
            j = lax.broadcasted_iota(jnp.int32, (hid, hid), 0) - t * half
            u = j + slot * hh
            for cut in range(1, 4):
                u = u + jnp.where(j >= cut * hh, hh, 0)
            inside = (j >= 0) & (j < half)
            there = lax.broadcasted_iota(jnp.int32, (hid, hid), 1)
            E[slot, t] = jnp.where(inside & (u == there), 1.0, 0.0).astype(bf)

    def row(i, src, to, part):
        where = (
            {"expert": sib, "dp": dd},
            {"expert": z * CORES, "dp": across_x},
            {"expert": z * CORES + 1, "dp": across_y},
        )[to]
        return pltpu.make_async_remote_copy(
            src_ref=C[i].at[src, (g_sib, 1 - x, 1 - y)[to]],
            dst_ref=RC[i].at[src, part],
            send_sem=row_s.at[i, src, to],
            recv_sem=row_r.at[i, src, part],
            device_id=where, device_id_type=MESH,
        )

    def each(s, work):
        @pl.loop(0, 2)
        def _(d):
            src = plane(s, d)

            @pl.when((src >= 0) & (src < n_z) & ((s > 0) | (d == 0)))
            def _():
                work(src, d)

    def tables(s):
        def work(src, d):
            @pl.when(s > 0)
            def _():
                tab_hop(d, src).wait_recv()

                @pl.when(can(d))
                def _():
                    tab_hop(d, src).start()

            slot = lax.broadcasted_iota(jnp.int32, (cap, rows), 0).astype(f32)
            for ee in range(2):
                hit = TB[src, pl.ds(lanes + z * CORES + ee, 1), :] == slot
                SEL[src, ee * cap : (ee + 1) * cap] = jnp.where(hit, 1.0, 0.0).astype(bf)
                weight = jnp.where(hit, TB[src, pl.ds(z * CORES + ee, 1), :], 0.0).sum(axis=1, keepdims=True)
                PSC[src, ee * cap : (ee + 1) * cap] = jnp.broadcast_to(weight, (cap, 128))

        each(s, work)

    def arrive(s, i):
        def work(src, d):
            @pl.when(s == 0)
            def _():
                own_copy(i).wait()

            @pl.when(s > 0)
            def _():
                hop(i, d, src, False).wait_recv()

                @pl.when(can(d))
                def _():
                    hop(i, d, src, False).start()

            picked = jnp.dot(SEL[src], B[i][src], preferred_element_type=f32)
            if chunks[i][0] == 1:
                picked = picked * PSC[src][:, :1]
            C[i][src] = picked.astype(bf).reshape(2, cap, chunks[i][2])
            row(i, src, 1, 2 + c).start()
            row(i, src, 2, 2 + c).start()
            row(i, src, 0, c).start()
            RC[i][src, c] = C[i][src, g]

        each(s, work)

    def collect(i, src):
        for part in (1 - c, 2, 3):
            row(i, src, 0, part).wait_recv()
        return RC[i][src].reshape(block, chunks[i][2])

    block = 4 * cap

    def base(src):
        return pl.multiple_of(src * block, block)

    def forward_tokens(s):
        def work(src, d):
            gate = jnp.zeros((block, hid), f32)
            up = jnp.zeros((block, hid), f32)
            for i in firsts:
                _, at, w = chunks[i]
                xs = collect(i, src)
                gate = gate + jnp.dot(xs, WGG[at : at + w], preferred_element_type=f32)
                up = up + jnp.dot(xs, WUU[at : at + w], preferred_element_type=f32)
                XT[at : at + w, pl.ds(base(src), block)] = xs.T
            sigma = jax.nn.sigmoid(gate)
            active = gate * sigma
            lane = lax.broadcasted_iota(jnp.int32, (block, hid), 1)
            SL[d] = jnp.where(lane < half, up * sigma * (1.0 + gate * (1.0 - sigma)), active)
            HT[:, pl.ds(base(src), block)] = (active * up).astype(bf).T[:half]

        each(s, work)

    def forward_cots(s, which):
        def work(src, d):
            total = jnp.zeros((block, hid), f32) if which[0] == seconds[0] else GH[d]
            for i in which:
                _, at, w = chunks[i]
                total = total + lax.dot_general(
                    collect(i, src), WDD[:, at : at + w], (((1,), (1,)), ((), ())), preferred_element_type=f32
                )
            if which[-1] == seconds[-1]:
                GG[pl.ds(base(src), block), :] = (total * SL[d]).astype(bf)
            else:
                GH[d] = total

        each(s, work)

    def prepare():
        for i in range(3):
            @pl.when(mine_here)
            def _():
                keep(i).wait()

            @pl.when(jnp.logical_not(mine_here))
            def _():
                share(i).wait_recv()
        spread = (E[c, 0].astype(f32) + E[c, 1].astype(f32)).astype(bf)
        for source, made in ((WG, WGG), (WU, WUU)):
            made[...] = lax.dot_general(
                source[...], spread, (((1,), (1,)), ((), ())), preferred_element_type=f32
            ).astype(bf)
        WDD[...] = jnp.dot(spread, WD[...], preferred_element_type=f32).astype(bf)

    @pl.loop(0, n_z - 1)
    def _(s):
        tables(s)
        for i in firsts:
            arrive(s, i)

        @pl.when(s > 0)
        def _():
            forward_cots(s - 1, seconds)

        for i in seconds[:-1]:
            arrive(s, i)

        @pl.when(s == 0)
        def _():
            prepare()

        forward_tokens(s)
        arrive(s, seconds[-1])

    last = n_z - 1
    tables(last)
    for i in firsts:
        arrive(last, i)
    forward_cots(last - 1, seconds)
    arrive(last, seconds[0])
    forward_tokens(last)
    for i in seconds[1:]:
        arrive(last, i)
    for n in range(n_s):
        forward_cots(last, seconds[n : n + 1])

    piece, hpiece = width // 4, half // 4
    part = piece // 4
    n_t = piece // part

    def quarter(ff, gg):
        return jnp.where(c == 0, ff * 2 + gg, gg * 2 + ff)

    def wide(j, t):
        at = pl.multiple_of(j * piece + t * part, part)
        return jnp.dot(XT[pl.ds(at, part), :], GG[...], preferred_element_type=f32)

    def deep(j, n):
        at = pl.multiple_of(j * hpiece, hpiece)
        i = seconds[n]
        return jnp.dot(
            HT[pl.ds(at, hpiece), :], RC[i][...].reshape(n_z * block, chunks[i][2]), preferred_element_type=f32
        )

    def columns(n):
        _, at, w = chunks[seconds[n]]
        return slice(at, at + w)

    def spot(M, D, i, t):
        return M.at[i, pl.ds(t * part, part)] if t < n_t else D.at[i]

    def reduce_copy(i, t):
        return pltpu.make_async_remote_copy(
            src_ref=spot(SM, SD, i, t), dst_ref=spot(RM, RD, i, t),
            send_sem=red_s.at[i, t], recv_sem=red_r.at[i, t],
            device_id={"expert": me, "dp": quarter(1 - f, g)}, device_id_type=MESH,
        )

    def final_copy(i, t):
        return pltpu.make_async_remote_copy(
            src_ref=spot(TM, TD, i, t), dst_ref=spot(FM, FD, c, t),
            send_sem=fin_s.at[i, t], recv_sem=fin_r.at[c, t],
            device_id={"expert": z * CORES + g, "dp": quarter(f, 1 - g) if i == 0 else dd}, device_id_type=MESH,
        )

    def lend(t):
        return pltpu.make_async_remote_copy(
            src_ref=spot(SM, SD, 1, t), dst_ref=RL.at[pl.ds(t * part, part)],
            send_sem=red_s.at[1, t], recv_sem=lent_r.at[t],
            device_id={"expert": inner * CORES + c, "dp": across}, device_id_type=MESH,
        )

    def give_back(t):
        return pltpu.make_async_remote_copy(
            src_ref=RL.at[pl.ds(t * part, part)], dst_ref=spot(RM, RD, 1, t),
            send_sem=lent_s.at[t], recv_sem=red_r.at[1, t],
            device_id={"expert": outer * CORES + c, "dp": dd}, device_id_type=MESH,
        )

    def send_wide(i, t):
        j = quarter(1 - f, (1 - g) if i == 0 else g)
        SM[i, t * part : (t + 1) * part] = wide(j, t).astype(bf)
        if i == 0 or t not in lent or not lends:
            reduce_copy(i, t).start()
        else:
            @pl.when(at_end)
            def _():
                lend(t).start()

            @pl.when(jnp.logical_not(at_end))
            def _():
                reduce_copy(1, t).start()

    def send_deep(i):
        j = quarter(1 - f, (1 - g) if i == 0 else g)
        for n in range(n_s):
            SD[i, :, columns(n)] = deep(j, n).astype(bf)
        reduce_copy(i, n_t).start()

    def keep_own(i, t):
        j = quarter(f, (1 - g) if i == 0 else g)
        if t < n_t:
            OM[i, t * part : (t + 1) * part] = wide(j, t)
        else:
            for n in range(n_s):
                OD[i, :, columns(n)] = deep(j, n)

    def pass_total(i, t):
        reduce_copy(i, t).wait_recv()
        if t < n_t:
            at = slice(t * part, (t + 1) * part)
            TM[i, at] = (OM[i, at] + RM[i, at].astype(f32)).astype(bf)
        else:
            TD[i] = (OD[i] + RD[i].astype(f32)).astype(bf)
        if i == 0:
            final_copy(0, t).start()
        else:
            @pl.when(g != c)
            def _():
                final_copy(1, t).start()

            @pl.when(g == c)
            def _():
                if t < n_t:
                    FM[c, at] = TM[1, at]
                else:
                    FD[c] = TD[1]

    send_wide(0, 0)
    send_wide(0, 1)
    send_wide(1, 0)
    send_wide(0, 2)
    send_wide(1, 1)
    send_wide(0, 3)
    send_wide(1, 2)
    send_deep(0)
    send_wide(1, 3)
    keep_own(0, 0)
    keep_own(0, 1)
    pass_total(0, 0)
    send_deep(1)
    keep_own(0, 2)
    pass_total(0, 1)
    keep_own(0, 3)
    pass_total(0, 2)
    pass_total(0, 3)
    keep_own(0, 4)
    pass_total(0, 4)
    keep_own(1, 0)
    keep_own(1, 1)
    keep_own(1, 2)
    keep_own(1, 3)
    keep_own(1, 4)
    pass_total(1, 0)
    pass_total(1, 1)
    pass_total(1, 2)
    pass_total(1, 3)
    pass_total(1, 4)
    def landed(slot, t):
        return pltpu.make_async_remote_copy(
            src_ref=spot(FM, FD, slot, t), dst_ref=spot(FM, FD, slot, t),
            send_sem=fin_s.at[0, t], recv_sem=fin_r.at[slot, t],
            device_id={"expert": sib, "dp": dd}, device_id_type=MESH,
        )

    for t in range(n_t + 1):
        @pl.when(g != c)
        def _():
            landed(c, t).wait_recv()

        landed(1 - c, t).wait_recv()
        if t < n_t:
            at = slice(t * part, (t + 1) * part)
            for o, out in enumerate((out_g, out_u)):
                out[0, at] = (
                    jnp.dot(FM[0, at], E[0, o], preferred_element_type=f32)
                    + jnp.dot(FM[1, at], E[1, o], preferred_element_type=f32)
                ).astype(bf)
        else:
            for slot in range(2):
                out_d[0, slot * hpiece : (slot + 1) * hpiece] = FD[slot]

    if lends:
        @pl.when(beside_end)
        def _():
            for t in lent:
                lend(t).wait_recv()
                give_back(t).start()
            for t in lent:
                give_back(t).wait_send()

    for i in range(2):
        for t in range(n_t + 1):
            reduce_copy(i, t).wait_send()
            if i == 0:
                final_copy(0, t).wait_send()
            else:
                @pl.when(g != c)
                def _():
                    final_copy(1, t).wait_send()

    @pl.when(mine_there)
    def _():
        for i in range(3):
            share(i).wait_send()

    @pl.loop(0, n_z)
    def _(src):
        for d in range(2):
            @pl.when(can(d) & (jnp.where(d == 0, z - src, src - z) >= 0))
            def _():
                tab_hop(d, src).wait_send()
                for i in range(n_c):
                    hop(i, d, src, False).wait_send()
        for i in range(n_c):
            for to in range(3):
                row(i, src, to, 0).wait_send()


def grid_step(n_e, tokens, out_grad, expert_ids, gate_probs, w_gate, w_up, w_down):
    rows, width = tokens.shape
    hid = w_gate.shape[2]
    n_z, top = n_e // CORES, expert_ids.shape[1]
    cap = rows * (top + 1) // n_e
    lanes = -(-n_e // 8) * 8
    block, half = 4 * cap, hid // 2
    piece, hpiece = width // 4, hid // 8
    total = n_z * block
    chunks = []
    for k, cuts in ((0, XCUTS), (1, GCUTS)):
        at = 0
        for eighths in cuts:
            chunks.append((k, at * width // 8, eighths * width // 8))
            at += eighths
    n_c = len(chunks)
    bf, f32 = jnp.bfloat16, jnp.float32
    vmem = pl.BlockSpec(memory_space=pltpu.VMEM)
    hbm = pl.BlockSpec(memory_space=pltpu.HBM)
    dma = pltpu.SemaphoreType.DMA
    scratch = [
        (expert_ids.shape[::-1], expert_ids.dtype),
        (gate_probs.shape[::-1], gate_probs.dtype),
        ((n_z, 2 * lanes, rows), f32),
        ((n_z, 2 * cap, rows), bf),
        ((n_z, 2 * cap, 128), f32),
        ((width, hid), bf),
        ((width, hid), bf),
        ((hid, width), bf),
        ((2, 2, hid, hid), bf),
        ((width, hid), bf),
        ((width, hid), bf),
        ((hid, width), bf),
        ((2, block, hid), f32),
        ((2, block, hid), f32),
        ((width, total), bf),
        ((total, hid), bf),
        ((half, total), bf),
    ]
    scratch += [((2, piece, hid), bf), ((2, hpiece, width), bf)] * 2
    scratch += [((2, piece, hid), f32), ((2, hpiece, width), f32)]
    scratch += [((2, piece, hid), bf), ((2, hpiece, width), bf)] * 2
    scratch += [((piece, hid), bf)]
    sizes = [w for _, _, w in chunks]
    scratch += [((n_z, rows, w), bf) for w in sizes]
    scratch += [((n_z, 2, cap, w), bf) for w in sizes]
    scratch += [((n_z, 4, cap, w), bf) for w in sizes]
    held = sum(math.prod(shape) * jnp.dtype(kind).itemsize for shape, kind in scratch)
    args = (tokens, out_grad, expert_ids.T, gate_probs.T, w_gate, w_up, w_down)
    made = pl.pallas_call(
        functools.partial(grid_kernel, n_e, cap, chunks),
        out_shape=(
            jax.ShapeDtypeStruct((1, piece, hid), bf),
            jax.ShapeDtypeStruct((1, piece, hid), bf),
            jax.ShapeDtypeStruct((1, 2 * hpiece, width), bf),
        ),
        in_specs=[hbm] * 7,
        out_specs=(vmem, vmem, vmem),
        scratch_shapes=[pltpu.VMEM(shape, kind) for shape, kind in scratch]
        + [
            dma((2,)),
            dma((n_c,)),
            dma((3,)),
            dma((3,)),
            dma((3,)),
            dma((2, n_z)),
            dma((n_z,)),
            dma((n_c, 2, n_z)),
            dma((n_c, n_z)),
            dma((n_c, n_z, 3)),
            dma((n_c, n_z, 4)),
        ]
        + [dma((2, 5))] * 4
        + [dma((4,))] * 2,
        compiler_params=pltpu.CompilerParams(
            collective_id=1, has_side_effects=True, vmem_limit_bytes=held + (12 << 20)
        ),
    )(*(pltpu.with_memory_space_constraint(x, pltpu.HBM) for x in args))
    return write_out(made)


def solution(mesh):
    n_e, n_d = mesh.shape["expert"], mesh.shape["dp"]
    n_b = max(b for b in range(1, n_d + 1) if n_d % b == 0 and b * b <= n_d)
    n_a = n_d // n_b

    def step(tokens, out_grad, expert_ids, gate_probs, w_gate, w_up, w_down):
        rows, width = tokens.shape
        hid = w_gate.shape[2]
        total = n_e * rows
        lanes = -(-n_e // 8) * 8
        bf, f32 = jnp.bfloat16, jnp.float32
        vmem = pl.BlockSpec(memory_space=pltpu.VMEM)
        hbm = pl.BlockSpec(memory_space=pltpu.HBM)
        piece, hpiece = width // n_d, hid // n_d
        dma = pltpu.SemaphoreType.DMA
        scratch = [
            (expert_ids.shape[::-1], expert_ids.dtype),
            (gate_probs.shape[::-1], gate_probs.dtype),
            ((n_e, rows, width), bf),
            ((n_e, rows, width), bf),
            ((n_e, lanes, rows), f32),
            ((width, hid), bf),
            ((width, hid), bf),
            ((hid, width), bf),
            ((2, CORES * rows, 2 * hid), f32),
            ((width, total), bf),
            ((hid, total), bf),
            ((total, 2 * hid), bf),
            ((total, width), bf),
            ((2, width, hid), bf),
            ((2, n_d, hpiece, width // 2), bf),
            ((2, n_a, n_a, piece, hid), bf),
            ((2, n_a, n_a, hpiece, width // 2), bf),
            ((2, n_a, piece, hid), bf),
            ((2, n_a, hpiece, width // 2), bf),
            ((2, n_a, piece, hid), bf),
            ((2, n_a, hpiece, width // 2), bf),
        ]
        held = sum(math.prod(shape) * jnp.dtype(kind).itemsize for shape, kind in scratch)
        args = (tokens, out_grad, expert_ids.T, gate_probs.T, w_gate, w_up, w_down)
        made = pl.pallas_call(
            functools.partial(kernel, n_e, n_a, n_b),
            out_shape=(
                jax.ShapeDtypeStruct((1, piece, hid), bf),
                jax.ShapeDtypeStruct((1, piece, hid), bf),
                jax.ShapeDtypeStruct((1, hpiece, width), bf),
            ),
            in_specs=[hbm] * 7,
            out_specs=(vmem, vmem, vmem),
            scratch_shapes=[pltpu.VMEM(shape, kind) for shape, kind in scratch]
            + [
                dma((7,)),
                dma((3, 2, n_e)),
                dma((3, n_e)),
                dma((3, n_e)),
                dma((2, 2, n_d)),
                dma((2, 2, n_a, n_a)),
                dma((2, 2, n_a)),
                dma((2, 2, n_a)),
            ],
            compiler_params=pltpu.CompilerParams(
                collective_id=0, has_side_effects=True, vmem_limit_bytes=held + (10 << 20)
            ),
        )(*(pltpu.with_memory_space_constraint(x, pltpu.HBM) for x in args))
        return write_out(made)

    if n_a == 2 and n_b == 2:
        step = functools.partial(grid_step, n_e)
    spread = P(("expert", "dp"), None)
    return jax.shard_map(
        step,
        mesh=mesh,
        in_specs=(spread, spread, spread, spread) + (P("expert", None, None),) * 3,
        out_specs=(P("expert", "dp", None),) * 3,
        check_vma=False,
    )
```

```python
import functools
import math

import jax
import jax.numpy as jnp
from jax import lax
from jax.experimental import pallas as pl
from jax.experimental.pallas import tpu as pltpu
from jax.sharding import PartitionSpec as P

MESH = pl.DeviceIdType.MESH
CORES = 2
XCUTS, GCUTS = (8,), (4, 4)


def kernel(
    n_e, n_a, n_b,
    tok, cot, ids_in, probs_in, wg_in, wu_in, wd_in,
    out_g, out_u, out_d,
    ids, probs, X, G, PT, WG, WU, WD, GU, XT, HT, GG, S, MB, DB, MR, DR, MP, DP, MQ, DQ,
    lsem, chain_s, sib_s, blk_r, one_s, one_r, two_s, two_r,
):
    n_d = n_a * n_b
    rows, width = tok.shape
    hid = wg_in.shape[2]
    top = ids_in.shape[0]
    n_z = n_e // CORES
    me = lax.axis_index("expert")
    dd = lax.axis_index("dp")
    z, c = me // CORES, me % CORES
    sib = z * CORES + (1 - c)

    barrier = pltpu.get_barrier_semaphore()
    for step in (-1, 1):
        @pl.when(jnp.logical_and(z + step >= 0, z + step < n_z))
        def _():
            pl.semaphore_signal(barrier, inc=1, device_id={"expert": me + step * CORES}, device_id_type=MESH)
    pl.semaphore_signal(barrier, inc=1, device_id={"expert": sib}, device_id_type=MESH)
    for i in range(1, n_a):
        pl.semaphore_signal(barrier, inc=1, device_id={"dp": ((dd // n_b + i) % n_a) * n_b + dd % n_b}, device_id_type=MESH)
    for i in range(1, n_b):
        pl.semaphore_signal(barrier, inc=1, device_id={"dp": dd // n_b * n_b + (dd % n_b + i) % n_b}, device_id_type=MESH)
    small = [
        pltpu.make_async_copy(ids_in, ids, lsem.at[5]),
        pltpu.make_async_copy(probs_in, probs, lsem.at[6]),
    ]
    for copy in small:
        copy.start()
    for copy in small:
        copy.wait()
    erow = lax.broadcasted_iota(jnp.int32, PT.shape[1:], 0)
    table = jnp.zeros(PT.shape[1:], jnp.float32)
    for k in range(top):
        table = table + jnp.where(ids[k : k + 1, :] == erow, probs[k : k + 1, :], 0.0)
    PT[me] = table

    arrivals = n_a + n_b - 1 + jnp.where(z > 0, 1, 0) + jnp.where(z < n_z - 1, 1, 0)
    pl.semaphore_wait(barrier, arrivals)

    full = (PT, X, G)
    own = (PT.at[me], tok, cot)

    def hop(k, d, src, mine):
        there = me + (CORES if d == 0 else -CORES)
        return pltpu.make_async_remote_copy(
            src_ref=own[k] if mine else full[k].at[src],
            dst_ref=full[k].at[src],
            send_sem=chain_s.at[k, d, src],
            recv_sem=blk_r.at[k, src],
            device_id={"expert": there},
            device_id_type=MESH,
        )

    def across(k, src, mine):
        return pltpu.make_async_remote_copy(
            src_ref=own[k] if mine else full[k].at[src],
            dst_ref=full[k].at[src],
            send_sem=sib_s.at[k, src],
            recv_sem=blk_r.at[k, src],
            device_id={"expert": sib},
            device_id_type=MESH,
        )

    def can(d):
        return z < n_z - 1 if d == 0 else z > 0

    for k in range(3):
        for d in range(2):
            @pl.when(can(d))
            def _():
                hop(k, d, me, True).start()
        across(k, me, True).start()
    local = [
        pltpu.make_async_copy(tok, X.at[me], lsem.at[0]),
        pltpu.make_async_copy(cot, G.at[me], lsem.at[1]),
        pltpu.make_async_copy(wg_in.at[0], WG, lsem.at[2]),
        pltpu.make_async_copy(wu_in.at[0], WU, lsem.at[3]),
        pltpu.make_async_copy(wd_in.at[0], WD, lsem.at[4]),
    ]
    for copy in local:
        copy.start()
    for copy in local:
        copy.wait()

    pair = CORES * rows

    def base(zz):
        return pl.multiple_of(zz * pair, pair)

    def forward_tokens(zz, d):
        for k in range(2):
            across(k, zz * CORES + (1 - c), False).wait_recv()
        x = X[pl.ds(zz * CORES, CORES)].reshape(pair, width)
        GU[d, :, :hid] = jnp.dot(x, WG[...], preferred_element_type=jnp.float32)
        GU[d, :, hid:] = jnp.dot(x, WU[...], preferred_element_type=jnp.float32)
        XT[:, pl.ds(base(zz), pair)] = x.T

    def forward_cots(zz, d):
        across(2, zz * CORES + (1 - c), False).wait_recv()
        at = base(zz)
        parts = []
        for h in range(CORES):
            p = PT[zz * CORES + h, pl.ds(me, 1), :]
            p = jnp.broadcast_to(p, (rows, rows)).T[:, :1]
            parts.append((p * G[zz * CORES + h].astype(jnp.float32)).astype(jnp.bfloat16))
        scaled = jnp.concatenate(parts, axis=0)
        S[pl.ds(at, pair), :] = scaled
        gh = lax.dot_general(scaled, WD[...], (((1,), (1,)), ((), ())), preferred_element_type=jnp.float32)
        gate, up = GU[d, :, :hid], GU[d, :, hid:]
        sigma = jax.nn.sigmoid(gate)
        active = gate * sigma
        GG[pl.ds(at, pair), :hid] = (gh * up * sigma * (1.0 + gate * (1.0 - sigma))).astype(jnp.bfloat16)
        GG[pl.ds(at, pair), hid:] = (gh * active).astype(jnp.bfloat16)
        HT[:, pl.ds(at, pair)] = (active * up).astype(jnp.bfloat16).T

    def both(s, work):
        @pl.loop(0, 2)
        def _(d):
            zz = jnp.where(d == 0, z - s, z + s)

            @pl.when((zz >= 0) & (zz < n_z) & ((s > 0) | (d == 0)))
            def _():
                work(zz, d)

    def pass_on(s, kinds):
        for k in kinds:
            for d in range(2):
                zz = z - s if d == 0 else z + s
                src = zz * CORES + c

                @pl.when((zz >= 0) & (zz < n_z))
                def _():
                    hop(k, d, src, False).wait_recv()

                    @pl.when(can(d))
                    def _():
                        hop(k, d, src, False).start()

                    across(k, src, False).start()

    @pl.loop(0, n_z)
    def _(s):
        @pl.when(s > 0)
        def _():
            pass_on(s, (0, 1))

        both(s, forward_tokens)

        @pl.when(s > 0)
        def _():
            pass_on(s, (2,))

        both(s, forward_cots)

    piece, hpiece = width // n_d, hid // n_d
    chunk = max(piece, min(256, width))
    n_c = width // chunk
    hchunk, per = hid // n_c, chunk // piece
    half = width // 2

    def index(p, second, first):
        return second * n_b + first if p == 0 else first * n_b + second

    def first_of(p, j):
        return j % n_b if p == 0 else j // n_b

    def second_of(p, j):
        return j // n_b if p == 0 else j % n_b

    def mpiece(p, j):
        return MB.at[p, pl.ds(pl.multiple_of(j * piece, piece), piece)]

    def one(p, t, j):
        mine, there = first_of(p, dd), second_of(p, j)
        return pltpu.make_async_remote_copy(
            src_ref=mpiece(p, j) if t == 0 else DB.at[p, j],
            dst_ref=(MR if t == 0 else DR).at[p, mine, there],
            send_sem=one_s.at[p, t, j],
            recv_sem=one_r.at[p, t, mine, there],
            device_id={"dp": index(p, second_of(p, dd), first_of(p, j))},
            device_id_type=MESH,
        )

    def one_from(p, t, first, second):
        dst = (MR if t == 0 else DR).at[p, first, second]
        return pltpu.make_async_remote_copy(
            src_ref=dst, dst_ref=dst,
            send_sem=one_s.at[p, t, 0],
            recv_sem=one_r.at[p, t, first, second],
            device_id={"dp": index(p, second_of(p, dd), first)},
            device_id_type=MESH,
        )

    def two(p, t, second, slot):
        return pltpu.make_async_remote_copy(
            src_ref=(MP if t == 0 else DP).at[p, second],
            dst_ref=(MQ if t == 0 else DQ).at[p, slot],
            send_sem=two_s.at[p, t, second],
            recv_sem=two_r.at[p, t, slot],
            device_id={"dp": index(p, second, first_of(p, dd))},
            device_id_type=MESH,
        )

    @pl.loop(0, n_c)
    def _(i):
        if per == 1:
            step_a, step_b = n_a - 1 - i // n_b, n_b - 1 - i % n_b
            cc = ((dd // n_b + step_a) % n_a) * n_b + (dd % n_b + step_b) % n_b
        else:
            cc = (dd // per + 1 + i) % n_c
        at = pl.multiple_of(cc * chunk, chunk)
        hat = pl.multiple_of(cc * hchunk, hchunk)
        up_gate = jnp.dot(
            XT[pl.ds(at, chunk), :], GG[...], preferred_element_type=jnp.float32
        ).astype(jnp.bfloat16)
        for p in range(2):
            MB[p, pl.ds(at, chunk), :] = up_gate[:, p * hid : (p + 1) * hid]
        for t in range(2):
            if t == 1:
                down = jnp.dot(
                    HT[pl.ds(hat, hchunk), :], S[...], preferred_element_type=jnp.float32
                ).astype(jnp.bfloat16)
                for p in range(2):
                    for q in range(per):
                        DB[p, cc * per + q] = down[q * hpiece : (q + 1) * hpiece, p * half : (p + 1) * half]
            for p in range(2):
                for q in range(per):
                    j = cc * per + q

                    @pl.when(first_of(p, j) != first_of(p, dd))
                    def _():
                        one(p, t, j).start()

    def partial(p, t, second):
        first = first_of(p, dd)
        count = n_b if p == 0 else n_a
        j = index(p, second, first)
        total = (mpiece(p, j)[...] if t == 0 else DB[p, j]).astype(jnp.float32)
        for i in range(1, count):
            other = (first + i) % count
            one_from(p, t, other, second).wait_recv()
            total = total + (MR if t == 0 else DR)[p, other, second].astype(jnp.float32)
        return total

    for t in range(2):
        for p in range(2):
            count = n_a if p == 0 else n_b

            @pl.loop(1, count)
            def _(i):
                second = (second_of(p, dd) + i) % count
                (MP if t == 0 else DP)[p, second] = partial(p, t, second).astype(jnp.bfloat16)
                two(p, t, second, second_of(p, dd)).start()

    for t in range(2):
        for p in range(2):
            count = n_a if p == 0 else n_b
            mine = second_of(p, dd)
            total = partial(p, t, mine)
            for i in range(1, count):
                other = (mine + i) % count
                two(p, t, other, other).wait_recv()
                total = total + (MQ if t == 0 else DQ)[p, other].astype(jnp.float32)
            if t == 0:
                (out_g, out_u)[p][0] = total.astype(jnp.bfloat16)
            else:
                out_d[0, :, p * half : (p + 1) * half] = total.astype(jnp.bfloat16)

    for p in range(2):
        for t in range(2):
            @pl.loop(0, n_d)
            def _(j):
                @pl.when(first_of(p, j) != first_of(p, dd))
                def _():
                    one(p, t, j).wait_send()

            count = n_a if p == 0 else n_b

            @pl.loop(1, count)
            def _(i):
                two(p, t, (second_of(p, dd) + i) % count, second_of(p, dd)).wait_send()

    @pl.loop(0, n_z)
    def _(s):
        for k in range(3):
            for d in range(2):
                zz = z - s if d == 0 else z + s
                src = zz * CORES + c

                @pl.when((zz >= 0) & (zz < n_z) & can(d))
                def _():
                    hop(k, d, src, False).wait_send()

            across(k, s * CORES + c, False).wait_send()


def copy_out(*refs):
    n = len(refs) // 2
    copies = [pltpu.make_async_copy(refs[i], refs[n + i], refs[-1].at[i]) for i in range(n)]
    for copy in copies:
        copy.start()
    for copy in copies:
        copy.wait()


def write_out(arrays):
    anywhere = pl.BlockSpec(memory_space=pl.ANY)
    return pl.pallas_call(
        copy_out,
        out_shape=tuple(jax.ShapeDtypeStruct(x.shape, x.dtype) for x in arrays),
        in_specs=[anywhere] * len(arrays),
        out_specs=(anywhere,) * len(arrays),
        scratch_shapes=[pltpu.SemaphoreType.DMA((len(arrays),))],
        compiler_params=pltpu.CompilerParams(vmem_limit_bytes=1 << 20),
    )(*arrays)


def grid_kernel(
    n_e, cap, chunks,
    tok, cot, ids_in, probs_in, wg_in, wu_in, wd_in,
    out_g, out_u, out_d,
    ids, probs, TB, SEL, PSC, WG, WU, WD, E, WGG, WUU, WDD, SL, GH, XT, GG, HT,
    SM, SD, RM, RD, OM, OD, TM, TD, FM, FD, RL, *more,
):
    n_c = len(chunks)
    firsts = [i for i, (k, _, _) in enumerate(chunks) if k == 0]
    seconds = [i for i, (k, _, _) in enumerate(chunks) if k == 1]
    groups = [more[i * n_c : (i + 1) * n_c] for i in range(3)]
    B, C, RC = groups
    more = more[3 * n_c :]
    n_s = len(seconds)
    (
        small_l, own_l, wt_l, wt_s, wt_r, tab_s, tab_r, blk_s, blk_r, row_s, row_r,
        red_s, red_r, fin_s, fin_r, lent_r, lent_s,
    ) = more
    bf, f32 = jnp.bfloat16, jnp.float32
    rows, width = tok.shape
    hid = wg_in.shape[2]
    top = ids_in.shape[0]
    n_z = n_e // CORES
    me = lax.axis_index("expert")
    dd = lax.axis_index("dp")
    z, c = me // CORES, me % CORES
    y, x = dd // 2, dd % 2
    sib = z * CORES + (1 - c)
    g, f = jnp.where(c == 0, x, y), jnp.where(c == 0, y, x)
    across_x, across_y = y * 2 + (1 - x), (1 - y) * 2 + x

    def greet(where):
        pl.semaphore_signal(barrier, inc=1, device_id=where, device_id_type=MESH)

    barrier = pltpu.get_barrier_semaphore()
    for step in (-1, 1):
        @pl.when(jnp.logical_and(z + step >= 0, z + step < n_z))
        def _():
            greet({"expert": me + step * CORES, "dp": dd})
    greet({"expert": sib, "dp": dd})
    for other in (across_x, across_y):
        for core in range(CORES):
            greet({"expert": z * CORES + core, "dp": other})

    lends, lent = n_z >= 4, [0, 1, 2]
    across = jnp.where(c == 0, across_y, across_x)
    at_end = (z == 0) | (z == n_z - 1)
    beside_end = (z == 1) | (z == n_z - 2)
    inner, outer = jnp.where(z == 0, 1, n_z - 2), jnp.where(z == 1, 0, n_z - 1)
    lenders = 0
    if lends:
        lenders = jnp.where(at_end, 1, 0)

        @pl.when(beside_end)
        def _():
            greet({"expert": outer * CORES + c, "dp": across})

    small = [
        pltpu.make_async_copy(ids_in, ids, small_l.at[0]),
        pltpu.make_async_copy(probs_in, probs, small_l.at[1]),
    ]
    for copy in small:
        copy.start()

    def own(i):
        k, at, w = chunks[i]
        return (tok, cot)[k].at[:, pl.ds(at, w)]

    def own_copy(i):
        return pltpu.make_async_copy(own(i), B[i].at[z], own_l.at[i])

    for i in range(n_c):
        own_copy(i).start()
    for copy in small:
        copy.wait()
    lanes = TB.shape[1] // 2
    erow = lax.broadcasted_iota(jnp.int32, (lanes, rows), 0)
    table = jnp.zeros((lanes, rows), f32)
    named = jnp.zeros((lanes, rows), f32)
    for k in range(top):
        hit = ids[k : k + 1, :] == erow
        table = table + jnp.where(hit, probs[k : k + 1, :], 0.0)
        named = named + jnp.where(hit, 1.0, 0.0)
    before = jnp.where(
        lax.broadcasted_iota(jnp.int32, (rows, rows), 0) < lax.broadcasted_iota(jnp.int32, (rows, rows), 1), 1.0, 0.0
    ).astype(bf)
    place = jnp.dot(named.astype(bf), before, preferred_element_type=f32)
    TB[z, :lanes] = table
    TB[z, lanes:] = jnp.where(named > 0.0, place, -1.0)

    pl.semaphore_wait(barrier, 5 + lenders + jnp.where(z > 0, 1, 0) + jnp.where(z < n_z - 1, 1, 0))

    def onward(d):
        return {"expert": me + jnp.where(d == 0, CORES, -CORES), "dp": dd}

    def can(d):
        return jnp.where(d == 0, n_z - 1 - z, z) > 0

    def plane(s, d):
        return jnp.where(d == 0, z - s, z + s)

    def tab_hop(d, src):
        return pltpu.make_async_remote_copy(
            src_ref=TB.at[src], dst_ref=TB.at[src], send_sem=tab_s.at[d, src], recv_sem=tab_r.at[src],
            device_id=onward(d), device_id_type=MESH,
        )

    def hop(i, d, src, mine):
        return pltpu.make_async_remote_copy(
            src_ref=own(i) if mine else B[i].at[src],
            dst_ref=B[i].at[src],
            send_sem=blk_s.at[i, d, src],
            recv_sem=blk_r.at[i, src],
            device_id=onward(d), device_id_type=MESH,
        )

    for d in range(2):
        @pl.when(can(d))
        def _():
            tab_hop(d, z).start()
    for i in range(n_c):
        for d in range(2):
            @pl.when(can(d))
            def _():
                hop(i, d, z, True).start()

    weights = ((wg_in, WG), (wu_in, WU), (wd_in, WD))

    def share(i):
        return pltpu.make_async_remote_copy(
            src_ref=weights[i][0].at[0], dst_ref=weights[i][1], send_sem=wt_s.at[i], recv_sem=wt_r.at[i],
            device_id={"expert": sib, "dp": dd}, device_id_type=MESH,
        )

    def keep(i):
        return pltpu.make_async_copy(weights[i][0].at[0], weights[i][1], wt_l.at[i])

    g_sib = jnp.where(c == 0, y, x)
    mine_here, mine_there = g == c, g_sib == c
    for i in range(3):
        @pl.when(mine_there)
        def _():
            share(i).start()

        @pl.when(mine_here)
        def _():
            keep(i).start()

    half, hh = hid // 2, hid // 8
    for slot in range(2):
        for t in range(2):
            j = lax.broadcasted_iota(jnp.int32, (hid, hid), 0) - t * half
            u = j + slot * hh
            for cut in range(1, 4):
                u = u + jnp.where(j >= cut * hh, hh, 0)
            inside = (j >= 0) & (j < half)
            there = lax.broadcasted_iota(jnp.int32, (hid, hid), 1)
            E[slot, t] = jnp.where(inside & (u == there), 1.0, 0.0).astype(bf)

    def row(i, src, to, part):
        where = (
            {"expert": sib, "dp": dd},
            {"expert": z * CORES, "dp": across_x},
            {"expert": z * CORES + 1, "dp": across_y},
        )[to]
        return pltpu.make_async_remote_copy(
            src_ref=C[i].at[src, (g_sib, 1 - x, 1 - y)[to]],
            dst_ref=RC[i].at[src, part],
            send_sem=row_s.at[i, src, to],
            recv_sem=row_r.at[i, src, part],
            device_id=where, device_id_type=MESH,
        )

    def each(s, work):
        @pl.loop(0, 2)
        def _(d):
            src = plane(s, d)

            @pl.when((src >= 0) & (src < n_z) & ((s > 0) | (d == 0)))
            def _():
                work(src, d)

    def tables(s):
        def work(src, d):
            @pl.when(s > 0)
            def _():
                tab_hop(d, src).wait_recv()

                @pl.when(can(d))
                def _():
                    tab_hop(d, src).start()

            slot = lax.broadcasted_iota(jnp.int32, (cap, rows), 0).astype(f32)
            for ee in range(2):
                hit = TB[src, pl.ds(lanes + z * CORES + ee, 1), :] == slot
                SEL[src, ee * cap : (ee + 1) * cap] = jnp.where(hit, 1.0, 0.0).astype(bf)
                weight = jnp.where(hit, TB[src, pl.ds(z * CORES + ee, 1), :], 0.0).sum(axis=1, keepdims=True)
                PSC[src, ee * cap : (ee + 1) * cap] = jnp.broadcast_to(weight, (cap, 128))

        each(s, work)

    def arrive(s, i):
        def work(src, d):
            @pl.when(s == 0)
            def _():
                own_copy(i).wait()

            @pl.when(s > 0)
            def _():
                hop(i, d, src, False).wait_recv()

                @pl.when(can(d))
                def _():
                    hop(i, d, src, False).start()

            picked = jnp.dot(SEL[src], B[i][src], preferred_element_type=f32)
            if chunks[i][0] == 1:
                picked = picked * PSC[src][:, :1]
            C[i][src] = picked.astype(bf).reshape(2, cap, chunks[i][2])
            row(i, src, 1, 2 + c).start()
            row(i, src, 2, 2 + c).start()
            row(i, src, 0, c).start()
            RC[i][src, c] = C[i][src, g]

        each(s, work)

    def collect(i, src):
        for part in (1 - c, 2, 3):
            row(i, src, 0, part).wait_recv()
        return RC[i][src].reshape(block, chunks[i][2])

    block = 4 * cap

    def base(src):
        return pl.multiple_of(src * block, block)

    def forward_tokens(s):
        def work(src, d):
            gate = jnp.zeros((block, hid), f32)
            up = jnp.zeros((block, hid), f32)
            for i in firsts:
                _, at, w = chunks[i]
                xs = collect(i, src)
                gate = gate + jnp.dot(xs, WGG[at : at + w], preferred_element_type=f32)
                up = up + jnp.dot(xs, WUU[at : at + w], preferred_element_type=f32)
                XT[at : at + w, pl.ds(base(src), block)] = xs.T
            sigma = jax.nn.sigmoid(gate)
            active = gate * sigma
            lane = lax.broadcasted_iota(jnp.int32, (block, hid), 1)
            SL[d] = jnp.where(lane < half, up * sigma * (1.0 + gate * (1.0 - sigma)), active)
            HT[:, pl.ds(base(src), block)] = (active * up).astype(bf).T[:half]

        each(s, work)

    def forward_cots(s, which):
        def work(src, d):
            total = jnp.zeros((block, hid), f32) if which[0] == seconds[0] else GH[d]
            for i in which:
                _, at, w = chunks[i]
                total = total + lax.dot_general(
                    collect(i, src), WDD[:, at : at + w], (((1,), (1,)), ((), ())), preferred_element_type=f32
                )
            if which[-1] == seconds[-1]:
                GG[pl.ds(base(src), block), :] = (total * SL[d]).astype(bf)
            else:
                GH[d] = total

        each(s, work)

    def prepare():
        for i in range(3):
            @pl.when(mine_here)
            def _():
                keep(i).wait()

            @pl.when(jnp.logical_not(mine_here))
            def _():
                share(i).wait_recv()
        spread = (E[c, 0].astype(f32) + E[c, 1].astype(f32)).astype(bf)
        for source, made in ((WG, WGG), (WU, WUU)):
            made[...] = lax.dot_general(
                source[...], spread, (((1,), (1,)), ((), ())), preferred_element_type=f32
            ).astype(bf)
        WDD[...] = jnp.dot(spread, WD[...], preferred_element_type=f32).astype(bf)

    @pl.loop(0, n_z - 1)
    def _(s):
        tables(s)
        for i in firsts:
            arrive(s, i)

        @pl.when(s > 0)
        def _():
            forward_cots(s - 1, seconds)

        for i in seconds[:-1]:
            arrive(s, i)

        @pl.when(s == 0)
        def _():
            prepare()

        forward_tokens(s)
        arrive(s, seconds[-1])

    last = n_z - 1
    tables(last)
    for i in firsts:
        arrive(last, i)
    forward_cots(last - 1, seconds)
    arrive(last, seconds[0])
    forward_tokens(last)
    for i in seconds[1:]:
        arrive(last, i)

    piece, hpiece = width // 4, half // 4
    part = piece // 4
    n_t = piece // part

    def quarter(ff, gg):
        return jnp.where(c == 0, ff * 2 + gg, gg * 2 + ff)

    def wide(j, t):
        at = pl.multiple_of(j * piece + t * part, part)
        return jnp.dot(XT[pl.ds(at, part), :], GG[...], preferred_element_type=f32)

    def deep(j, n):
        at = pl.multiple_of(j * hpiece, hpiece)
        i = seconds[n]
        return jnp.dot(
            HT[pl.ds(at, hpiece), :], RC[i][...].reshape(n_z * block, chunks[i][2]), preferred_element_type=f32
        )

    def columns(n):
        _, at, w = chunks[seconds[n]]
        return pl.ds(at, w)

    def spot(M, D, i, t):
        return M.at[i, pl.ds(t * part, part)] if t < n_t else D.at[i, :, columns(t - n_t)]

    def reduce_copy(i, t):
        return pltpu.make_async_remote_copy(
            src_ref=spot(SM, SD, i, t), dst_ref=spot(RM, RD, i, t),
            send_sem=red_s.at[i, t], recv_sem=red_r.at[i, t],
            device_id={"expert": me, "dp": quarter(1 - f, g)}, device_id_type=MESH,
        )

    def final_copy(i, t):
        return pltpu.make_async_remote_copy(
            src_ref=spot(TM, TD, i, t), dst_ref=spot(FM, FD, c, t),
            send_sem=fin_s.at[i, t], recv_sem=fin_r.at[c, t],
            device_id={"expert": z * CORES + g, "dp": quarter(f, 1 - g) if i == 0 else dd}, device_id_type=MESH,
        )

    def lend(t):
        return pltpu.make_async_remote_copy(
            src_ref=spot(SM, SD, 1, t), dst_ref=RL.at[pl.ds(t * part, part)],
            send_sem=red_s.at[1, t], recv_sem=lent_r.at[t],
            device_id={"expert": inner * CORES + c, "dp": across}, device_id_type=MESH,
        )

    def give_back(t):
        return pltpu.make_async_remote_copy(
            src_ref=RL.at[pl.ds(t * part, part)], dst_ref=spot(RM, RD, 1, t),
            send_sem=lent_s.at[t], recv_sem=red_r.at[1, t],
            device_id={"expert": outer * CORES + c, "dp": dd}, device_id_type=MESH,
        )

    def send_wide(i, t):
        j = quarter(1 - f, (1 - g) if i == 0 else g)
        SM[i, t * part : (t + 1) * part] = wide(j, t).astype(bf)
        if i == 0 or t not in lent or not lends:
            reduce_copy(i, t).start()
        else:
            @pl.when(at_end)
            def _():
                lend(t).start()

            @pl.when(jnp.logical_not(at_end))
            def _():
                reduce_copy(1, t).start()

    def send_deep(i, n):
        SD[i, :, columns(n)] = deep(quarter(1 - f, (1 - g) if i == 0 else g), n).astype(bf)
        reduce_copy(i, n_t + n).start()

    def keep_own(i, t):
        j = quarter(f, (1 - g) if i == 0 else g)
        if t < n_t:
            OM[i, t * part : (t + 1) * part] = wide(j, t)
        else:
            OD[i, :, columns(t - n_t)] = deep(j, t - n_t)

    def pass_total(i, t):
        reduce_copy(i, t).wait_recv()
        if t < n_t:
            at = slice(t * part, (t + 1) * part)
            TM[i, at] = (OM[i, at] + RM[i, at].astype(f32)).astype(bf)
        else:
            to = columns(t - n_t)
            TD[i, :, to] = (OD[i, :, to] + RD[i, :, to].astype(f32)).astype(bf)
        if i == 0:
            final_copy(0, t).start()
        else:
            @pl.when(g != c)
            def _():
                final_copy(1, t).start()

            @pl.when(g == c)
            def _():
                if t < n_t:
                    FM[c, at] = TM[1, at]
                else:
                    FD[c, :, to] = TD[1, :, to]

    forward_cots(last, seconds[:1])
    send_deep(0, 0)
    send_deep(1, 0)
    keep_own(0, 4)
    keep_own(1, 4)
    forward_cots(last, seconds[1:])
    send_wide(0, 0)
    send_wide(1, 0)
    send_wide(0, 1)
    send_wide(1, 1)
    send_wide(0, 2)
    send_wide(1, 2)
    send_wide(0, 3)
    send_deep(0, 1)
    send_deep(1, 1)
    send_wide(1, 3)
    keep_own(0, 0)
    pass_total(0, 4)
    keep_own(0, 1)
    pass_total(0, 0)
    keep_own(0, 2)
    pass_total(0, 1)
    keep_own(0, 3)
    pass_total(0, 2)
    pass_total(0, 3)
    keep_own(0, 5)
    pass_total(0, 5)
    pass_total(1, 4)
    keep_own(1, 0)
    keep_own(1, 1)
    keep_own(1, 2)
    keep_own(1, 3)
    keep_own(1, 5)
    pass_total(1, 0)
    pass_total(1, 1)
    pass_total(1, 2)
    pass_total(1, 3)
    pass_total(1, 5)

    def landed(slot, t):
        return pltpu.make_async_remote_copy(
            src_ref=spot(FM, FD, slot, t), dst_ref=spot(FM, FD, slot, t),
            send_sem=fin_s.at[0, t], recv_sem=fin_r.at[slot, t],
            device_id={"expert": sib, "dp": dd}, device_id_type=MESH,
        )

    for t in [*range(n_t, n_t + n_s - 1), *range(n_t), n_t + n_s - 1]:
        @pl.when(g != c)
        def _():
            landed(c, t).wait_recv()

        landed(1 - c, t).wait_recv()
        if t < n_t:
            at = slice(t * part, (t + 1) * part)
            for o, out in enumerate((out_g, out_u)):
                out[0, at] = (
                    jnp.dot(FM[0, at], E[0, o], preferred_element_type=f32)
                    + jnp.dot(FM[1, at], E[1, o], preferred_element_type=f32)
                ).astype(bf)
        else:
            for slot in range(2):
                to = columns(t - n_t)
                out_d[0, slot * hpiece : (slot + 1) * hpiece, to] = FD[slot, :, to]

    if lends:
        @pl.when(beside_end)
        def _():
            for t in lent:
                lend(t).wait_recv()
                give_back(t).start()
            for t in lent:
                give_back(t).wait_send()

    for i in range(2):
        for t in range(n_t + n_s):
            reduce_copy(i, t).wait_send()
            if i == 0:
                final_copy(0, t).wait_send()
            else:
                @pl.when(g != c)
                def _():
                    final_copy(1, t).wait_send()

    @pl.when(mine_there)
    def _():
        for i in range(3):
            share(i).wait_send()

    @pl.loop(0, n_z)
    def _(src):
        for d in range(2):
            @pl.when(can(d) & (jnp.where(d == 0, z - src, src - z) >= 0))
            def _():
                tab_hop(d, src).wait_send()
                for i in range(n_c):
                    hop(i, d, src, False).wait_send()
        for i in range(n_c):
            for to in range(3):
                row(i, src, to, 0).wait_send()


def grid_step(n_e, tokens, out_grad, expert_ids, gate_probs, w_gate, w_up, w_down):
    rows, width = tokens.shape
    hid = w_gate.shape[2]
    n_z, top = n_e // CORES, expert_ids.shape[1]
    cap = rows * (top + 1) // n_e
    lanes = -(-n_e // 8) * 8
    block, half = 4 * cap, hid // 2
    piece, hpiece = width // 4, hid // 8
    total = n_z * block
    chunks = []
    for k, cuts in ((0, XCUTS), (1, GCUTS)):
        at = 0
        for eighths in cuts:
            chunks.append((k, at * width // 8, eighths * width // 8))
            at += eighths
    n_c = len(chunks)
    bf, f32 = jnp.bfloat16, jnp.float32
    vmem = pl.BlockSpec(memory_space=pltpu.VMEM)
    hbm = pl.BlockSpec(memory_space=pltpu.HBM)
    dma = pltpu.SemaphoreType.DMA
    scratch = [
        (expert_ids.shape[::-1], expert_ids.dtype),
        (gate_probs.shape[::-1], gate_probs.dtype),
        ((n_z, 2 * lanes, rows), f32),
        ((n_z, 2 * cap, rows), bf),
        ((n_z, 2 * cap, 128), f32),
        ((width, hid), bf),
        ((width, hid), bf),
        ((hid, width), bf),
        ((2, 2, hid, hid), bf),
        ((width, hid), bf),
        ((width, hid), bf),
        ((hid, width), bf),
        ((2, block, hid), f32),
        ((2, block, hid), f32),
        ((width, total), bf),
        ((total, hid), bf),
        ((half, total), bf),
    ]
    scratch += [((2, piece, hid), bf), ((2, hpiece, width), bf)] * 2
    scratch += [((2, piece, hid), f32), ((2, hpiece, width), f32)]
    scratch += [((2, piece, hid), bf), ((2, hpiece, width), bf)] * 2
    scratch += [((piece, hid), bf)]
    sizes = [w for _, _, w in chunks]
    scratch += [((n_z, rows, w), bf) for w in sizes]
    scratch += [((n_z, 2, cap, w), bf) for w in sizes]
    scratch += [((n_z, 4, cap, w), bf) for w in sizes]
    held = sum(math.prod(shape) * jnp.dtype(kind).itemsize for shape, kind in scratch)
    args = (tokens, out_grad, expert_ids.T, gate_probs.T, w_gate, w_up, w_down)
    made = pl.pallas_call(
        functools.partial(grid_kernel, n_e, cap, chunks),
        out_shape=(
            jax.ShapeDtypeStruct((1, piece, hid), bf),
            jax.ShapeDtypeStruct((1, piece, hid), bf),
            jax.ShapeDtypeStruct((1, 2 * hpiece, width), bf),
        ),
        in_specs=[hbm] * 7,
        out_specs=(vmem, vmem, vmem),
        scratch_shapes=[pltpu.VMEM(shape, kind) for shape, kind in scratch]
        + [
            dma((2,)),
            dma((n_c,)),
            dma((3,)),
            dma((3,)),
            dma((3,)),
            dma((2, n_z)),
            dma((n_z,)),
            dma((n_c, 2, n_z)),
            dma((n_c, n_z)),
            dma((n_c, n_z, 3)),
            dma((n_c, n_z, 4)),
        ]
        + [dma((2, 6))] * 4
        + [dma((4,))] * 2,
        compiler_params=pltpu.CompilerParams(
            collective_id=1, has_side_effects=True, vmem_limit_bytes=held + (12 << 20)
        ),
    )(*(pltpu.with_memory_space_constraint(x, pltpu.HBM) for x in args))
    return write_out(made)


def solution(mesh):
    n_e, n_d = mesh.shape["expert"], mesh.shape["dp"]
    n_b = max(b for b in range(1, n_d + 1) if n_d % b == 0 and b * b <= n_d)
    n_a = n_d // n_b

    def step(tokens, out_grad, expert_ids, gate_probs, w_gate, w_up, w_down):
        rows, width = tokens.shape
        hid = w_gate.shape[2]
        total = n_e * rows
        lanes = -(-n_e // 8) * 8
        bf, f32 = jnp.bfloat16, jnp.float32
        vmem = pl.BlockSpec(memory_space=pltpu.VMEM)
        hbm = pl.BlockSpec(memory_space=pltpu.HBM)
        piece, hpiece = width // n_d, hid // n_d
        dma = pltpu.SemaphoreType.DMA
        scratch = [
            (expert_ids.shape[::-1], expert_ids.dtype),
            (gate_probs.shape[::-1], gate_probs.dtype),
            ((n_e, rows, width), bf),
            ((n_e, rows, width), bf),
            ((n_e, lanes, rows), f32),
            ((width, hid), bf),
            ((width, hid), bf),
            ((hid, width), bf),
            ((2, CORES * rows, 2 * hid), f32),
            ((width, total), bf),
            ((hid, total), bf),
            ((total, 2 * hid), bf),
            ((total, width), bf),
            ((2, width, hid), bf),
            ((2, n_d, hpiece, width // 2), bf),
            ((2, n_a, n_a, piece, hid), bf),
            ((2, n_a, n_a, hpiece, width // 2), bf),
            ((2, n_a, piece, hid), bf),
            ((2, n_a, hpiece, width // 2), bf),
            ((2, n_a, piece, hid), bf),
            ((2, n_a, hpiece, width // 2), bf),
        ]
        held = sum(math.prod(shape) * jnp.dtype(kind).itemsize for shape, kind in scratch)
        args = (tokens, out_grad, expert_ids.T, gate_probs.T, w_gate, w_up, w_down)
        made = pl.pallas_call(
            functools.partial(kernel, n_e, n_a, n_b),
            out_shape=(
                jax.ShapeDtypeStruct((1, piece, hid), bf),
                jax.ShapeDtypeStruct((1, piece, hid), bf),
                jax.ShapeDtypeStruct((1, hpiece, width), bf),
            ),
            in_specs=[hbm] * 7,
            out_specs=(vmem, vmem, vmem),
            scratch_shapes=[pltpu.VMEM(shape, kind) for shape, kind in scratch]
            + [
                dma((7,)),
                dma((3, 2, n_e)),
                dma((3, n_e)),
                dma((3, n_e)),
                dma((2, 2, n_d)),
                dma((2, 2, n_a, n_a)),
                dma((2, 2, n_a)),
                dma((2, 2, n_a)),
            ],
            compiler_params=pltpu.CompilerParams(
                collective_id=0, has_side_effects=True, vmem_limit_bytes=held + (10 << 20)
            ),
        )(*(pltpu.with_memory_space_constraint(x, pltpu.HBM) for x in args))
        return write_out(made)

    if n_a == 2 and n_b == 2:
        step = functools.partial(grid_step, n_e)
    spread = P(("expert", "dp"), None)
    return jax.shard_map(
        step,
        mesh=mesh,
        in_specs=(spread, spread, spread, spread) + (P("expert", None, None),) * 3,
        out_specs=(P("expert", "dp", None),) * 3,
        check_vma=False,
    )
```

```python
import functools
import math

import jax
import jax.numpy as jnp
from jax import lax
from jax.experimental import pallas as pl
from jax.experimental.pallas import tpu as pltpu
from jax.sharding import PartitionSpec as P

MESH = pl.DeviceIdType.MESH
CORES = 2
XCUTS, GCUTS = (8,), (4, 4)


def kernel(
    n_e, n_a, n_b,
    tok, cot, ids_in, probs_in, wg_in, wu_in, wd_in,
    out_g, out_u, out_d,
    ids, probs, X, G, PT, WG, WU, WD, GU, XT, HT, GG, S, MB, DB, MR, DR, MP, DP, MQ, DQ,
    lsem, chain_s, sib_s, blk_r, one_s, one_r, two_s, two_r,
):
    n_d = n_a * n_b
    rows, width = tok.shape
    hid = wg_in.shape[2]
    top = ids_in.shape[0]
    n_z = n_e // CORES
    me = lax.axis_index("expert")
    dd = lax.axis_index("dp")
    z, c = me // CORES, me % CORES
    sib = z * CORES + (1 - c)

    barrier = pltpu.get_barrier_semaphore()
    for step in (-1, 1):
        @pl.when(jnp.logical_and(z + step >= 0, z + step < n_z))
        def _():
            pl.semaphore_signal(barrier, inc=1, device_id={"expert": me + step * CORES}, device_id_type=MESH)
    pl.semaphore_signal(barrier, inc=1, device_id={"expert": sib}, device_id_type=MESH)
    for i in range(1, n_a):
        pl.semaphore_signal(barrier, inc=1, device_id={"dp": ((dd // n_b + i) % n_a) * n_b + dd % n_b}, device_id_type=MESH)
    for i in range(1, n_b):
        pl.semaphore_signal(barrier, inc=1, device_id={"dp": dd // n_b * n_b + (dd % n_b + i) % n_b}, device_id_type=MESH)
    small = [
        pltpu.make_async_copy(ids_in, ids, lsem.at[5]),
        pltpu.make_async_copy(probs_in, probs, lsem.at[6]),
    ]
    for copy in small:
        copy.start()
    for copy in small:
        copy.wait()
    erow = lax.broadcasted_iota(jnp.int32, PT.shape[1:], 0)
    table = jnp.zeros(PT.shape[1:], jnp.float32)
    for k in range(top):
        table = table + jnp.where(ids[k : k + 1, :] == erow, probs[k : k + 1, :], 0.0)
    PT[me] = table

    arrivals = n_a + n_b - 1 + jnp.where(z > 0, 1, 0) + jnp.where(z < n_z - 1, 1, 0)
    pl.semaphore_wait(barrier, arrivals)

    full = (PT, X, G)
    own = (PT.at[me], tok, cot)

    def hop(k, d, src, mine):
        there = me + (CORES if d == 0 else -CORES)
        return pltpu.make_async_remote_copy(
            src_ref=own[k] if mine else full[k].at[src],
            dst_ref=full[k].at[src],
            send_sem=chain_s.at[k, d, src],
            recv_sem=blk_r.at[k, src],
            device_id={"expert": there},
            device_id_type=MESH,
        )

    def across(k, src, mine):
        return pltpu.make_async_remote_copy(
            src_ref=own[k] if mine else full[k].at[src],
            dst_ref=full[k].at[src],
            send_sem=sib_s.at[k, src],
            recv_sem=blk_r.at[k, src],
            device_id={"expert": sib},
            device_id_type=MESH,
        )

    def can(d):
        return z < n_z - 1 if d == 0 else z > 0

    for k in range(3):
        for d in range(2):
            @pl.when(can(d))
            def _():
                hop(k, d, me, True).start()
        across(k, me, True).start()
    local = [
        pltpu.make_async_copy(tok, X.at[me], lsem.at[0]),
        pltpu.make_async_copy(cot, G.at[me], lsem.at[1]),
        pltpu.make_async_copy(wg_in.at[0], WG, lsem.at[2]),
        pltpu.make_async_copy(wu_in.at[0], WU, lsem.at[3]),
        pltpu.make_async_copy(wd_in.at[0], WD, lsem.at[4]),
    ]
    for copy in local:
        copy.start()
    for copy in local:
        copy.wait()

    pair = CORES * rows

    def base(zz):
        return pl.multiple_of(zz * pair, pair)

    def forward_tokens(zz, d):
        for k in range(2):
            across(k, zz * CORES + (1 - c), False).wait_recv()
        x = X[pl.ds(zz * CORES, CORES)].reshape(pair, width)
        GU[d, :, :hid] = jnp.dot(x, WG[...], preferred_element_type=jnp.float32)
        GU[d, :, hid:] = jnp.dot(x, WU[...], preferred_element_type=jnp.float32)
        XT[:, pl.ds(base(zz), pair)] = x.T

    def forward_cots(zz, d):
        across(2, zz * CORES + (1 - c), False).wait_recv()
        at = base(zz)
        parts = []
        for h in range(CORES):
            p = PT[zz * CORES + h, pl.ds(me, 1), :]
            p = jnp.broadcast_to(p, (rows, rows)).T[:, :1]
            parts.append((p * G[zz * CORES + h].astype(jnp.float32)).astype(jnp.bfloat16))
        scaled = jnp.concatenate(parts, axis=0)
        S[pl.ds(at, pair), :] = scaled
        gh = lax.dot_general(scaled, WD[...], (((1,), (1,)), ((), ())), preferred_element_type=jnp.float32)
        gate, up = GU[d, :, :hid], GU[d, :, hid:]
        sigma = jax.nn.sigmoid(gate)
        active = gate * sigma
        GG[pl.ds(at, pair), :hid] = (gh * up * sigma * (1.0 + gate * (1.0 - sigma))).astype(jnp.bfloat16)
        GG[pl.ds(at, pair), hid:] = (gh * active).astype(jnp.bfloat16)
        HT[:, pl.ds(at, pair)] = (active * up).astype(jnp.bfloat16).T

    def both(s, work):
        @pl.loop(0, 2)
        def _(d):
            zz = jnp.where(d == 0, z - s, z + s)

            @pl.when((zz >= 0) & (zz < n_z) & ((s > 0) | (d == 0)))
            def _():
                work(zz, d)

    def pass_on(s, kinds):
        for k in kinds:
            for d in range(2):
                zz = z - s if d == 0 else z + s
                src = zz * CORES + c

                @pl.when((zz >= 0) & (zz < n_z))
                def _():
                    hop(k, d, src, False).wait_recv()

                    @pl.when(can(d))
                    def _():
                        hop(k, d, src, False).start()

                    across(k, src, False).start()

    @pl.loop(0, n_z)
    def _(s):
        @pl.when(s > 0)
        def _():
            pass_on(s, (0, 1))

        both(s, forward_tokens)

        @pl.when(s > 0)
        def _():
            pass_on(s, (2,))

        both(s, forward_cots)

    piece, hpiece = width // n_d, hid // n_d
    chunk = max(piece, min(256, width))
    n_c = width // chunk
    hchunk, per = hid // n_c, chunk // piece
    half = width // 2

    def index(p, second, first):
        return second * n_b + first if p == 0 else first * n_b + second

    def first_of(p, j):
        return j % n_b if p == 0 else j // n_b

    def second_of(p, j):
        return j // n_b if p == 0 else j % n_b

    def mpiece(p, j):
        return MB.at[p, pl.ds(pl.multiple_of(j * piece, piece), piece)]

    def one(p, t, j):
        mine, there = first_of(p, dd), second_of(p, j)
        return pltpu.make_async_remote_copy(
            src_ref=mpiece(p, j) if t == 0 else DB.at[p, j],
            dst_ref=(MR if t == 0 else DR).at[p, mine, there],
            send_sem=one_s.at[p, t, j],
            recv_sem=one_r.at[p, t, mine, there],
            device_id={"dp": index(p, second_of(p, dd), first_of(p, j))},
            device_id_type=MESH,
        )

    def one_from(p, t, first, second):
        dst = (MR if t == 0 else DR).at[p, first, second]
        return pltpu.make_async_remote_copy(
            src_ref=dst, dst_ref=dst,
            send_sem=one_s.at[p, t, 0],
            recv_sem=one_r.at[p, t, first, second],
            device_id={"dp": index(p, second_of(p, dd), first)},
            device_id_type=MESH,
        )

    def two(p, t, second, slot):
        return pltpu.make_async_remote_copy(
            src_ref=(MP if t == 0 else DP).at[p, second],
            dst_ref=(MQ if t == 0 else DQ).at[p, slot],
            send_sem=two_s.at[p, t, second],
            recv_sem=two_r.at[p, t, slot],
            device_id={"dp": index(p, second, first_of(p, dd))},
            device_id_type=MESH,
        )

    @pl.loop(0, n_c)
    def _(i):
        if per == 1:
            step_a, step_b = n_a - 1 - i // n_b, n_b - 1 - i % n_b
            cc = ((dd // n_b + step_a) % n_a) * n_b + (dd % n_b + step_b) % n_b
        else:
            cc = (dd // per + 1 + i) % n_c
        at = pl.multiple_of(cc * chunk, chunk)
        hat = pl.multiple_of(cc * hchunk, hchunk)
        up_gate = jnp.dot(
            XT[pl.ds(at, chunk), :], GG[...], preferred_element_type=jnp.float32
        ).astype(jnp.bfloat16)
        for p in range(2):
            MB[p, pl.ds(at, chunk), :] = up_gate[:, p * hid : (p + 1) * hid]
        for t in range(2):
            if t == 1:
                down = jnp.dot(
                    HT[pl.ds(hat, hchunk), :], S[...], preferred_element_type=jnp.float32
                ).astype(jnp.bfloat16)
                for p in range(2):
                    for q in range(per):
                        DB[p, cc * per + q] = down[q * hpiece : (q + 1) * hpiece, p * half : (p + 1) * half]
            for p in range(2):
                for q in range(per):
                    j = cc * per + q

                    @pl.when(first_of(p, j) != first_of(p, dd))
                    def _():
                        one(p, t, j).start()

    def partial(p, t, second):
        first = first_of(p, dd)
        count = n_b if p == 0 else n_a
        j = index(p, second, first)
        total = (mpiece(p, j)[...] if t == 0 else DB[p, j]).astype(jnp.float32)
        for i in range(1, count):
            other = (first + i) % count
            one_from(p, t, other, second).wait_recv()
            total = total + (MR if t == 0 else DR)[p, other, second].astype(jnp.float32)
        return total

    for t in range(2):
        for p in range(2):
            count = n_a if p == 0 else n_b

            @pl.loop(1, count)
            def _(i):
                second = (second_of(p, dd) + i) % count
                (MP if t == 0 else DP)[p, second] = partial(p, t, second).astype(jnp.bfloat16)
                two(p, t, second, second_of(p, dd)).start()

    for t in range(2):
        for p in range(2):
            count = n_a if p == 0 else n_b
            mine = second_of(p, dd)
            total = partial(p, t, mine)
            for i in range(1, count):
                other = (mine + i) % count
                two(p, t, other, other).wait_recv()
                total = total + (MQ if t == 0 else DQ)[p, other].astype(jnp.float32)
            if t == 0:
                (out_g, out_u)[p][0] = total.astype(jnp.bfloat16)
            else:
                out_d[0, :, p * half : (p + 1) * half] = total.astype(jnp.bfloat16)

    for p in range(2):
        for t in range(2):
            @pl.loop(0, n_d)
            def _(j):
                @pl.when(first_of(p, j) != first_of(p, dd))
                def _():
                    one(p, t, j).wait_send()

            count = n_a if p == 0 else n_b

            @pl.loop(1, count)
            def _(i):
                two(p, t, (second_of(p, dd) + i) % count, second_of(p, dd)).wait_send()

    @pl.loop(0, n_z)
    def _(s):
        for k in range(3):
            for d in range(2):
                zz = z - s if d == 0 else z + s
                src = zz * CORES + c

                @pl.when((zz >= 0) & (zz < n_z) & can(d))
                def _():
                    hop(k, d, src, False).wait_send()

            across(k, s * CORES + c, False).wait_send()


def copy_out(*refs):
    n = len(refs) // 2
    copies = [pltpu.make_async_copy(refs[i], refs[n + i], refs[-1].at[i]) for i in range(n)]
    for copy in copies:
        copy.start()
    for copy in copies:
        copy.wait()


def write_out(arrays):
    anywhere = pl.BlockSpec(memory_space=pl.ANY)
    return pl.pallas_call(
        copy_out,
        out_shape=tuple(jax.ShapeDtypeStruct(x.shape, x.dtype) for x in arrays),
        in_specs=[anywhere] * len(arrays),
        out_specs=(anywhere,) * len(arrays),
        scratch_shapes=[pltpu.SemaphoreType.DMA((len(arrays),))],
        compiler_params=pltpu.CompilerParams(vmem_limit_bytes=1 << 20),
    )(*arrays)


def grid_kernel(
    n_e, cap, chunks,
    tok, cot, ids_in, probs_in, wg_in, wu_in, wd_in,
    out_g, out_u, out_d,
    ids, probs, TB, SEL, PSC, WG, WU, WD, E, WGG, WUU, WDD, SL, GH, XT, GG, HT,
    SM, SD, RM, RD, OM, OD, TM, TD, FM, FD, RL, *more,
):
    n_c = len(chunks)
    firsts = [i for i, (k, _, _) in enumerate(chunks) if k == 0]
    seconds = [i for i, (k, _, _) in enumerate(chunks) if k == 1]
    groups = [more[i * n_c : (i + 1) * n_c] for i in range(3)]
    B, C, RC = groups
    more = more[3 * n_c :]
    n_s = len(seconds)
    (
        small_l, own_l, wt_l, wt_s, wt_r, tab_s, tab_r, blk_s, blk_r, row_s, row_r,
        red_s, red_r, fin_s, fin_r, lent_r, lent_s,
    ) = more
    bf, f32 = jnp.bfloat16, jnp.float32
    rows, width = tok.shape
    hid = wg_in.shape[2]
    top = ids_in.shape[0]
    n_z = n_e // CORES
    me = lax.axis_index("expert")
    dd = lax.axis_index("dp")
    z, c = me // CORES, me % CORES
    y, x = dd // 2, dd % 2
    sib = z * CORES + (1 - c)
    g, f = jnp.where(c == 0, x, y), jnp.where(c == 0, y, x)
    across_x, across_y = y * 2 + (1 - x), (1 - y) * 2 + x

    def greet(where):
        pl.semaphore_signal(barrier, inc=1, device_id=where, device_id_type=MESH)

    barrier = pltpu.get_barrier_semaphore()
    for step in (-1, 1):
        @pl.when(jnp.logical_and(z + step >= 0, z + step < n_z))
        def _():
            greet({"expert": me + step * CORES, "dp": dd})
    greet({"expert": sib, "dp": dd})
    for other in (across_x, across_y):
        for core in range(CORES):
            greet({"expert": z * CORES + core, "dp": other})

    lends, lent = n_z >= 4, [0, 1]
    across = jnp.where(c == 0, across_y, across_x)
    at_end = (z == 0) | (z == n_z - 1)
    beside_end = (z == 1) | (z == n_z - 2)
    inner, outer = jnp.where(z == 0, 1, n_z - 2), jnp.where(z == 1, 0, n_z - 1)
    lenders = 0
    if lends:
        lenders = jnp.where(at_end, 1, 0)

        @pl.when(beside_end)
        def _():
            greet({"expert": outer * CORES + c, "dp": across})

    small = [
        pltpu.make_async_copy(ids_in, ids, small_l.at[0]),
        pltpu.make_async_copy(probs_in, probs, small_l.at[1]),
    ]
    for copy in small:
        copy.start()

    def own(i):
        k, at, w = chunks[i]
        return (tok, cot)[k].at[:, pl.ds(at, w)]

    def own_copy(i):
        return pltpu.make_async_copy(own(i), B[i].at[z], own_l.at[i])

    for i in range(n_c):
        own_copy(i).start()
    for copy in small:
        copy.wait()
    lanes = TB.shape[1] // 2
    erow = lax.broadcasted_iota(jnp.int32, (lanes, rows), 0)
    table = jnp.zeros((lanes, rows), f32)
    named = jnp.zeros((lanes, rows), f32)
    for k in range(top):
        hit = ids[k : k + 1, :] == erow
        table = table + jnp.where(hit, probs[k : k + 1, :], 0.0)
        named = named + jnp.where(hit, 1.0, 0.0)
    before = jnp.where(
        lax.broadcasted_iota(jnp.int32, (rows, rows), 0) < lax.broadcasted_iota(jnp.int32, (rows, rows), 1), 1.0, 0.0
    ).astype(bf)
    place = jnp.dot(named.astype(bf), before, preferred_element_type=f32)
    TB[z, :lanes] = table
    TB[z, lanes:] = jnp.where(named > 0.0, place, -1.0)

    pl.semaphore_wait(barrier, 5 + lenders + jnp.where(z > 0, 1, 0) + jnp.where(z < n_z - 1, 1, 0))

    def onward(d):
        return {"expert": me + jnp.where(d == 0, CORES, -CORES), "dp": dd}

    def can(d):
        return jnp.where(d == 0, n_z - 1 - z, z) > 0

    def plane(s, d):
        return jnp.where(d == 0, z - s, z + s)

    def tab_hop(d, src):
        return pltpu.make_async_remote_copy(
            src_ref=TB.at[src], dst_ref=TB.at[src], send_sem=tab_s.at[d, src], recv_sem=tab_r.at[src],
            device_id=onward(d), device_id_type=MESH,
        )

    def hop(i, d, src, mine):
        return pltpu.make_async_remote_copy(
            src_ref=own(i) if mine else B[i].at[src],
            dst_ref=B[i].at[src],
            send_sem=blk_s.at[i, d, src],
            recv_sem=blk_r.at[i, src],
            device_id=onward(d), device_id_type=MESH,
        )

    for d in range(2):
        @pl.when(can(d))
        def _():
            tab_hop(d, z).start()
    for i in range(n_c):
        for d in range(2):
            @pl.when(can(d))
            def _():
                hop(i, d, z, True).start()

    weights = ((wg_in, WG), (wu_in, WU), (wd_in, WD))

    def share(i):
        return pltpu.make_async_remote_copy(
            src_ref=weights[i][0].at[0], dst_ref=weights[i][1], send_sem=wt_s.at[i], recv_sem=wt_r.at[i],
            device_id={"expert": sib, "dp": dd}, device_id_type=MESH,
        )

    def keep(i):
        return pltpu.make_async_copy(weights[i][0].at[0], weights[i][1], wt_l.at[i])

    g_sib = jnp.where(c == 0, y, x)
    mine_here, mine_there = g == c, g_sib == c
    for i in range(3):
        @pl.when(mine_there)
        def _():
            share(i).start()

        @pl.when(mine_here)
        def _():
            keep(i).start()

    half, hh = hid // 2, hid // 8
    for slot in range(2):
        for t in range(2):
            j = lax.broadcasted_iota(jnp.int32, (hid, hid), 0) - t * half
            u = j + slot * hh
            for cut in range(1, 4):
                u = u + jnp.where(j >= cut * hh, hh, 0)
            inside = (j >= 0) & (j < half)
            there = lax.broadcasted_iota(jnp.int32, (hid, hid), 1)
            E[slot, t] = jnp.where(inside & (u == there), 1.0, 0.0).astype(bf)

    def row(i, src, to, part):
        where = (
            {"expert": sib, "dp": dd},
            {"expert": z * CORES, "dp": across_x},
            {"expert": z * CORES + 1, "dp": across_y},
        )[to]
        return pltpu.make_async_remote_copy(
            src_ref=C[i].at[src, (g_sib, 1 - x, 1 - y)[to]],
            dst_ref=RC[i].at[src, part],
            send_sem=row_s.at[i, src, to],
            recv_sem=row_r.at[i, src, part],
            device_id=where, device_id_type=MESH,
        )

    def each(s, work):
        @pl.loop(0, 2)
        def _(d):
            src = plane(s, d)

            @pl.when((src >= 0) & (src < n_z) & ((s > 0) | (d == 0)))
            def _():
                work(src, d)

    def tables(s):
        def work(src, d):
            @pl.when(s > 0)
            def _():
                tab_hop(d, src).wait_recv()

                @pl.when(can(d))
                def _():
                    tab_hop(d, src).start()

            slot = lax.broadcasted_iota(jnp.int32, (cap, rows), 0).astype(f32)
            for ee in range(2):
                hit = TB[src, pl.ds(lanes + z * CORES + ee, 1), :] == slot
                SEL[src, ee * cap : (ee + 1) * cap] = jnp.where(hit, 1.0, 0.0).astype(bf)
                weight = jnp.where(hit, TB[src, pl.ds(z * CORES + ee, 1), :], 0.0).sum(axis=1, keepdims=True)
                PSC[src, ee * cap : (ee + 1) * cap] = jnp.broadcast_to(weight, (cap, 128))

        each(s, work)

    def arrive(s, i):
        def work(src, d):
            @pl.when(s == 0)
            def _():
                own_copy(i).wait()

            @pl.when(s > 0)
            def _():
                hop(i, d, src, False).wait_recv()

                @pl.when(can(d))
                def _():
                    hop(i, d, src, False).start()

            picked = jnp.dot(SEL[src], B[i][src], preferred_element_type=f32)
            if chunks[i][0] == 1:
                picked = picked * PSC[src][:, :1]
            C[i][src] = picked.astype(bf).reshape(2, cap, chunks[i][2])
            row(i, src, 1, 2 + c).start()
            row(i, src, 2, 2 + c).start()
            row(i, src, 0, c).start()
            RC[i][src, c] = C[i][src, g]

        each(s, work)

    def collect(i, src):
        for part in (1 - c, 2, 3):
            row(i, src, 0, part).wait_recv()
        return RC[i][src].reshape(block, chunks[i][2])

    block = 4 * cap

    def base(src):
        return pl.multiple_of(src * block, block)

    def forward_tokens(s):
        def work(src, d):
            gate = jnp.zeros((block, hid), f32)
            up = jnp.zeros((block, hid), f32)
            for i in firsts:
                _, at, w = chunks[i]
                xs = collect(i, src)
                gate = gate + jnp.dot(xs, WGG[at : at + w], preferred_element_type=f32)
                up = up + jnp.dot(xs, WUU[at : at + w], preferred_element_type=f32)
                XT[at : at + w, pl.ds(base(src), block)] = xs.T
            sigma = jax.nn.sigmoid(gate)
            active = gate * sigma
            lane = lax.broadcasted_iota(jnp.int32, (block, hid), 1)
            SL[d] = jnp.where(lane < half, up * sigma * (1.0 + gate * (1.0 - sigma)), active)
            HT[:, pl.ds(base(src), block)] = (active * up).astype(bf).T[:half]

        each(s, work)

    def forward_cots(s, which):
        def work(src, d):
            total = jnp.zeros((block, hid), f32) if which[0] == seconds[0] else GH[d]
            for i in which:
                _, at, w = chunks[i]
                total = total + lax.dot_general(
                    collect(i, src), WDD[:, at : at + w], (((1,), (1,)), ((), ())), preferred_element_type=f32
                )
            if which[-1] == seconds[-1]:
                GG[pl.ds(base(src), block), :] = (total * SL[d]).astype(bf)
            else:
                GH[d] = total

        each(s, work)

    def prepare():
        for i in range(3):
            @pl.when(mine_here)
            def _():
                keep(i).wait()

            @pl.when(jnp.logical_not(mine_here))
            def _():
                share(i).wait_recv()
        spread = (E[c, 0].astype(f32) + E[c, 1].astype(f32)).astype(bf)
        for source, made in ((WG, WGG), (WU, WUU)):
            made[...] = lax.dot_general(
                source[...], spread, (((1,), (1,)), ((), ())), preferred_element_type=f32
            ).astype(bf)
        WDD[...] = jnp.dot(spread, WD[...], preferred_element_type=f32).astype(bf)

    @pl.loop(0, n_z - 1)
    def _(s):
        tables(s)
        for i in firsts:
            arrive(s, i)

        @pl.when(s > 0)
        def _():
            forward_cots(s - 1, seconds)

        for i in seconds[:-1]:
            arrive(s, i)

        @pl.when(s == 0)
        def _():
            prepare()

        forward_tokens(s)
        arrive(s, seconds[-1])

    last = n_z - 1
    tables(last)
    for i in firsts:
        arrive(last, i)
    forward_cots(last - 1, seconds)
    arrive(last, seconds[0])
    forward_tokens(last)
    for i in seconds[1:]:
        arrive(last, i)

    piece, hpiece = width // 4, half // 4
    part = piece // 4
    n_t = piece // part

    def quarter(ff, gg):
        return jnp.where(c == 0, ff * 2 + gg, gg * 2 + ff)

    def wide(j, t):
        at = pl.multiple_of(j * piece + t * part, part)
        return jnp.dot(XT[pl.ds(at, part), :], GG[...], preferred_element_type=f32)

    def deep(j, n):
        at = pl.multiple_of(j * hpiece, hpiece)
        i = seconds[n]
        return jnp.dot(
            HT[pl.ds(at, hpiece), :], RC[i][...].reshape(n_z * block, chunks[i][2]), preferred_element_type=f32
        )

    def columns(n):
        _, at, w = chunks[seconds[n]]
        return pl.ds(at, w)

    def spot(M, D, i, t):
        return M.at[i, pl.ds(t * part, part)] if t < n_t else D.at[i, :, columns(t - n_t)]

    def reduce_copy(i, t):
        return pltpu.make_async_remote_copy(
            src_ref=spot(SM, SD, i, t), dst_ref=spot(RM, RD, i, t),
            send_sem=red_s.at[i, t], recv_sem=red_r.at[i, t],
            device_id={"expert": me, "dp": quarter(1 - f, g)}, device_id_type=MESH,
        )

    def final_copy(i, t):
        return pltpu.make_async_remote_copy(
            src_ref=spot(TM, TD, i, t), dst_ref=spot(FM, FD, c, t),
            send_sem=fin_s.at[i, t], recv_sem=fin_r.at[c, t],
            device_id={"expert": z * CORES + g, "dp": quarter(f, 1 - g) if i == 0 else dd}, device_id_type=MESH,
        )

    def lend(t):
        return pltpu.make_async_remote_copy(
            src_ref=spot(SM, SD, 1, t), dst_ref=RL.at[pl.ds(t * part, part)],
            send_sem=red_s.at[1, t], recv_sem=lent_r.at[t],
            device_id={"expert": inner * CORES + c, "dp": across}, device_id_type=MESH,
        )

    def give_back(t):
        return pltpu.make_async_remote_copy(
            src_ref=RL.at[pl.ds(t * part, part)], dst_ref=spot(RM, RD, 1, t),
            send_sem=lent_s.at[t], recv_sem=red_r.at[1, t],
            device_id={"expert": outer * CORES + c, "dp": dd}, device_id_type=MESH,
        )

    def send_wide(i, t):
        j = quarter(1 - f, (1 - g) if i == 0 else g)
        SM[i, t * part : (t + 1) * part] = wide(j, t).astype(bf)
        if i == 0 or t not in lent or not lends:
            reduce_copy(i, t).start()
        else:
            @pl.when(at_end)
            def _():
                lend(t).start()

            @pl.when(jnp.logical_not(at_end))
            def _():
                reduce_copy(1, t).start()

    def send_deep(i, n):
        SD[i, :, columns(n)] = deep(quarter(1 - f, (1 - g) if i == 0 else g), n).astype(bf)
        reduce_copy(i, n_t + n).start()

    def keep_own(i, t):
        j = quarter(f, (1 - g) if i == 0 else g)
        if t < n_t:
            OM[i, t * part : (t + 1) * part] = wide(j, t)
        else:
            OD[i, :, columns(t - n_t)] = deep(j, t - n_t)

    def pass_total(i, t):
        reduce_copy(i, t).wait_recv()
        if t < n_t:
            at = slice(t * part, (t + 1) * part)
            TM[i, at] = (OM[i, at] + RM[i, at].astype(f32)).astype(bf)
        else:
            to = columns(t - n_t)
            TD[i, :, to] = (OD[i, :, to] + RD[i, :, to].astype(f32)).astype(bf)
        if i == 0:
            final_copy(0, t).start()
        else:
            @pl.when(g != c)
            def _():
                final_copy(1, t).start()

            @pl.when(g == c)
            def _():
                if t < n_t:
                    FM[c, at] = TM[1, at]
                else:
                    FD[c, :, to] = TD[1, :, to]

    forward_cots(last, seconds[:1])
    send_deep(0, 0)
    send_deep(1, 0)
    keep_own(0, 4)
    keep_own(1, 4)
    forward_cots(last, seconds[1:])
    send_wide(0, 0)
    send_wide(1, 0)
    send_wide(0, 1)
    send_wide(1, 1)
    send_wide(0, 2)
    send_wide(0, 3)
    send_deep(0, 1)
    send_deep(1, 1)
    send_wide(1, 2)
    send_wide(1, 3)
    keep_own(0, 0)
    pass_total(0, 4)
    keep_own(0, 1)
    pass_total(0, 0)
    keep_own(0, 2)
    pass_total(0, 1)
    keep_own(0, 3)
    pass_total(0, 2)
    pass_total(0, 3)
    keep_own(0, 5)
    pass_total(0, 5)
    pass_total(1, 4)
    keep_own(1, 0)
    keep_own(1, 1)
    keep_own(1, 2)
    keep_own(1, 3)
    keep_own(1, 5)
    pass_total(1, 0)
    pass_total(1, 1)
    pass_total(1, 2)
    pass_total(1, 3)
    pass_total(1, 5)

    def landed(slot, t):
        return pltpu.make_async_remote_copy(
            src_ref=spot(FM, FD, slot, t), dst_ref=spot(FM, FD, slot, t),
            send_sem=fin_s.at[0, t], recv_sem=fin_r.at[slot, t],
            device_id={"expert": sib, "dp": dd}, device_id_type=MESH,
        )

    for t in [*range(n_t, n_t + n_s - 1), *range(n_t), n_t + n_s - 1]:
        @pl.when(g != c)
        def _():
            landed(c, t).wait_recv()

        landed(1 - c, t).wait_recv()
        if t < n_t:
            at = slice(t * part, (t + 1) * part)
            for o, out in enumerate((out_g, out_u)):
                out[0, at] = (
                    jnp.dot(FM[0, at], E[0, o], preferred_element_type=f32)
                    + jnp.dot(FM[1, at], E[1, o], preferred_element_type=f32)
                ).astype(bf)
        else:
            for slot in range(2):
                to = columns(t - n_t)
                out_d[0, slot * hpiece : (slot + 1) * hpiece, to] = FD[slot, :, to]

    if lends:
        @pl.when(beside_end)
        def _():
            for t in lent:
                lend(t).wait_recv()
                give_back(t).start()
            for t in lent:
                give_back(t).wait_send()

    for i in range(2):
        for t in range(n_t + n_s):
            reduce_copy(i, t).wait_send()
            if i == 0:
                final_copy(0, t).wait_send()
            else:
                @pl.when(g != c)
                def _():
                    final_copy(1, t).wait_send()

    @pl.when(mine_there)
    def _():
        for i in range(3):
            share(i).wait_send()

    @pl.loop(0, n_z)
    def _(src):
        for d in range(2):
            @pl.when(can(d) & (jnp.where(d == 0, z - src, src - z) >= 0))
            def _():
                tab_hop(d, src).wait_send()
                for i in range(n_c):
                    hop(i, d, src, False).wait_send()
        for i in range(n_c):
            for to in range(3):
                row(i, src, to, 0).wait_send()


def grid_step(n_e, tokens, out_grad, expert_ids, gate_probs, w_gate, w_up, w_down):
    rows, width = tokens.shape
    hid = w_gate.shape[2]
    n_z, top = n_e // CORES, expert_ids.shape[1]
    cap = rows * (top + 1) // n_e
    lanes = -(-n_e // 8) * 8
    block, half = 4 * cap, hid // 2
    piece, hpiece = width // 4, hid // 8
    total = n_z * block
    chunks = []
    for k, cuts in ((0, XCUTS), (1, GCUTS)):
        at = 0
        for eighths in cuts:
            chunks.append((k, at * width // 8, eighths * width // 8))
            at += eighths
    n_c = len(chunks)
    bf, f32 = jnp.bfloat16, jnp.float32
    vmem = pl.BlockSpec(memory_space=pltpu.VMEM)
    hbm = pl.BlockSpec(memory_space=pltpu.HBM)
    dma = pltpu.SemaphoreType.DMA
    scratch = [
        (expert_ids.shape[::-1], expert_ids.dtype),
        (gate_probs.shape[::-1], gate_probs.dtype),
        ((n_z, 2 * lanes, rows), f32),
        ((n_z, 2 * cap, rows), bf),
        ((n_z, 2 * cap, 128), f32),
        ((width, hid), bf),
        ((width, hid), bf),
        ((hid, width), bf),
        ((2, 2, hid, hid), bf),
        ((width, hid), bf),
        ((width, hid), bf),
        ((hid, width), bf),
        ((2, block, hid), f32),
        ((2, block, hid), f32),
        ((width, total), bf),
        ((total, hid), bf),
        ((half, total), bf),
    ]
    scratch += [((2, piece, hid), bf), ((2, hpiece, width), bf)] * 2
    scratch += [((2, piece, hid), f32), ((2, hpiece, width), f32)]
    scratch += [((2, piece, hid), bf), ((2, hpiece, width), bf)] * 2
    scratch += [((piece, hid), bf)]
    sizes = [w for _, _, w in chunks]
    scratch += [((n_z, rows, w), bf) for w in sizes]
    scratch += [((n_z, 2, cap, w), bf) for w in sizes]
    scratch += [((n_z, 4, cap, w), bf) for w in sizes]
    held = sum(math.prod(shape) * jnp.dtype(kind).itemsize for shape, kind in scratch)
    args = (tokens, out_grad, expert_ids.T, gate_probs.T, w_gate, w_up, w_down)
    made = pl.pallas_call(
        functools.partial(grid_kernel, n_e, cap, chunks),
        out_shape=(
            jax.ShapeDtypeStruct((1, piece, hid), bf),
            jax.ShapeDtypeStruct((1, piece, hid), bf),
            jax.ShapeDtypeStruct((1, 2 * hpiece, width), bf),
        ),
        in_specs=[hbm] * 7,
        out_specs=(vmem, vmem, vmem),
        scratch_shapes=[pltpu.VMEM(shape, kind) for shape, kind in scratch]
        + [
            dma((2,)),
            dma((n_c,)),
            dma((3,)),
            dma((3,)),
            dma((3,)),
            dma((2, n_z)),
            dma((n_z,)),
            dma((n_c, 2, n_z)),
            dma((n_c, n_z)),
            dma((n_c, n_z, 3)),
            dma((n_c, n_z, 4)),
        ]
        + [dma((2, 6))] * 4
        + [dma((4,))] * 2,
        compiler_params=pltpu.CompilerParams(
            collective_id=1, has_side_effects=True, vmem_limit_bytes=held + (12 << 20)
        ),
    )(*(pltpu.with_memory_space_constraint(x, pltpu.HBM) for x in args))
    return write_out(made)


def solution(mesh):
    n_e, n_d = mesh.shape["expert"], mesh.shape["dp"]
    n_b = max(b for b in range(1, n_d + 1) if n_d % b == 0 and b * b <= n_d)
    n_a = n_d // n_b

    def step(tokens, out_grad, expert_ids, gate_probs, w_gate, w_up, w_down):
        rows, width = tokens.shape
        hid = w_gate.shape[2]
        total = n_e * rows
        lanes = -(-n_e // 8) * 8
        bf, f32 = jnp.bfloat16, jnp.float32
        vmem = pl.BlockSpec(memory_space=pltpu.VMEM)
        hbm = pl.BlockSpec(memory_space=pltpu.HBM)
        piece, hpiece = width // n_d, hid // n_d
        dma = pltpu.SemaphoreType.DMA
        scratch = [
            (expert_ids.shape[::-1], expert_ids.dtype),
            (gate_probs.shape[::-1], gate_probs.dtype),
            ((n_e, rows, width), bf),
            ((n_e, rows, width), bf),
            ((n_e, lanes, rows), f32),
            ((width, hid), bf),
            ((width, hid), bf),
            ((hid, width), bf),
            ((2, CORES * rows, 2 * hid), f32),
            ((width, total), bf),
            ((hid, total), bf),
            ((total, 2 * hid), bf),
            ((total, width), bf),
            ((2, width, hid), bf),
            ((2, n_d, hpiece, width // 2), bf),
            ((2, n_a, n_a, piece, hid), bf),
            ((2, n_a, n_a, hpiece, width // 2), bf),
            ((2, n_a, piece, hid), bf),
            ((2, n_a, hpiece, width // 2), bf),
            ((2, n_a, piece, hid), bf),
            ((2, n_a, hpiece, width // 2), bf),
        ]
        held = sum(math.prod(shape) * jnp.dtype(kind).itemsize for shape, kind in scratch)
        args = (tokens, out_grad, expert_ids.T, gate_probs.T, w_gate, w_up, w_down)
        made = pl.pallas_call(
            functools.partial(kernel, n_e, n_a, n_b),
            out_shape=(
                jax.ShapeDtypeStruct((1, piece, hid), bf),
                jax.ShapeDtypeStruct((1, piece, hid), bf),
                jax.ShapeDtypeStruct((1, hpiece, width), bf),
            ),
            in_specs=[hbm] * 7,
            out_specs=(vmem, vmem, vmem),
            scratch_shapes=[pltpu.VMEM(shape, kind) for shape, kind in scratch]
            + [
                dma((7,)),
                dma((3, 2, n_e)),
                dma((3, n_e)),
                dma((3, n_e)),
                dma((2, 2, n_d)),
                dma((2, 2, n_a, n_a)),
                dma((2, 2, n_a)),
                dma((2, 2, n_a)),
            ],
            compiler_params=pltpu.CompilerParams(
                collective_id=0, has_side_effects=True, vmem_limit_bytes=held + (10 << 20)
            ),
        )(*(pltpu.with_memory_space_constraint(x, pltpu.HBM) for x in args))
        return write_out(made)

    if n_a == 2 and n_b == 2:
        step = functools.partial(grid_step, n_e)
    spread = P(("expert", "dp"), None)
    return jax.shard_map(
        step,
        mesh=mesh,
        in_specs=(spread, spread, spread, spread) + (P("expert", None, None),) * 3,
        out_specs=(P("expert", "dp", None),) * 3,
        check_vma=False,
    )
```

```python
import functools
import math

import jax
import jax.numpy as jnp
from jax import lax
from jax.experimental import pallas as pl
from jax.experimental.pallas import tpu as pltpu
from jax.sharding import PartitionSpec as P

MESH = pl.DeviceIdType.MESH
CORES = 2
XCUTS, GCUTS = (8,), (4, 4)


def kernel(
    n_e, n_a, n_b,
    tok, cot, ids_in, probs_in, wg_in, wu_in, wd_in,
    out_g, out_u, out_d,
    ids, probs, X, G, PT, WG, WU, WD, GU, XT, HT, GG, S, MB, DB, MR, DR, MP, DP, MQ, DQ,
    lsem, chain_s, sib_s, blk_r, one_s, one_r, two_s, two_r,
):
    n_d = n_a * n_b
    rows, width = tok.shape
    hid = wg_in.shape[2]
    top = ids_in.shape[0]
    n_z = n_e // CORES
    me = lax.axis_index("expert")
    dd = lax.axis_index("dp")
    z, c = me // CORES, me % CORES
    sib = z * CORES + (1 - c)

    barrier = pltpu.get_barrier_semaphore()
    for step in (-1, 1):
        @pl.when(jnp.logical_and(z + step >= 0, z + step < n_z))
        def _():
            pl.semaphore_signal(barrier, inc=1, device_id={"expert": me + step * CORES}, device_id_type=MESH)
    pl.semaphore_signal(barrier, inc=1, device_id={"expert": sib}, device_id_type=MESH)
    for i in range(1, n_a):
        pl.semaphore_signal(barrier, inc=1, device_id={"dp": ((dd // n_b + i) % n_a) * n_b + dd % n_b}, device_id_type=MESH)
    for i in range(1, n_b):
        pl.semaphore_signal(barrier, inc=1, device_id={"dp": dd // n_b * n_b + (dd % n_b + i) % n_b}, device_id_type=MESH)
    small = [
        pltpu.make_async_copy(ids_in, ids, lsem.at[5]),
        pltpu.make_async_copy(probs_in, probs, lsem.at[6]),
    ]
    for copy in small:
        copy.start()
    for copy in small:
        copy.wait()
    erow = lax.broadcasted_iota(jnp.int32, PT.shape[1:], 0)
    table = jnp.zeros(PT.shape[1:], jnp.float32)
    for k in range(top):
        table = table + jnp.where(ids[k : k + 1, :] == erow, probs[k : k + 1, :], 0.0)
    PT[me] = table

    arrivals = n_a + n_b - 1 + jnp.where(z > 0, 1, 0) + jnp.where(z < n_z - 1, 1, 0)
    pl.semaphore_wait(barrier, arrivals)

    full = (PT, X, G)
    own = (PT.at[me], tok, cot)

    def hop(k, d, src, mine):
        there = me + (CORES if d == 0 else -CORES)
        return pltpu.make_async_remote_copy(
            src_ref=own[k] if mine else full[k].at[src],
            dst_ref=full[k].at[src],
            send_sem=chain_s.at[k, d, src],
            recv_sem=blk_r.at[k, src],
            device_id={"expert": there},
            device_id_type=MESH,
        )

    def across(k, src, mine):
        return pltpu.make_async_remote_copy(
            src_ref=own[k] if mine else full[k].at[src],
            dst_ref=full[k].at[src],
            send_sem=sib_s.at[k, src],
            recv_sem=blk_r.at[k, src],
            device_id={"expert": sib},
            device_id_type=MESH,
        )

    def can(d):
        return z < n_z - 1 if d == 0 else z > 0

    for k in range(3):
        for d in range(2):
            @pl.when(can(d))
            def _():
                hop(k, d, me, True).start()
        across(k, me, True).start()
    local = [
        pltpu.make_async_copy(tok, X.at[me], lsem.at[0]),
        pltpu.make_async_copy(cot, G.at[me], lsem.at[1]),
        pltpu.make_async_copy(wg_in.at[0], WG, lsem.at[2]),
        pltpu.make_async_copy(wu_in.at[0], WU, lsem.at[3]),
        pltpu.make_async_copy(wd_in.at[0], WD, lsem.at[4]),
    ]
    for copy in local:
        copy.start()
    for copy in local:
        copy.wait()

    pair = CORES * rows

    def base(zz):
        return pl.multiple_of(zz * pair, pair)

    def forward_tokens(zz, d):
        for k in range(2):
            across(k, zz * CORES + (1 - c), False).wait_recv()
        x = X[pl.ds(zz * CORES, CORES)].reshape(pair, width)
        GU[d, :, :hid] = jnp.dot(x, WG[...], preferred_element_type=jnp.float32)
        GU[d, :, hid:] = jnp.dot(x, WU[...], preferred_element_type=jnp.float32)
        XT[:, pl.ds(base(zz), pair)] = x.T

    def forward_cots(zz, d):
        across(2, zz * CORES + (1 - c), False).wait_recv()
        at = base(zz)
        parts = []
        for h in range(CORES):
            p = PT[zz * CORES + h, pl.ds(me, 1), :]
            p = jnp.broadcast_to(p, (rows, rows)).T[:, :1]
            parts.append((p * G[zz * CORES + h].astype(jnp.float32)).astype(jnp.bfloat16))
        scaled = jnp.concatenate(parts, axis=0)
        S[pl.ds(at, pair), :] = scaled
        gh = lax.dot_general(scaled, WD[...], (((1,), (1,)), ((), ())), preferred_element_type=jnp.float32)
        gate, up = GU[d, :, :hid], GU[d, :, hid:]
        sigma = jax.nn.sigmoid(gate)
        active = gate * sigma
        GG[pl.ds(at, pair), :hid] = (gh * up * sigma * (1.0 + gate * (1.0 - sigma))).astype(jnp.bfloat16)
        GG[pl.ds(at, pair), hid:] = (gh * active).astype(jnp.bfloat16)
        HT[:, pl.ds(at, pair)] = (active * up).astype(jnp.bfloat16).T

    def both(s, work):
        @pl.loop(0, 2)
        def _(d):
            zz = jnp.where(d == 0, z - s, z + s)

            @pl.when((zz >= 0) & (zz < n_z) & ((s > 0) | (d == 0)))
            def _():
                work(zz, d)

    def pass_on(s, kinds):
        for k in kinds:
            for d in range(2):
                zz = z - s if d == 0 else z + s
                src = zz * CORES + c

                @pl.when((zz >= 0) & (zz < n_z))
                def _():
                    hop(k, d, src, False).wait_recv()

                    @pl.when(can(d))
                    def _():
                        hop(k, d, src, False).start()

                    across(k, src, False).start()

    @pl.loop(0, n_z)
    def _(s):
        @pl.when(s > 0)
        def _():
            pass_on(s, (0, 1))

        both(s, forward_tokens)

        @pl.when(s > 0)
        def _():
            pass_on(s, (2,))

        both(s, forward_cots)

    piece, hpiece = width // n_d, hid // n_d
    chunk = max(piece, min(256, width))
    n_c = width // chunk
    hchunk, per = hid // n_c, chunk // piece
    half = width // 2

    def index(p, second, first):
        return second * n_b + first if p == 0 else first * n_b + second

    def first_of(p, j):
        return j % n_b if p == 0 else j // n_b

    def second_of(p, j):
        return j // n_b if p == 0 else j % n_b

    def mpiece(p, j):
        return MB.at[p, pl.ds(pl.multiple_of(j * piece, piece), piece)]

    def one(p, t, j):
        mine, there = first_of(p, dd), second_of(p, j)
        return pltpu.make_async_remote_copy(
            src_ref=mpiece(p, j) if t == 0 else DB.at[p, j],
            dst_ref=(MR if t == 0 else DR).at[p, mine, there],
            send_sem=one_s.at[p, t, j],
            recv_sem=one_r.at[p, t, mine, there],
            device_id={"dp": index(p, second_of(p, dd), first_of(p, j))},
            device_id_type=MESH,
        )

    def one_from(p, t, first, second):
        dst = (MR if t == 0 else DR).at[p, first, second]
        return pltpu.make_async_remote_copy(
            src_ref=dst, dst_ref=dst,
            send_sem=one_s.at[p, t, 0],
            recv_sem=one_r.at[p, t, first, second],
            device_id={"dp": index(p, second_of(p, dd), first)},
            device_id_type=MESH,
        )

    def two(p, t, second, slot):
        return pltpu.make_async_remote_copy(
            src_ref=(MP if t == 0 else DP).at[p, second],
            dst_ref=(MQ if t == 0 else DQ).at[p, slot],
            send_sem=two_s.at[p, t, second],
            recv_sem=two_r.at[p, t, slot],
            device_id={"dp": index(p, second, first_of(p, dd))},
            device_id_type=MESH,
        )

    @pl.loop(0, n_c)
    def _(i):
        if per == 1:
            step_a, step_b = n_a - 1 - i // n_b, n_b - 1 - i % n_b
            cc = ((dd // n_b + step_a) % n_a) * n_b + (dd % n_b + step_b) % n_b
        else:
            cc = (dd // per + 1 + i) % n_c
        at = pl.multiple_of(cc * chunk, chunk)
        hat = pl.multiple_of(cc * hchunk, hchunk)
        up_gate = jnp.dot(
            XT[pl.ds(at, chunk), :], GG[...], preferred_element_type=jnp.float32
        ).astype(jnp.bfloat16)
        for p in range(2):
            MB[p, pl.ds(at, chunk), :] = up_gate[:, p * hid : (p + 1) * hid]
        for t in range(2):
            if t == 1:
                down = jnp.dot(
                    HT[pl.ds(hat, hchunk), :], S[...], preferred_element_type=jnp.float32
                ).astype(jnp.bfloat16)
                for p in range(2):
                    for q in range(per):
                        DB[p, cc * per + q] = down[q * hpiece : (q + 1) * hpiece, p * half : (p + 1) * half]
            for p in range(2):
                for q in range(per):
                    j = cc * per + q

                    @pl.when(first_of(p, j) != first_of(p, dd))
                    def _():
                        one(p, t, j).start()

    def partial(p, t, second):
        first = first_of(p, dd)
        count = n_b if p == 0 else n_a
        j = index(p, second, first)
        total = (mpiece(p, j)[...] if t == 0 else DB[p, j]).astype(jnp.float32)
        for i in range(1, count):
            other = (first + i) % count
            one_from(p, t, other, second).wait_recv()
            total = total + (MR if t == 0 else DR)[p, other, second].astype(jnp.float32)
        return total

    for t in range(2):
        for p in range(2):
            count = n_a if p == 0 else n_b

            @pl.loop(1, count)
            def _(i):
                second = (second_of(p, dd) + i) % count
                (MP if t == 0 else DP)[p, second] = partial(p, t, second).astype(jnp.bfloat16)
                two(p, t, second, second_of(p, dd)).start()

    for t in range(2):
        for p in range(2):
            count = n_a if p == 0 else n_b
            mine = second_of(p, dd)
            total = partial(p, t, mine)
            for i in range(1, count):
                other = (mine + i) % count
                two(p, t, other, other).wait_recv()
                total = total + (MQ if t == 0 else DQ)[p, other].astype(jnp.float32)
            if t == 0:
                (out_g, out_u)[p][0] = total.astype(jnp.bfloat16)
            else:
                out_d[0, :, p * half : (p + 1) * half] = total.astype(jnp.bfloat16)

    for p in range(2):
        for t in range(2):
            @pl.loop(0, n_d)
            def _(j):
                @pl.when(first_of(p, j) != first_of(p, dd))
                def _():
                    one(p, t, j).wait_send()

            count = n_a if p == 0 else n_b

            @pl.loop(1, count)
            def _(i):
                two(p, t, (second_of(p, dd) + i) % count, second_of(p, dd)).wait_send()

    @pl.loop(0, n_z)
    def _(s):
        for k in range(3):
            for d in range(2):
                zz = z - s if d == 0 else z + s
                src = zz * CORES + c

                @pl.when((zz >= 0) & (zz < n_z) & can(d))
                def _():
                    hop(k, d, src, False).wait_send()

            across(k, s * CORES + c, False).wait_send()


def copy_out(*refs):
    n = len(refs) // 2
    copies = [pltpu.make_async_copy(refs[i], refs[n + i], refs[-1].at[i]) for i in range(n)]
    for copy in copies:
        copy.start()
    for copy in copies:
        copy.wait()


def write_out(arrays):
    anywhere = pl.BlockSpec(memory_space=pl.ANY)
    return pl.pallas_call(
        copy_out,
        out_shape=tuple(jax.ShapeDtypeStruct(x.shape, x.dtype) for x in arrays),
        in_specs=[anywhere] * len(arrays),
        out_specs=(anywhere,) * len(arrays),
        scratch_shapes=[pltpu.SemaphoreType.DMA((len(arrays),))],
        compiler_params=pltpu.CompilerParams(vmem_limit_bytes=1 << 20),
    )(*arrays)


def grid_kernel(
    n_e, cap, chunks,
    tok, cot, ids_in, probs_in, wg_in, wu_in, wd_in,
    out_g, out_u, out_d,
    ids, probs, TB, SEL, PSC, WG, WU, WD, E, WGG, WUU, WDD, SL, GH, XT, GG, HT,
    SM, SD, RM, RD, OM, OD, TM, TD, FM, FD, RL, *more,
):
    n_c = len(chunks)
    firsts = [i for i, (k, _, _) in enumerate(chunks) if k == 0]
    seconds = [i for i, (k, _, _) in enumerate(chunks) if k == 1]
    groups = [more[i * n_c : (i + 1) * n_c] for i in range(3)]
    B, C, RC = groups
    more = more[3 * n_c :]
    n_s = len(seconds)
    (
        small_l, own_l, wt_l, wt_s, wt_r, tab_s, tab_r, blk_s, blk_r, row_s, row_r,
        red_s, red_r, fin_s, fin_r, lent_r, lent_s,
    ) = more
    bf, f32 = jnp.bfloat16, jnp.float32
    rows, width = tok.shape
    hid = wg_in.shape[2]
    top = ids_in.shape[0]
    n_z = n_e // CORES
    me = lax.axis_index("expert")
    dd = lax.axis_index("dp")
    z, c = me // CORES, me % CORES
    y, x = dd // 2, dd % 2
    sib = z * CORES + (1 - c)
    g, f = jnp.where(c == 0, x, y), jnp.where(c == 0, y, x)
    across_x, across_y = y * 2 + (1 - x), (1 - y) * 2 + x

    def greet(where):
        pl.semaphore_signal(barrier, inc=1, device_id=where, device_id_type=MESH)

    barrier = pltpu.get_barrier_semaphore()
    for step in (-1, 1):
        @pl.when(jnp.logical_and(z + step >= 0, z + step < n_z))
        def _():
            greet({"expert": me + step * CORES, "dp": dd})
    greet({"expert": sib, "dp": dd})
    for other in (across_x, across_y):
        for core in range(CORES):
            greet({"expert": z * CORES + core, "dp": other})

    lends, lent = n_z >= 4, [0, 1]
    across = jnp.where(c == 0, across_y, across_x)
    at_end = (z == 0) | (z == n_z - 1)
    beside_end = (z == 1) | (z == n_z - 2)
    inner, outer = jnp.where(z == 0, 1, n_z - 2), jnp.where(z == 1, 0, n_z - 1)
    lenders = 0
    if lends:
        lenders = jnp.where(at_end, 1, 0)

        @pl.when(beside_end)
        def _():
            greet({"expert": outer * CORES + c, "dp": across})

    small = [
        pltpu.make_async_copy(ids_in, ids, small_l.at[0]),
        pltpu.make_async_copy(probs_in, probs, small_l.at[1]),
    ]
    for copy in small:
        copy.start()

    def own(i):
        k, at, w = chunks[i]
        return (tok, cot)[k].at[:, pl.ds(at, w)]

    def own_copy(i):
        return pltpu.make_async_copy(own(i), B[i].at[z], own_l.at[i])

    for i in range(n_c):
        own_copy(i).start()
    for copy in small:
        copy.wait()
    lanes = TB.shape[1] // 2
    erow = lax.broadcasted_iota(jnp.int32, (lanes, rows), 0)
    table = jnp.zeros((lanes, rows), f32)
    named = jnp.zeros((lanes, rows), f32)
    for k in range(top):
        hit = ids[k : k + 1, :] == erow
        table = table + jnp.where(hit, probs[k : k + 1, :], 0.0)
        named = named + jnp.where(hit, 1.0, 0.0)
    before = jnp.where(
        lax.broadcasted_iota(jnp.int32, (rows, rows), 0) < lax.broadcasted_iota(jnp.int32, (rows, rows), 1), 1.0, 0.0
    ).astype(bf)
    place = jnp.dot(named.astype(bf), before, preferred_element_type=f32)
    TB[z, :lanes] = table
    TB[z, lanes:] = jnp.where(named > 0.0, place, -1.0)

    pl.semaphore_wait(barrier, 5 + lenders + jnp.where(z > 0, 1, 0) + jnp.where(z < n_z - 1, 1, 0))

    def onward(d):
        return {"expert": me + jnp.where(d == 0, CORES, -CORES), "dp": dd}

    def can(d):
        return jnp.where(d == 0, n_z - 1 - z, z) > 0

    def plane(s, d):
        return jnp.where(d == 0, z - s, z + s)

    def tab_hop(d, src):
        return pltpu.make_async_remote_copy(
            src_ref=TB.at[src], dst_ref=TB.at[src], send_sem=tab_s.at[d, src], recv_sem=tab_r.at[src],
            device_id=onward(d), device_id_type=MESH,
        )

    def hop(i, d, src, mine):
        return pltpu.make_async_remote_copy(
            src_ref=own(i) if mine else B[i].at[src],
            dst_ref=B[i].at[src],
            send_sem=blk_s.at[i, d, src],
            recv_sem=blk_r.at[i, src],
            device_id=onward(d), device_id_type=MESH,
        )

    for d in range(2):
        @pl.when(can(d))
        def _():
            tab_hop(d, z).start()
    for i in range(n_c):
        for d in range(2):
            @pl.when(can(d))
            def _():
                hop(i, d, z, True).start()

    weights = ((wg_in, WG), (wu_in, WU), (wd_in, WD))

    def share(i):
        return pltpu.make_async_remote_copy(
            src_ref=weights[i][0].at[0], dst_ref=weights[i][1], send_sem=wt_s.at[i], recv_sem=wt_r.at[i],
            device_id={"expert": sib, "dp": dd}, device_id_type=MESH,
        )

    def keep(i):
        return pltpu.make_async_copy(weights[i][0].at[0], weights[i][1], wt_l.at[i])

    g_sib = jnp.where(c == 0, y, x)
    mine_here, mine_there = g == c, g_sib == c
    for i in range(3):
        @pl.when(mine_there)
        def _():
            share(i).start()

        @pl.when(mine_here)
        def _():
            keep(i).start()

    half, hh = hid // 2, hid // 8
    for slot in range(2):
        for t in range(2):
            j = lax.broadcasted_iota(jnp.int32, (hid, hid), 0) - t * half
            u = j + slot * hh
            for cut in range(1, 4):
                u = u + jnp.where(j >= cut * hh, hh, 0)
            inside = (j >= 0) & (j < half)
            there = lax.broadcasted_iota(jnp.int32, (hid, hid), 1)
            E[slot, t] = jnp.where(inside & (u == there), 1.0, 0.0).astype(bf)

    def row(i, src, to, part):
        where = (
            {"expert": sib, "dp": dd},
            {"expert": z * CORES, "dp": across_x},
            {"expert": z * CORES + 1, "dp": across_y},
        )[to]
        return pltpu.make_async_remote_copy(
            src_ref=C[i].at[src, (g_sib, 1 - x, 1 - y)[to]],
            dst_ref=RC[i].at[src, part],
            send_sem=row_s.at[i, src, to],
            recv_sem=row_r.at[i, src, part],
            device_id=where, device_id_type=MESH,
        )

    def each(s, work):
        @pl.loop(0, 2)
        def _(d):
            src = plane(s, d)

            @pl.when((src >= 0) & (src < n_z) & ((s > 0) | (d == 0)))
            def _():
                work(src, d)

    def tables(s):
        def work(src, d):
            @pl.when(s > 0)
            def _():
                tab_hop(d, src).wait_recv()

                @pl.when(can(d))
                def _():
                    tab_hop(d, src).start()

            slot = lax.broadcasted_iota(jnp.int32, (cap, rows), 0).astype(f32)
            for ee in range(2):
                hit = TB[src, pl.ds(lanes + z * CORES + ee, 1), :] == slot
                SEL[src, ee * cap : (ee + 1) * cap] = jnp.where(hit, 1.0, 0.0).astype(bf)
                weight = jnp.where(hit, TB[src, pl.ds(z * CORES + ee, 1), :], 0.0).sum(axis=1, keepdims=True)
                PSC[src, ee * cap : (ee + 1) * cap] = jnp.broadcast_to(weight, (cap, 128))

        each(s, work)

    def arrive(s, i):
        def work(src, d):
            @pl.when(s == 0)
            def _():
                own_copy(i).wait()

            @pl.when(s > 0)
            def _():
                hop(i, d, src, False).wait_recv()

                @pl.when(can(d))
                def _():
                    hop(i, d, src, False).start()

            picked = jnp.dot(SEL[src], B[i][src], preferred_element_type=f32)
            if chunks[i][0] == 1:
                picked = picked * PSC[src][:, :1]
            C[i][src] = picked.astype(bf).reshape(2, cap, chunks[i][2])
            row(i, src, 1, 2 + c).start()
            row(i, src, 2, 2 + c).start()
            row(i, src, 0, c).start()
            RC[i][src, c] = C[i][src, g]

        each(s, work)

    def collect(i, src):
        for part in (1 - c, 2, 3):
            row(i, src, 0, part).wait_recv()
        return RC[i][src].reshape(block, chunks[i][2])

    block = 4 * cap

    def base(src):
        return pl.multiple_of(src * block, block)

    def forward_tokens(s):
        def work(src, d):
            gate = jnp.zeros((block, hid), f32)
            up = jnp.zeros((block, hid), f32)
            for i in firsts:
                _, at, w = chunks[i]
                xs = collect(i, src)
                gate = gate + jnp.dot(xs, WGG[at : at + w], preferred_element_type=f32)
                up = up + jnp.dot(xs, WUU[at : at + w], preferred_element_type=f32)
                XT[at : at + w, pl.ds(base(src), block)] = xs.T
            sigma = jax.nn.sigmoid(gate)
            active = gate * sigma
            lane = lax.broadcasted_iota(jnp.int32, (block, hid), 1)
            SL[d] = jnp.where(lane < half, up * sigma * (1.0 + gate * (1.0 - sigma)), active)
            HT[:, pl.ds(base(src), block)] = (active * up).astype(bf).T[:half]

        each(s, work)

    def forward_cots(s, which):
        def work(src, d):
            total = jnp.zeros((block, hid), f32) if which[0] == seconds[0] else GH[d]
            for i in which:
                _, at, w = chunks[i]
                total = total + lax.dot_general(
                    collect(i, src), WDD[:, at : at + w], (((1,), (1,)), ((), ())), preferred_element_type=f32
                )
            if which[-1] == seconds[-1]:
                GG[pl.ds(base(src), block), :] = (total * SL[d]).astype(bf)
            else:
                GH[d] = total

        each(s, work)

    def prepare():
        for i in range(3):
            @pl.when(mine_here)
            def _():
                keep(i).wait()

            @pl.when(jnp.logical_not(mine_here))
            def _():
                share(i).wait_recv()
        spread = (E[c, 0].astype(f32) + E[c, 1].astype(f32)).astype(bf)
        for source, made in ((WG, WGG), (WU, WUU)):
            made[...] = lax.dot_general(
                source[...], spread, (((1,), (1,)), ((), ())), preferred_element_type=f32
            ).astype(bf)
        WDD[...] = jnp.dot(spread, WD[...], preferred_element_type=f32).astype(bf)

    @pl.loop(0, n_z - 1)
    def _(s):
        tables(s)
        for i in firsts:
            arrive(s, i)

        @pl.when(s > 0)
        def _():
            forward_cots(s - 1, seconds)

        for i in seconds[:-1]:
            arrive(s, i)

        @pl.when(s == 0)
        def _():
            prepare()

        forward_tokens(s)
        arrive(s, seconds[-1])

    last = n_z - 1
    tables(last)
    for i in firsts:
        arrive(last, i)
    forward_cots(last - 1, seconds)
    arrive(last, seconds[0])
    forward_tokens(last)
    for i in seconds[1:]:
        arrive(last, i)

    piece, hpiece = width // 4, half // 4
    part = piece // 4
    n_t = piece // part

    def quarter(ff, gg):
        return jnp.where(c == 0, ff * 2 + gg, gg * 2 + ff)

    def wide(j, t):
        at = pl.multiple_of(j * piece + t * part, part)
        return jnp.dot(XT[pl.ds(at, part), :], GG[...], preferred_element_type=f32)

    def deep(j, n):
        at = pl.multiple_of(j * hpiece, hpiece)
        i = seconds[n]
        return jnp.dot(
            HT[pl.ds(at, hpiece), :], RC[i][...].reshape(n_z * block, chunks[i][2]), preferred_element_type=f32
        )

    def columns(n):
        _, at, w = chunks[seconds[n]]
        return pl.ds(at, w)

    def spot(M, D, i, t):
        return M.at[i, pl.ds(t * part, part)] if t < n_t else D.at[i, :, columns(t - n_t)]

    def reduce_copy(i, t):
        return pltpu.make_async_remote_copy(
            src_ref=spot(SM, SD, i, t), dst_ref=spot(RM, RD, i, t),
            send_sem=red_s.at[i, t], recv_sem=red_r.at[i, t],
            device_id={"expert": me, "dp": quarter(1 - f, g)}, device_id_type=MESH,
        )

    def final_copy(i, t):
        return pltpu.make_async_remote_copy(
            src_ref=spot(TM, TD, i, t), dst_ref=spot(FM, FD, c, t),
            send_sem=fin_s.at[i, t], recv_sem=fin_r.at[c, t],
            device_id={"expert": z * CORES + g, "dp": quarter(f, 1 - g) if i == 0 else dd}, device_id_type=MESH,
        )

    def lend(t):
        return pltpu.make_async_remote_copy(
            src_ref=spot(SM, SD, 1, t), dst_ref=RL.at[pl.ds(t * part, part)],
            send_sem=red_s.at[1, t], recv_sem=lent_r.at[t],
            device_id={"expert": inner * CORES + c, "dp": across}, device_id_type=MESH,
        )

    def give_back(t):
        return pltpu.make_async_remote_copy(
            src_ref=RL.at[pl.ds(t * part, part)], dst_ref=spot(RM, RD, 1, t),
            send_sem=lent_s.at[t], recv_sem=red_r.at[1, t],
            device_id={"expert": outer * CORES + c, "dp": dd}, device_id_type=MESH,
        )

    def send_wide(i, t):
        j = quarter(1 - f, (1 - g) if i == 0 else g)
        SM[i, t * part : (t + 1) * part] = wide(j, t).astype(bf)
        if i == 0 or t not in lent or not lends:
            reduce_copy(i, t).start()
        else:
            @pl.when(at_end)
            def _():
                lend(t).start()

            @pl.when(jnp.logical_not(at_end))
            def _():
                reduce_copy(1, t).start()

    def send_deep(i, n):
        SD[i, :, columns(n)] = deep(quarter(1 - f, (1 - g) if i == 0 else g), n).astype(bf)
        reduce_copy(i, n_t + n).start()

    def keep_own(i, t):
        j = quarter(f, (1 - g) if i == 0 else g)
        if t < n_t:
            OM[i, t * part : (t + 1) * part] = wide(j, t)
        else:
            OD[i, :, columns(t - n_t)] = deep(j, t - n_t)

    def pass_total(i, t):
        reduce_copy(i, t).wait_recv()
        if t < n_t:
            at = slice(t * part, (t + 1) * part)
            TM[i, at] = (OM[i, at] + RM[i, at].astype(f32)).astype(bf)
        else:
            to = columns(t - n_t)
            TD[i, :, to] = (OD[i, :, to] + RD[i, :, to].astype(f32)).astype(bf)
        if i == 0:
            final_copy(0, t).start()
        else:
            @pl.when(g != c)
            def _():
                final_copy(1, t).start()

            @pl.when(g == c)
            def _():
                if t < n_t:
                    FM[c, at] = TM[1, at]
                else:
                    FD[c, :, to] = TD[1, :, to]

    forward_cots(last, seconds[:1])
    send_deep(0, 0)
    send_deep(1, 0)
    keep_own(0, 4)
    forward_cots(last, seconds[1:])
    send_wide(0, 0)
    send_wide(1, 0)
    send_wide(0, 1)
    send_wide(1, 1)
    send_wide(0, 2)
    send_wide(0, 3)
    send_deep(0, 1)
    send_deep(1, 1)
    send_wide(1, 2)
    send_wide(1, 3)
    keep_own(0, 0)
    pass_total(0, 4)
    keep_own(0, 1)
    pass_total(0, 0)
    keep_own(0, 2)
    pass_total(0, 1)
    keep_own(0, 3)
    pass_total(0, 2)
    pass_total(0, 3)
    keep_own(0, 5)
    pass_total(0, 5)
    keep_own(1, 4)
    pass_total(1, 4)
    keep_own(1, 0)
    keep_own(1, 1)
    keep_own(1, 2)
    keep_own(1, 3)
    keep_own(1, 5)
    pass_total(1, 0)
    pass_total(1, 1)
    pass_total(1, 2)
    pass_total(1, 3)
    pass_total(1, 5)

    def landed(slot, t):
        return pltpu.make_async_remote_copy(
            src_ref=spot(FM, FD, slot, t), dst_ref=spot(FM, FD, slot, t),
            send_sem=fin_s.at[0, t], recv_sem=fin_r.at[slot, t],
            device_id={"expert": sib, "dp": dd}, device_id_type=MESH,
        )

    for t in [*range(n_t, n_t + n_s - 1), *range(n_t), n_t + n_s - 1]:
        @pl.when(g != c)
        def _():
            landed(c, t).wait_recv()

        landed(1 - c, t).wait_recv()
        if t < n_t:
            at = slice(t * part, (t + 1) * part)
            for o, out in enumerate((out_g, out_u)):
                out[0, at] = (
                    jnp.dot(FM[0, at], E[0, o], preferred_element_type=f32)
                    + jnp.dot(FM[1, at], E[1, o], preferred_element_type=f32)
                ).astype(bf)
        else:
            for slot in range(2):
                to = columns(t - n_t)
                out_d[0, slot * hpiece : (slot + 1) * hpiece, to] = FD[slot, :, to]

    if lends:
        @pl.when(beside_end)
        def _():
            for t in lent:
                lend(t).wait_recv()
                give_back(t).start()
            for t in lent:
                give_back(t).wait_send()

    for i in range(2):
        for t in range(n_t + n_s):
            reduce_copy(i, t).wait_send()
            if i == 0:
                final_copy(0, t).wait_send()
            else:
                @pl.when(g != c)
                def _():
                    final_copy(1, t).wait_send()

    @pl.when(mine_there)
    def _():
        for i in range(3):
            share(i).wait_send()

    @pl.loop(0, n_z)
    def _(src):
        for d in range(2):
            @pl.when(can(d) & (jnp.where(d == 0, z - src, src - z) >= 0))
            def _():
                tab_hop(d, src).wait_send()
                for i in range(n_c):
                    hop(i, d, src, False).wait_send()
        for i in range(n_c):
            for to in range(3):
                row(i, src, to, 0).wait_send()


def grid_step(n_e, tokens, out_grad, expert_ids, gate_probs, w_gate, w_up, w_down):
    rows, width = tokens.shape
    hid = w_gate.shape[2]
    n_z, top = n_e // CORES, expert_ids.shape[1]
    cap = rows * (top + 1) // n_e
    lanes = -(-n_e // 8) * 8
    block, half = 4 * cap, hid // 2
    piece, hpiece = width // 4, hid // 8
    total = n_z * block
    chunks = []
    for k, cuts in ((0, XCUTS), (1, GCUTS)):
        at = 0
        for eighths in cuts:
            chunks.append((k, at * width // 8, eighths * width // 8))
            at += eighths
    n_c = len(chunks)
    bf, f32 = jnp.bfloat16, jnp.float32
    vmem = pl.BlockSpec(memory_space=pltpu.VMEM)
    hbm = pl.BlockSpec(memory_space=pltpu.HBM)
    dma = pltpu.SemaphoreType.DMA
    scratch = [
        (expert_ids.shape[::-1], expert_ids.dtype),
        (gate_probs.shape[::-1], gate_probs.dtype),
        ((n_z, 2 * lanes, rows), f32),
        ((n_z, 2 * cap, rows), bf),
        ((n_z, 2 * cap, 128), f32),
        ((width, hid), bf),
        ((width, hid), bf),
        ((hid, width), bf),
        ((2, 2, hid, hid), bf),
        ((width, hid), bf),
        ((width, hid), bf),
        ((hid, width), bf),
        ((2, block, hid), f32),
        ((2, block, hid), f32),
        ((width, total), bf),
        ((total, hid), bf),
        ((half, total), bf),
    ]
    scratch += [((2, piece, hid), bf), ((2, hpiece, width), bf)] * 2
    scratch += [((2, piece, hid), f32), ((2, hpiece, width), f32)]
    scratch += [((2, piece, hid), bf), ((2, hpiece, width), bf)] * 2
    scratch += [((piece, hid), bf)]
    sizes = [w for _, _, w in chunks]
    scratch += [((n_z, rows, w), bf) for w in sizes]
    scratch += [((n_z, 2, cap, w), bf) for w in sizes]
    scratch += [((n_z, 4, cap, w), bf) for w in sizes]
    held = sum(math.prod(shape) * jnp.dtype(kind).itemsize for shape, kind in scratch)
    args = (tokens, out_grad, expert_ids.T, gate_probs.T, w_gate, w_up, w_down)
    made = pl.pallas_call(
        functools.partial(grid_kernel, n_e, cap, chunks),
        out_shape=(
            jax.ShapeDtypeStruct((1, piece, hid), bf),
            jax.ShapeDtypeStruct((1, piece, hid), bf),
            jax.ShapeDtypeStruct((1, 2 * hpiece, width), bf),
        ),
        in_specs=[hbm] * 7,
        out_specs=(vmem, vmem, vmem),
        scratch_shapes=[pltpu.VMEM(shape, kind) for shape, kind in scratch]
        + [
            dma((2,)),
            dma((n_c,)),
            dma((3,)),
            dma((3,)),
            dma((3,)),
            dma((2, n_z)),
            dma((n_z,)),
            dma((n_c, 2, n_z)),
            dma((n_c, n_z)),
            dma((n_c, n_z, 3)),
            dma((n_c, n_z, 4)),
        ]
        + [dma((2, 6))] * 4
        + [dma((4,))] * 2,
        compiler_params=pltpu.CompilerParams(
            collective_id=1, has_side_effects=True, vmem_limit_bytes=held + (12 << 20)
        ),
    )(*(pltpu.with_memory_space_constraint(x, pltpu.HBM) for x in args))
    return write_out(made)


def solution(mesh):
    n_e, n_d = mesh.shape["expert"], mesh.shape["dp"]
    n_b = max(b for b in range(1, n_d + 1) if n_d % b == 0 and b * b <= n_d)
    n_a = n_d // n_b

    def step(tokens, out_grad, expert_ids, gate_probs, w_gate, w_up, w_down):
        rows, width = tokens.shape
        hid = w_gate.shape[2]
        total = n_e * rows
        lanes = -(-n_e // 8) * 8
        bf, f32 = jnp.bfloat16, jnp.float32
        vmem = pl.BlockSpec(memory_space=pltpu.VMEM)
        hbm = pl.BlockSpec(memory_space=pltpu.HBM)
        piece, hpiece = width // n_d, hid // n_d
        dma = pltpu.SemaphoreType.DMA
        scratch = [
            (expert_ids.shape[::-1], expert_ids.dtype),
            (gate_probs.shape[::-1], gate_probs.dtype),
            ((n_e, rows, width), bf),
            ((n_e, rows, width), bf),
            ((n_e, lanes, rows), f32),
            ((width, hid), bf),
            ((width, hid), bf),
            ((hid, width), bf),
            ((2, CORES * rows, 2 * hid), f32),
            ((width, total), bf),
            ((hid, total), bf),
            ((total, 2 * hid), bf),
            ((total, width), bf),
            ((2, width, hid), bf),
            ((2, n_d, hpiece, width // 2), bf),
            ((2, n_a, n_a, piece, hid), bf),
            ((2, n_a, n_a, hpiece, width // 2), bf),
            ((2, n_a, piece, hid), bf),
            ((2, n_a, hpiece, width // 2), bf),
            ((2, n_a, piece, hid), bf),
            ((2, n_a, hpiece, width // 2), bf),
        ]
        held = sum(math.prod(shape) * jnp.dtype(kind).itemsize for shape, kind in scratch)
        args = (tokens, out_grad, expert_ids.T, gate_probs.T, w_gate, w_up, w_down)
        made = pl.pallas_call(
            functools.partial(kernel, n_e, n_a, n_b),
            out_shape=(
                jax.ShapeDtypeStruct((1, piece, hid), bf),
                jax.ShapeDtypeStruct((1, piece, hid), bf),
                jax.ShapeDtypeStruct((1, hpiece, width), bf),
            ),
            in_specs=[hbm] * 7,
            out_specs=(vmem, vmem, vmem),
            scratch_shapes=[pltpu.VMEM(shape, kind) for shape, kind in scratch]
            + [
                dma((7,)),
                dma((3, 2, n_e)),
                dma((3, n_e)),
                dma((3, n_e)),
                dma((2, 2, n_d)),
                dma((2, 2, n_a, n_a)),
                dma((2, 2, n_a)),
                dma((2, 2, n_a)),
            ],
            compiler_params=pltpu.CompilerParams(
                collective_id=0, has_side_effects=True, vmem_limit_bytes=held + (10 << 20)
            ),
        )(*(pltpu.with_memory_space_constraint(x, pltpu.HBM) for x in args))
        return write_out(made)

    if n_a == 2 and n_b == 2:
        step = functools.partial(grid_step, n_e)
    spread = P(("expert", "dp"), None)
    return jax.shard_map(
        step,
        mesh=mesh,
        in_specs=(spread, spread, spread, spread) + (P("expert", None, None),) * 3,
        out_specs=(P("expert", "dp", None),) * 3,
        check_vma=False,
    )
```
